32 devices in a mesh: dp: 8 (over y, x, core), fsdp: 4 (over z).
Axes of the slice: x: 2, y: 2, z: 4, core: 2. Of those that a mesh axis runs over, the one named last changes fastest.
Arguments:
- inputs: bfloat16 [8, 512, 1024], P('dp', 'fsdp'), may hold values from -6 to 6
- gain_mixer: bfloat16 [1024], P(('dp', 'fsdp')), may hold values from 0.5 to 1.5
- weight_in: bfloat16 [1024, 3072], P(('dp', 'fsdp')), may hold values from -0.1875 to 0.1875
- conv_taps: bfloat16 [3, 1024], P(None, ('dp', 'fsdp')), may hold values from -3.5 to 3.5
- weight_out: bfloat16 [1024, 1024], P(('dp', 'fsdp')), may hold values from -0.1875 to 0.1875
- gain_ffn: bfloat16 [1024], P(('dp', 'fsdp')), may hold values from 0.5 to 1.5
- weight_gate: bfloat16 [1024, 4608], P(('dp', 'fsdp')), may hold values from -0.1875 to 0.1875
- weight_up: bfloat16 [1024, 4608], P(('dp', 'fsdp')), may hold values from -0.1875 to 0.1875
- weight_down: bfloat16 [4608, 1024], P(('dp', 'fsdp')), may hold values from -0.09375 to 0.09375
- cotangent: bfloat16 [8, 512, 1024], P('dp', 'fsdp'), may hold values from -6 to 6
Outputs:
- outputs: bfloat16 [8, 512, 1024], P('dp', 'fsdp')
- grad_inputs: float32 [8, 512, 1024], P('dp', 'fsdp')
- grad_gain_mixer: float32 [1024], P(('dp', 'fsdp'))
- grad_weight_in: float32 [1024, 3072], P(('dp', 'fsdp'))
- grad_conv_taps: float32 [3, 1024], P(None, ('dp', 'fsdp'))
- grad_weight_out: float32 [1024, 1024], P(('dp', 'fsdp'))
- grad_gain_ffn: float32 [1024], P(('dp', 'fsdp'))
- grad_weight_gate: float32 [1024, 4608], P(('dp', 'fsdp'))
- grad_weight_up: float32 [1024, 4608], P(('dp', 'fsdp'))
- grad_weight_down: float32 [4608, 1024], P(('dp', 'fsdp'))
The draws below stay inside these ranges and needn't reach their ends.
All inputs are finite; a program needn't handle non-finite values.
Results may differ from the reference program's by a relative error of at most 0.0088.
Values may be sent and summed in bfloat16 or wider, within the bound.
A program may use at most 192 MiB of HBM per device.

```python
import jax
import jax.numpy as jnp
from jax import lax

D = 1024
FF = 4608
KW = 3
LENGTH = 512
SEQS = 8


def spiked(array, key, source, target, shards_of, factor):
    owner, partner = [(jnp.arange(array.shape[position]) // (array.shape[position] // shards_of)).reshape([-1 if axis == position else 1 for axis in range(array.ndim)]) for position in (source, target)]
    chosen = jax.random.permutation(key, shards_of)[partner]
    strong = (owner == chosen) | (owner == (partner + shards_of // 2) % shards_of)
    return jnp.where(strong, factor * array, array)


def levels(key, dims, cuts, least, high):
    factor_of, own = 1.0, jax.random.fold_in(key, 6)
    for position, shards_of in cuts:
        heights = jnp.exp(jax.random.uniform(jax.random.fold_in(own, position), (shards_of,), jnp.float32, least / len(cuts), high / len(cuts)))
        factor_of = factor_of * jnp.repeat(heights, dims[position] // shards_of).reshape([-1 if axis == position else 1 for axis in range(len(dims))])
    return factor_of


def gaussian(key, shape, deviation, limit, split=(), held_as=jnp.bfloat16):
    factor_of = levels(key, shape, split, -0.22, 0.18) if split else 1.0
    values = jax.random.normal(key, shape, jnp.float32) * deviation * factor_of
    return jnp.minimum(jnp.maximum(values, -limit), limit).astype(held_as)


def noise_with(key, extent, scale, reach, cuts, heavy, held_as=jnp.bfloat16):
    values = scale * jax.random.normal(key, extent, jnp.float32)
    if cuts:
        values = values * levels(key, extent, cuts, -0.22, 0.18)
    return jnp.clip(spiked(values, jax.random.fold_in(key, 3), *heavy), -reach, reach).astype(held_as)


def setup_inputs(seed: int = 0) -> dict:
    key_of = jax.random.split(jax.random.key(seed), 11)
    return {
        "inputs": noise_with(key_of[0], (SEQS, LENGTH, D), 1.0, 6.0, ((0, 8), (1, 4)), (0, 2, 8, 2.0)),
        "gain_mixer": jnp.clip(1.0 + 0.1 * jax.random.normal(key_of[1], (D,), jnp.float32), 0.5, 1.5).astype(jnp.bfloat16),
        "weight_in": gaussian(key_of[2], (D, 3 * D), D ** -0.5, 0.1875, ((0, 32),)),
        "conv_taps": gaussian(key_of[3], (KW, D), KW ** -0.5, 3.5, ((1, 32),)),
        "weight_out": gaussian(key_of[4], (D, D), D ** -0.5, 0.1875, ((0, 32),)),
        "gain_ffn": jnp.clip(1.0 + 0.1 * jax.random.normal(key_of[5], (D,), jnp.float32), 0.5, 1.5).astype(jnp.bfloat16),
        "weight_gate": gaussian(key_of[6], (D, FF), D ** -0.5, 0.1875, ((0, 32),)),
        "weight_up": gaussian(key_of[7], (D, FF), D ** -0.5, 0.1875, ((0, 32),)),
        "weight_down": gaussian(key_of[8], (FF, D), FF ** -0.5, 0.09375, ((0, 32),)),
        "cotangent": gaussian(key_of[9], (SEQS, LENGTH, D), 1.0, 6.0, ((0, 8), (1, 4))),
    }


EPS = 1e-05

def product(left, right):
    return jnp.dot(left, right, preferred_element_type=jnp.float32)

def norm_forward(hidden, gain):
    scale = lax.rsqrt(lax.optimization_barrier(jnp.mean(hidden * hidden, axis=-1, keepdims=True)) + EPS)
    normed = hidden * scale
    return (normed, scale, normed * gain.astype(jnp.float32))

def norm_backward(dact, normed, scale, gain):
    dnormed = dact * gain.astype(jnp.float32)
    dhidden = scale * (dnormed - normed * lax.optimization_barrier(jnp.mean(dnormed * normed, axis=-1, keepdims=True)))
    return (dhidden, lax.optimization_barrier(jnp.sum(dact * normed, axis=0)))

def lagged(values, offset):
    zeros = jnp.zeros((offset, values.shape[1]), values.dtype)
    return jnp.concatenate([zeros, values[:values.shape[0] - offset]], axis=0)

def leading(values, offset):
    zeros = jnp.zeros((offset, values.shape[1]), values.dtype)
    return jnp.concatenate([values[offset:], zeros], axis=0)

def reference(inputs, gain_mixer, weight_in, conv_taps, weight_out, gain_ffn, weight_gate, weight_up, weight_down, cotangent):
    width = weight_out.shape[0]
    taps32 = conv_taps.astype(jnp.float32)

    def one_sequence(carry, pair):
        tokens, grad_out = pair
        hidden = tokens.astype(jnp.float32)
        normed1, scale1, pre1 = norm_forward(hidden, gain_mixer)
        act1 = pre1.astype(jnp.bfloat16)
        projected = product(act1, weight_in)
        bpart = projected[:, :width]
        cpart = projected[:, width:2 * width]
        xpart = projected[:, 2 * width:]
        gated = bpart * xpart
        conv = jnp.zeros_like(gated)
        for offset in range(KW):
            conv = conv + taps32[offset] * lagged(gated, offset)
        act2 = (cpart * conv).astype(jnp.bfloat16)
        resid = hidden + product(act2, weight_out)
        normed2, scale2, pre2 = norm_forward(resid, gain_ffn)
        act3 = pre2.astype(jnp.bfloat16)
        gate = product(act3, weight_gate)
        upval = product(act3, weight_up)
        sig = jax.nn.sigmoid(gate)
        act4 = (gate * sig * upval).astype(jnp.bfloat16)
        outputs = (resid + product(act4, weight_down)).astype(jnp.bfloat16)
        g_down = product(act4.T, grad_out)
        dact4 = product(grad_out, weight_down.T)
        dgate = (dact4 * upval * sig * (1.0 + gate * (1.0 - sig))).astype(jnp.bfloat16)
        dupval = (dact4 * gate * sig).astype(jnp.bfloat16)
        g_gate = product(act3.T, dgate)
        g_up = product(act3.T, dupval)
        dact3 = product(dgate, weight_gate.T) + product(dupval, weight_up.T)
        dnorm2, g_gain2 = norm_backward(dact3, normed2, scale2, gain_ffn)
        dresid = grad_out.astype(jnp.float32) + dnorm2
        dres16 = dresid.astype(jnp.bfloat16)
        g_out = product(act2.T, dres16)
        dact2 = product(dres16, weight_out.T)
        dcpart = dact2 * conv
        dconv = dact2 * cpart
        g_taps = jnp.stack([lax.optimization_barrier(jnp.sum(dconv * lagged(gated, offset), axis=0)) for offset in range(KW)], axis=0)
        dgated = jnp.zeros_like(dconv)
        for offset in range(KW):
            dgated = dgated + taps32[offset] * leading(dconv, offset)
        dproj = jnp.concatenate([dgated * xpart, dcpart, dgated * bpart], axis=1).astype(jnp.bfloat16)
        g_in = product(act1.T, dproj)
        dact1 = product(dproj, weight_in.T)
        dnorm1, g_gain1 = norm_backward(dact1, normed1, scale1, gain_mixer)
        grad_in = dresid + dnorm1
        terms = (g_gain1, g_in, g_taps, g_out, g_gain2, g_gate, g_up, g_down)
        carry = tuple((total + term for total, term in zip(carry, terms)))
        return (carry, (outputs, grad_in))
    start = (jnp.zeros(gain_mixer.shape, jnp.float32), jnp.zeros(weight_in.shape, jnp.float32), jnp.zeros(conv_taps.shape, jnp.float32), jnp.zeros(weight_out.shape, jnp.float32), jnp.zeros(gain_ffn.shape, jnp.float32), jnp.zeros(weight_gate.shape, jnp.float32), jnp.zeros(weight_up.shape, jnp.float32), jnp.zeros(weight_down.shape, jnp.float32))
    totals, stacked = lax.scan(one_sequence, start, (inputs, cotangent))
    outputs, grad_inputs = stacked
    return (outputs, grad_inputs, totals[0], totals[1], totals[2], totals[3], totals[4], totals[5], totals[6], totals[7])
```

```python
import functools

import jax
import jax.numpy as jnp
from jax import lax
from jax.experimental import pallas as pl
from jax.experimental.pallas import tpu as pltpu
from jax.sharding import PartitionSpec as P

KW = 3


EPS = 1e-05

CORES = 2
MESH = pl.DeviceIdType.MESH


def product(left, right):
    return jnp.dot(left, right, preferred_element_type=jnp.float32)


def product_tn(left, right):
    return lax.dot_general(
        left, right, (((0,), (0,)), ((), ())), preferred_element_type=jnp.float32
    )


def product_nt(left, right):
    return lax.dot_general(
        left, right, (((1,), (1,)), ((), ())), preferred_element_type=jnp.float32
    )


def norm_forward(hidden, gain):
    scale = lax.rsqrt(jnp.mean(hidden * hidden, axis=-1, keepdims=True) + EPS)
    normed = hidden * scale
    return (normed, scale, normed * gain.astype(jnp.float32))


def norm_backward(dact, normed, scale, gain):
    dnormed = dact * gain.astype(jnp.float32)
    dhidden = scale * (dnormed - normed * jnp.mean(dnormed * normed, axis=-1, keepdims=True))
    return (dhidden, jnp.sum(dact * normed, axis=0))


def lagged(values, offset):
    zeros = jnp.zeros((offset, values.shape[1]), values.dtype)
    return jnp.concatenate([zeros, values[: values.shape[0] - offset]], axis=0)


def leading(values, offset):
    zeros = jnp.zeros((offset, values.shape[1]), values.dtype)
    return jnp.concatenate([values[offset:], zeros], axis=0)


def column_blocks(shard, lead, dp_count, fs_count):
    rows, columns = shard.shape
    inner = columns // (lead * dp_count * fs_count)
    pieces = shard.reshape(rows, lead, dp_count, fs_count, inner).transpose(3, 0, 1, 2, 4)
    return pieces.reshape(fs_count, rows, lead * dp_count * inner)


def column_join(blocks, lead, dp_count, fs_count):
    _, rows, columns = blocks.shape
    inner = columns // (lead * dp_count)
    pieces = blocks.reshape(fs_count, rows, lead, dp_count, inner).transpose(1, 2, 3, 0, 4)
    return pieces.reshape(rows, lead * dp_count * fs_count * inner)


def greet(peers):
    barrier = pltpu.get_barrier_semaphore()
    for peer in peers:
        pl.semaphore_signal(barrier, inc=1, device_id=peer, device_id_type=MESH)
    pl.semaphore_wait(barrier, len(peers))


def push(src, dst, sends, recvs, index, peer):
    copy = pltpu.make_async_remote_copy(
        src_ref=src,
        dst_ref=dst,
        send_sem=sends.at[index],
        recv_sem=recvs.at[index],
        device_id=peer,
        device_id_type=MESH,
    )
    copy.start()
    return copy


def place():
    dp, fs = lax.axis_index("dp"), lax.axis_index("fsdp")
    pair, core = dp // CORES, lax.rem(dp, CORES)
    return dp, fs, pair, core, (pair * CORES + 1 - core, fs)


def gather_kernel(
    pairs, fs_count,
    x_ref, cot_ref, small_ref, in_ref, gu_ref, out_ref, down_ref,
    x_all, cot_all, small_all, in_all, gu_all, out_all, down_all,
    local_sem, z_send, z_recv, p_send, p_recv, c_send, c_recv,
):
    dp, fs, pair, core, partner = place()
    z_peers = [(dp, lax.rem(fs + o, fs_count)) for o in range(1, fs_count)]
    p_peers = [(lax.rem(pair + o, pairs) * CORES + core, fs) for o in range(1, pairs)]
    p_from = [lax.rem(pair + pairs - o, pairs) * CORES + core for o in range(1, pairs)]
    greet(z_peers + p_peers + [partner])
    spread = [small_all, in_all, gu_all, out_all, down_all]

    across = [[None] * len(p_peers) for _ in spread]
    twins = [[None] * pairs for _ in spread]

    def spread_own(kind, src):
        dst = spread[kind].at[dp]
        for o, peer in enumerate(p_peers):
            across[kind][o] = push(src, dst, p_send, p_recv, (kind, o), peer)
        twins[kind][0] = push(src, dst, c_send, c_recv, (kind, 0), partner)

    along = [[], [], [], [], []]
    for o, peer in enumerate(z_peers):
        to = peer[1]
        along[0].append(push(small_ref, small_all.at[dp, fs], z_send, z_recv, (0, o), peer))
        along[1].append(push(in_ref.at[to], in_all.at[dp, fs], z_send, z_recv, (1, o), peer))
    for o, peer in enumerate(z_peers):
        to = peer[1]
        along[2].append(push(gu_ref.at[to], gu_all.at[dp, fs], z_send, z_recv, (2, o), peer))
    for o, peer in enumerate(z_peers):
        along[3].append(push(x_ref, x_all.at[fs], z_send, z_recv, (3, o), peer))
    for o, peer in enumerate(z_peers):
        along[4].append(push(cot_ref, cot_all.at[fs], z_send, z_recv, (4, o), peer))
    spread_own(3, out_ref)
    spread_own(4, down_ref)
    local = []
    for index, (src, dst) in enumerate(
        [
            (small_ref, small_all.at[dp, fs]),
            (in_ref.at[fs], in_all.at[dp, fs]),
            (gu_ref.at[fs], gu_all.at[dp, fs]),
            (x_ref, x_all.at[fs]),
            (cot_ref, cot_all.at[fs]),
            (out_ref, out_all.at[dp]),
            (down_ref, down_all.at[dp]),
        ]
    ):
        copy = pltpu.make_async_copy(src, dst, local_sem.at[index])
        copy.start()
        local.append(copy)
    for kind in range(3):
        local[kind].wait()
        for copy in along[kind]:
            copy.wait_recv()
        spread_own(kind, spread[kind].at[dp])
    for kind in (3, 0, 1, 4, 2):
        for o, source in enumerate(p_from):
            across[kind][o].wait_recv()
            block = spread[kind].at[source]
            twins[kind][o + 1] = push(block, block, c_send, c_recv, (kind, o + 1), partner)
    for copy in local[3:]:
        copy.wait()
    for copy in along[3] + along[4]:
        copy.wait_recv()
    for row in along + across:
        for copy in row:
            copy.wait_send()
    for row in twins:
        for copy in row:
            copy.wait()


def gather_all(x, cot, small, in_blocks, gu_blocks, out_shard, down_shard):
    dp_count, fs_count = lax.axis_size("dp"), lax.axis_size("fsdp")
    pairs = dp_count // CORES
    arrays = (x, cot, small, in_blocks, gu_blocks, out_shard, down_shard)
    shapes = (
        (fs_count,) + x.shape,
        (fs_count,) + cot.shape,
        (dp_count, fs_count) + small.shape,
        (dp_count,) + in_blocks.shape,
        (dp_count,) + gu_blocks.shape,
        (dp_count,) + out_shard.shape,
        (dp_count,) + down_shard.shape,
    )
    return pl.pallas_call(
        functools.partial(gather_kernel, pairs, fs_count),
        out_shape=[jax.ShapeDtypeStruct(shape, x.dtype) for shape in shapes],
        in_specs=[pl.BlockSpec(memory_space=pltpu.VMEM)] * len(arrays),
        out_specs=[pl.BlockSpec(memory_space=pl.ANY)] * len(shapes),
        scratch_shapes=[
            pltpu.SemaphoreType.DMA((7,)),
            pltpu.SemaphoreType.DMA((5, fs_count - 1)),
            pltpu.SemaphoreType.DMA((5, fs_count - 1)),
            pltpu.SemaphoreType.DMA((5, pairs - 1)),
            pltpu.SemaphoreType.DMA((5, pairs - 1)),
            pltpu.SemaphoreType.DMA((5, pairs)),
            pltpu.SemaphoreType.DMA((5, pairs)),
        ],
        compiler_params=pltpu.CompilerParams(collective_id=0, has_side_effects=True),
        name="gather_all",
    )(*arrays)


def line_kernel(count, fs_count, whole, *refs):
    sources, landed = refs[:count], refs[count : 2 * count]
    local_sem, sends, recvs = refs[2 * count :]
    dp, fs, _, _, _ = place()
    targets = [lax.rem(fs + o, fs_count) for o in range(1, fs_count)]
    greet([(dp, to) for to in targets])
    copies = [
        push(src if whole else src.at[to], dst.at[fs], sends, recvs, (k, o), (dp, to))
        for k, (src, dst) in enumerate(zip(sources, landed))
        for o, to in enumerate(targets)
    ]
    local = []
    for k, (src, dst) in enumerate(zip(sources, landed)):
        copy = pltpu.make_async_copy(src if whole else src.at[fs], dst.at[fs], local_sem.at[k])
        copy.start()
        local.append(copy)
    for copy in local + copies:
        copy.wait()


def along_line(arrays, whole, collective_id, name):
    fs_count = lax.axis_size("fsdp")
    count = len(arrays)
    return pl.pallas_call(
        functools.partial(line_kernel, count, fs_count, whole),
        out_shape=[
            jax.ShapeDtypeStruct(((fs_count,) + a.shape) if whole else a.shape, a.dtype)
            for a in arrays
        ],
        in_specs=[pl.BlockSpec(memory_space=pltpu.VMEM)] * count,
        out_specs=[pl.BlockSpec(memory_space=pl.ANY)] * count,
        scratch_shapes=[
            pltpu.SemaphoreType.DMA((count,)),
            pltpu.SemaphoreType.DMA((count, fs_count - 1)),
            pltpu.SemaphoreType.DMA((count, fs_count - 1)),
        ],
        compiler_params=pltpu.CompilerParams(collective_id=collective_id, has_side_effects=True),
        name=name,
    )(*arrays)


def whole_sequence(rows, collective_id, name):
    (received,) = along_line([rows], True, collective_id, name)
    return received.reshape(-1, rows.shape[1])


def token_pieces(partial_value):
    fs_count = lax.axis_size("fsdp")
    rows, columns = partial_value.shape
    return partial_value.astype(jnp.bfloat16).reshape(fs_count, rows // fs_count, columns)


def token_share(partial_value, collective_id, name):
    (received,) = along_line([token_pieces(partial_value)], False, collective_id, name)
    return jnp.sum(received.astype(jnp.float32), axis=0)


def token_share_async(partial_value):
    received = lax.all_to_all(
        token_pieces(partial_value), "fsdp", split_axis=0, concat_axis=0, tiled=True
    )
    return jnp.sum(received.astype(jnp.float32), axis=0)


def twin_kernel(count, pairs, *refs):
    partials, received = refs[:count], refs[count : 2 * count]
    sends, recvs = refs[2 * count :]
    _, _, _, core, partner = place()
    greet([partner])
    copies = [
        push(partial.at[j, 1 - core], landed.at[j], sends, recvs, (k, j), partner)
        for k, (partial, landed) in enumerate(zip(partials, received))
        for j in range(pairs)
    ]
    for copy in copies:
        copy.wait()


def pair_kernel(count, pairs, fs_count, *refs):
    partials, pieces = refs[:count], refs[count]
    received, pieces_in = refs[count + 1 : 2 * count + 1], refs[2 * count + 1]
    sends, recvs, z_sends, z_recvs = refs[2 * count + 2 :]
    dp, fs, pair, core, _ = place()
    targets = [lax.rem(pair + o, pairs) for o in range(1, pairs)]
    peers = [(to * CORES + core, fs) for to in targets]
    z_targets = [lax.rem(fs + o, fs_count) for o in range(1, fs_count)]
    greet(peers + [(dp, to) for to in z_targets])
    copies = [
        push(partial.at[to], landed.at[o], sends, recvs, (k, o), peer)
        for k, (partial, landed) in enumerate(zip(partials, received))
        for o, (to, peer) in enumerate(zip(targets, peers))
    ]
    copies += [
        push(pieces.at[to], pieces_in.at[o], z_sends, z_recvs, o, (dp, to))
        for o, to in enumerate(z_targets)
    ]
    for copy in copies:
        copy.wait()


def twin_exchange(partials):
    count = len(partials)
    pairs = lax.axis_size("dp") // CORES
    return pl.pallas_call(
        functools.partial(twin_kernel, count, pairs),
        out_shape=[jax.ShapeDtypeStruct((pairs,) + p.shape[-2:], p.dtype) for p in partials],
        in_specs=[pl.BlockSpec(memory_space=pl.ANY)] * count,
        out_specs=[pl.BlockSpec(memory_space=pl.ANY)] * count,
        scratch_shapes=[pltpu.SemaphoreType.DMA((count, pairs))] * 2,
        compiler_params=pltpu.CompilerParams(collective_id=1, has_side_effects=True),
        name="twin_exchange",
    )(*partials)


def pair_exchange(partials, pieces):
    count = len(partials)
    pairs, fs_count = lax.axis_size("dp") // CORES, lax.axis_size("fsdp")
    slots = [(pairs - 1, p) for p in partials] + [(fs_count - 1, pieces)]
    return pl.pallas_call(
        functools.partial(pair_kernel, count, pairs, fs_count),
        out_shape=[jax.ShapeDtypeStruct((n,) + p.shape[-2:], p.dtype) for n, p in slots],
        in_specs=[pl.BlockSpec(memory_space=pl.ANY)] * len(slots),
        out_specs=[pl.BlockSpec(memory_space=pl.ANY)] * len(slots),
        scratch_shapes=[
            pltpu.SemaphoreType.DMA((count, pairs - 1)),
            pltpu.SemaphoreType.DMA((count, pairs - 1)),
            pltpu.SemaphoreType.DMA((fs_count - 1,)),
            pltpu.SemaphoreType.DMA((fs_count - 1,)),
        ],
        compiler_params=pltpu.CompilerParams(collective_id=2, has_side_effects=True),
        name="pair_exchange",
    )(*partials, pieces)


def reduce_all(partials, pieces):
    dp_count = lax.axis_size("dp")
    pairs = dp_count // CORES
    dp = lax.axis_index("dp")
    core, pair = lax.rem(dp, CORES), dp // CORES
    split = [
        p.reshape(pairs, CORES, p.shape[0] // dp_count, p.shape[1])
        for p in partials
    ]
    landed = twin_exchange(split)
    chip = [
        (
            lax.dynamic_index_in_dim(p, core, axis=1, keepdims=False).astype(jnp.float32)
            + r.astype(jnp.float32)
        ).astype(p.dtype)
        for p, r in zip(split, landed)
    ]
    *others, pieces_in = pair_exchange(chip, pieces)
    own_piece = lax.dynamic_index_in_dim(pieces, lax.axis_index("fsdp"), axis=0, keepdims=False)
    tokens = own_piece.astype(jnp.float32) + jnp.sum(pieces_in.astype(jnp.float32), axis=0)
    return tokens, [
        lax.dynamic_index_in_dim(p, pair, axis=0, keepdims=False).astype(jnp.float32)
        + jnp.sum(r.astype(jnp.float32), axis=0)
        for p, r in zip(chip, others)
    ]


def split_features(
    inputs,
    gain_mixer,
    weight_in,
    conv_taps,
    weight_out,
    gain_ffn,
    weight_gate,
    weight_up,
    weight_down,
    cotangent,
):
    dp_count = lax.axis_size("dp")
    fs_count = lax.axis_size("fsdp")
    width = weight_out.shape[1]
    part = weight_out.shape[0]
    quarter = dp_count * part
    hid = dp_count * weight_down.shape[0]

    small = jnp.concatenate([gain_mixer[None], gain_ffn[None], conv_taps], axis=0)
    lanes = max(128, part)
    small = jnp.pad(small, ((0, 8 - small.shape[0]), (0, lanes - part)))
    gu_blocks = jnp.concatenate(
        [
            column_blocks(weight_gate, 1, dp_count, fs_count),
            column_blocks(weight_up, 1, dp_count, fs_count),
        ],
        axis=2,
    )
    grad_out = cotangent[0]
    x_all, grad_all, small_all, in_cols, gu_cols, out_rows, down_rows = gather_all(
        inputs[0],
        grad_out,
        small,
        column_blocks(weight_in, 3, dp_count, fs_count),
        gu_blocks,
        weight_out,
        weight_down,
    )
    x_all = x_all.reshape(-1, width)
    grad_all = grad_all.reshape(-1, width)
    in_cols = in_cols.reshape(width, 3 * quarter)
    gu_cols = gu_cols.reshape(width, 2 * hid)
    out_rows = out_rows.reshape(quarter, width)
    down_rows = down_rows.reshape(hid, width)
    small_all = small_all[:, :, : KW + 2, :part]
    gain1 = small_all[:, :, 0].reshape(width)
    gain2 = small_all[:, :, 1].reshape(width)
    taps32 = (
        lax.dynamic_index_in_dim(small_all, lax.axis_index("fsdp"), axis=1, keepdims=False)[:, 2:]
        .transpose(1, 0, 2)
        .reshape(KW, quarter)
        .astype(jnp.float32)
    )

    _, _, pre1_all = norm_forward(x_all.astype(jnp.float32), gain1)
    act1_all = pre1_all.astype(jnp.bfloat16)
    projected = product(act1_all, in_cols)
    bpart = projected[:, :quarter]
    cpart = projected[:, quarter : 2 * quarter]
    xpart = projected[:, 2 * quarter :]
    gated = bpart * xpart
    lagged_rows = [lagged(gated, offset) for offset in range(KW)]
    conv = taps32[0] * lagged_rows[0]
    for offset in range(1, KW):
        conv = conv + taps32[offset] * lagged_rows[offset]
    act2 = (cpart * conv).astype(jnp.bfloat16)
    hidden = inputs[0].astype(jnp.float32)
    normed1, scale1, _ = norm_forward(hidden, gain1)
    resid = hidden + token_share(product(act2, out_rows), 3, "share_out")
    normed2, scale2, pre2 = norm_forward(resid, gain2)
    act3_all = whole_sequence(pre2.astype(jnp.bfloat16), 4, "gather_ffn")
    gate_up = product(act3_all, gu_cols)
    gate, upval = gate_up[:, :hid], gate_up[:, hid:]
    sig = jax.nn.sigmoid(gate)
    act4 = (gate * sig * upval).astype(jnp.bfloat16)
    dact4 = product_nt(grad_all, down_rows)
    dgate = (dact4 * upval * sig * (1.0 + gate * (1.0 - sig))).astype(jnp.bfloat16)
    dupval = (dact4 * gate * sig).astype(jnp.bfloat16)
    dgu = jnp.concatenate([dgate, dupval], axis=1)
    dact3 = token_share(product_nt(dgu, gu_cols), 5, "share_ffn")
    down_pieces = token_pieces(product(act4, down_rows))
    dnorm2, g_gain2 = norm_backward(dact3, normed2, scale2, gain2)
    dresid = grad_out.astype(jnp.float32) + dnorm2
    dres_all = whole_sequence(dresid.astype(jnp.bfloat16), 6, "gather_dres")
    dact2 = product_nt(dres_all, out_rows)
    dcpart = dact2 * conv
    dconv = dact2 * cpart
    g_taps = jnp.stack(
        [jnp.sum(dconv * lagged_rows[offset], axis=0) for offset in range(KW)], axis=0
    )
    dgated = taps32[0] * dconv
    for offset in range(1, KW):
        dgated = dgated + taps32[offset] * leading(dconv, offset)
    dproj = jnp.concatenate([dgated * xpart, dcpart, dgated * bpart], axis=1).astype(jnp.bfloat16)
    dact1 = token_share_async(product_nt(dproj, in_cols))
    dnorm1, g_gain1 = norm_backward(dact1, normed1, scale1, gain1)
    grad_inputs = dresid + dnorm1

    own_column = (jnp.arange(fs_count) == lax.axis_index("fsdp"))[None, None, :, None]
    taps_spread = jnp.where(own_column, g_taps.reshape(KW, dp_count, 1, part), 0.0).reshape(KW, width)
    small_grad = jnp.concatenate([g_gain1[None], g_gain2[None], taps_spread], axis=0)
    small_grad = jnp.pad(small_grad, ((0, 8 - small_grad.shape[0]), (0, 0)))
    small_grad = small_grad.reshape(8, dp_count, fs_count, part).transpose(1, 2, 0, 3)
    small_grad = jnp.pad(small_grad, ((0, 0), (0, 0), (0, 0), (0, lanes - part)))
    down_sum, (g_small, g_gu, g_down, g_in, g_out) = reduce_all(
        [small_grad.reshape(dp_count * fs_count * 8, lanes)]
        + [
            grad.astype(jnp.bfloat16)
            for grad in (
                product_tn(act3_all, dgu),
                product_tn(act4, grad_all),
                product_tn(act1_all, dproj),
                product_tn(act2, dres_all),
            )
        ],
        down_pieces,
    )
    outputs = (resid + down_sum).astype(jnp.bfloat16)
    moved = jnp.concatenate([g_in, g_gu], axis=1).astype(jnp.bfloat16)
    moved, small_parts = along_line(
        [
            moved.reshape(fs_count, part, 3 * quarter + 2 * hid),
            g_small.reshape(fs_count, 8, lanes),
        ],
        False,
        7,
        "owner_exchange",
    )
    moved = moved.astype(jnp.float32)
    g_in_owned = moved[:, :, : 3 * quarter]
    g_gu_owned = moved[:, :, 3 * quarter :]
    small_owned = jnp.sum(small_parts, axis=0)[: KW + 2, :part]
    return (
        outputs[None],
        grad_inputs[None],
        small_owned[0],
        column_join(g_in_owned, 3, dp_count, fs_count),
        small_owned[2:],
        g_out,
        small_owned[1],
        column_join(g_gu_owned[:, :, :hid], 1, dp_count, fs_count),
        column_join(g_gu_owned[:, :, hid:], 1, dp_count, fs_count),
        g_down,
    )

HALO = 16


class Mover:
    def __init__(self, sends, recvs, locals_):
        self.sends, self.recvs, self.locals = sends, recvs, locals_
        self.count = 0
        self.local_count = 0
        self.open = []

    def push(self, src, dst, peer):
        copy = push(src, dst, self.sends, self.recvs, self.count, peer)
        self.count += 1
        self.open.append(copy)
        return copy

    def local(self, src, dst):
        copy = pltpu.make_async_copy(src, dst, self.locals.at[self.local_count])
        self.local_count += 1
        copy.start()
        return copy

    def finish(self):
        for copy in self.open:
            copy.wait_send()


def seats(pairs, fs_count):
    dp, fs, pair, core, partner = place()
    z_peers = [(dp, lax.rem(fs + o, fs_count)) for o in range(1, fs_count)]
    p_peers = [(lax.rem(pair + o, pairs) * CORES + core, fs) for o in range(1, pairs)]
    p_from = [lax.rem(pair + pairs - o, pairs) for o in range(1, pairs)]
    return dp, fs, pair, core, partner, z_peers, p_peers, p_from


def norm_scale(hidden):
    return lax.rsqrt(jnp.mean(hidden * hidden, axis=-1, keepdims=True) + EPS)


def mixer_forward_kernel(
    pairs, fs_count,
    x_ref, cot_ref, small_ref, in_ref, gate_ref, up_ref, out_ref, down_ref,
    act1_o, proj_o, act2_o, in_all, out_all, gains_o, taps_o, resid_o,
    act3_all, cot_all, gu_all, down_all,
    x_all, halo_all, small_all, in_blk, in_stage, gu_blk, act3_own,
    tw_out, tw_in, pr_out, pr_in, local_sem, sends, recvs,
):
    dp, fs, pair, core, partner, z_peers, p_peers, p_from = seats(pairs, fs_count)
    count = pairs * CORES
    tokens, width = x_ref.shape
    part = in_ref.shape[0]
    feat = width // count
    inner = gate_ref.shape[1] // (count * fs_count)
    hid = inner * count
    other = 1 - core
    move = Mover(sends, recvs, local_sem)
    f32 = jnp.float32

    greet(z_peers + p_peers + [partner])
    small_z = [move.push(small_ref, small_all.at[dp, fs], peer) for peer in z_peers]
    halo_next = move.push(x_ref.at[pl.ds(tokens - HALO, HALO)], halo_all.at[dp, pl.ds(0, HALO)], z_peers[0])
    halo_prev = move.push(x_ref.at[pl.ds(0, HALO)], halo_all.at[dp, pl.ds(HALO, HALO)], z_peers[-1])
    for to in range(count):
        for k in range(3):
            in_blk[to % CORES, to // CORES, :, k * feat : (k + 1) * feat] = in_ref[
                :, k * width + to * feat : k * width + (to + 1) * feat
            ]
    in_twin = move.push(in_blk.at[other], in_stage, partner)
    in_out = [move.push(in_blk.at[core, peer[0] // CORES], in_all.at[dp, fs], peer) for peer in p_peers]
    x_out = [move.push(x_ref, x_all.at[dp], peer) for peer in p_peers]
    x_twin = move.push(x_ref, x_all.at[dp], partner)
    small_all[dp, fs] = small_ref[...]
    x_all[dp] = x_ref[...]
    in_all[dp, fs] = in_blk[core, pair]
    in_twin.wait_recv()
    twin_dp = pair * CORES + other
    in_all[twin_dp, fs] = in_stage[pair]
    in_via = [
        move.push(in_stage.at[peer[0] // CORES], in_all.at[twin_dp, fs], peer) for peer in p_peers
    ]
    for copy in small_z:
        copy.wait_recv()
    small_out = [move.push(small_all.at[dp], small_all.at[dp], peer) for peer in p_peers]
    small_twin = [move.push(small_all.at[dp], small_all.at[dp], partner)]
    halo_next.wait_recv()
    halo_prev.wait_recv()
    halo_out = [move.push(halo_all.at[dp], halo_all.at[dp], peer) for peer in p_peers]
    halo_twin = [move.push(halo_all.at[dp], halo_all.at[dp], partner)]
    for copy in in_out + in_via:
        copy.wait_recv()
    in_z = [move.push(in_all.at[:, fs], in_all.at[:, fs], peer) for peer in z_peers]
    out_z = [move.push(out_ref, out_all.at[fs], peer) for peer in z_peers]
    out_all[fs] = out_ref[...]
    down_out = [move.push(down_ref, down_all.at[dp], peer) for peer in p_peers]
    down_twin = [move.push(down_ref, down_all.at[dp], partner)]
    down_local = move.local(down_ref, down_all.at[dp])
    for which, ref in enumerate((gate_ref, up_ref)):
        wide = ref[...].astype(f32)
        for to in range(fs_count):
            pieces = [
                wide[:, (d * fs_count + to) * inner : (d * fs_count + to + 1) * inner]
                for d in range(count)
            ]
            gu_blk[to, :, which * hid : (which + 1) * hid] = jnp.concatenate(pieces, axis=1).astype(
                jnp.bfloat16
            )
    gu_z = [move.push(gu_blk.at[peer[1]], gu_all.at[dp, fs], peer) for peer in z_peers]
    gu_local = move.local(gu_blk.at[fs], gu_all.at[dp, fs])
    cot_z = [move.push(cot_ref, cot_all.at[fs], peer) for peer in z_peers]
    cot_local = move.local(cot_ref, cot_all.at[fs])

    small_rel, x_rel = [], []
    for o, source in enumerate(p_from):
        src = source * CORES + core
        small_out[o].wait_recv()
        halo_out[o].wait_recv()
        x_out[o].wait_recv()
        small_rel.append(move.push(small_all.at[src], small_all.at[src], partner))
        x_rel.append(move.push(halo_all.at[src], halo_all.at[src], partner))
        x_rel.append(move.push(x_all.at[src], x_all.at[src], partner))
    for copy in small_twin + small_rel + [x_twin] + halo_twin + x_rel:
        copy.wait_recv()

    for d in range(count):
        total = small_all[d, 0].astype(f32)
        for f in range(1, fs_count):
            total = total + small_all[d, f].astype(f32)
        gains_o[:, d * feat : (d + 1) * feat] = total
    total = small_all[dp, 0].astype(f32)
    for f in range(1, fs_count):
        total = total + small_all[dp, f].astype(f32)
    taps_o[...] = total
    has_prev, has_next = fs > 0, fs < fs_count - 1

    def norm_step(i, carry):
        gain = gains_o[0:1, :]
        rows = x_all[i].astype(f32)
        act1_o[i, HALO : HALO + tokens] = (rows * norm_scale(rows) * gain).astype(jnp.bfloat16)
        edge = halo_all[i].astype(f32)
        edge = edge * norm_scale(edge) * gain
        act1_o[i, 0:HALO] = jnp.where(has_prev, edge[:HALO], 0.0).astype(jnp.bfloat16)
        act1_o[i, HALO + tokens :] = jnp.where(has_next, edge[HALO:], 0.0).astype(jnp.bfloat16)
        return carry

    lax.fori_loop(0, count, norm_step, 0)
    for copy in in_z + out_z:
        copy.wait_recv()

    def project_step(i, carry):
        proj_o[i] = product(act1_o[i], in_all[...].reshape(width, 3 * feat))
        gated = proj_o[i, :, 0:feat] * proj_o[i, :, 2 * feat :]
        conv = taps_o[2:3, :] * gated[HALO : HALO + tokens]
        for k in range(1, KW):
            conv = conv + taps_o[2 + k : 3 + k, :] * gated[HALO - k : HALO - k + tokens]
        act2_o[i] = (proj_o[i, HALO : HALO + tokens, feat : 2 * feat] * conv).astype(jnp.bfloat16)
        return carry

    lax.fori_loop(0, count, project_step, 0)

    def out_partial(dest):
        return product(act2_o[dest], out_all[...].reshape(feat, width))

    order = [lax.rem(pair + o, pairs) for o in range(1, pairs)] + [pair]
    share_tw = []
    for o, j in enumerate(order):
        tw_out[o] = out_partial(j * CORES + other).astype(jnp.bfloat16)
        share_tw.append(move.push(tw_out.at[o], tw_in.at[o], partner))
    share_pr = []
    own = None
    for o, j in enumerate(order):
        value = out_partial(j * CORES + core)
        share_tw[o].wait_recv()
        value = value + tw_in[o].astype(f32)
        if o < pairs - 1:
            pr_out[o] = value.astype(jnp.bfloat16)
            share_pr.append(move.push(pr_out.at[o], pr_in.at[o], p_peers[o]))
        else:
            resid_o[...] = value + x_ref[...].astype(f32)
    for copy in gu_z:
        copy.wait_recv()
    gu_local.wait()
    gu_out = [move.push(gu_all.at[dp], gu_all.at[dp], peer) for peer in p_peers]
    gu_twin = [move.push(gu_all.at[dp], gu_all.at[dp], partner)]
    for copy in share_pr:
        copy.wait_recv()
    resid = resid_o[...]
    for o in range(pairs - 1):
        resid = resid + pr_in[o].astype(f32)
    resid_o[...] = resid
    act3_own[...] = (resid * norm_scale(resid) * gains_o[1:2, :]).astype(jnp.bfloat16)
    act3_z = [move.push(act3_own, act3_all.at[fs], peer) for peer in z_peers]
    act3_local = move.local(act3_own, act3_all.at[fs])
    for o, source in enumerate(p_from):
        src = source * CORES + core
        down_out[o].wait_recv()
        down_twin.append(move.push(down_all.at[src], down_all.at[src], partner))
    for o, source in enumerate(p_from):
        src = source * CORES + core
        gu_out[o].wait_recv()
        gu_twin.append(move.push(gu_all.at[src], gu_all.at[src], partner))
    for copy in down_twin + gu_twin + cot_z + act3_z:
        copy.wait_recv()
    for copy in (down_local, cot_local, act3_local):
        copy.wait()
    move.finish()


def mixer_forward(x, cot, small, w_in, w_gate, w_up, w_out, w_down):
    dp_count, fs_count = lax.axis_size("dp"), lax.axis_size("fsdp")
    pairs = dp_count // CORES
    tokens, width = x.shape
    part = w_in.shape[0]
    feat = width // dp_count
    hid = w_gate.shape[1] // fs_count
    bf, f32 = jnp.bfloat16, jnp.float32
    shape = jax.ShapeDtypeStruct
    long = tokens + 2 * HALO
    in_vmem = [
        shape((dp_count, long, width), bf),
        shape((dp_count, long, 3 * feat), f32),
        shape((dp_count, tokens, feat), bf),
        shape((dp_count, fs_count, part, 3 * feat), bf),
        shape((fs_count, part, width), bf),
        shape((small.shape[0], width), f32),
        shape((small.shape[0], feat), f32),
        shape((tokens, width), f32),
    ]
    anywhere = [
        shape((fs_count, tokens, width), bf),
        shape((fs_count, tokens, width), bf),
        shape((dp_count, fs_count, part, 2 * hid), bf),
        shape((dp_count,) + w_down.shape, bf),
    ]
    slots = 12 * fs_count + 20 * pairs + 40
    return pl.pallas_call(
        functools.partial(mixer_forward_kernel, pairs, fs_count),
        out_shape=in_vmem + anywhere,
        in_specs=[pl.BlockSpec(memory_space=pltpu.VMEM)] * 8,
        out_specs=[pl.BlockSpec(memory_space=pltpu.VMEM)] * len(in_vmem)
        + [pl.BlockSpec(memory_space=pl.ANY)] * len(anywhere),
        scratch_shapes=[
            pltpu.VMEM((dp_count, tokens, width), bf),
            pltpu.VMEM((dp_count, 2 * HALO, width), bf),
            pltpu.VMEM((dp_count, fs_count) + small.shape, bf),
            pltpu.VMEM((CORES, pairs, part, 3 * feat), bf),
            pltpu.VMEM((pairs, part, 3 * feat), bf),
            pltpu.VMEM((fs_count, part, 2 * hid), bf),
            pltpu.VMEM((tokens, width), bf),
            pltpu.VMEM((pairs, tokens, width), bf),
            pltpu.VMEM((pairs, tokens, width), bf),
            pltpu.VMEM((pairs - 1, tokens, width), bf),
            pltpu.VMEM((pairs - 1, tokens, width), bf),
            pltpu.SemaphoreType.DMA((8,)),
            pltpu.SemaphoreType.DMA((slots,)),
            pltpu.SemaphoreType.DMA((slots,)),
        ],
        compiler_params=pltpu.CompilerParams(
            collective_id=8, has_side_effects=True, vmem_limit_bytes=40 * 1024 * 1024
        ),
        name="mixer_forward",
    )(x, cot, small, w_in, w_gate, w_up, w_out, w_down)


def mixer_backward_kernel(
    pairs, fs_count,
    x_ref, cot_ref, gains_ref, taps_ref, resid_ref, act1_ref, proj_ref, act2_ref, in_w, out_w,
    d3_ref, dn_ref, ggu_ref, gdown_ref,
    out_o, gx_o, gin_o, gout_o, ggate_o, gup_o, gdown_o, small_o,
    d3_rx, dn_rx, gu_tw, down_tw, gu_chip, down_chip, gu_rx, down_rx, gu_zo, gu_zi,
    dres_all, dproj, taps_acc, gin_p, gin_rx, gout_p, gout_rx, gin_own, gin_stage, gin_fin,
    tw_out, tw_in, pr_out, pr_in, sm_own, sm_rx, tp_rx, sm_p, sm_tw, sm_pr,
    sends, recvs,
):
    dp, fs, pair, core, partner, z_peers, p_peers, p_from = seats(pairs, fs_count)
    count = pairs * CORES
    tokens, width = x_ref.shape
    feat = width // count
    part = feat // fs_count
    hid = ggu_ref.shape[2] // 2
    inner = hid // count
    other = 1 - core
    twin_dp = pair * CORES + other
    move = Mover(sends, recvs, None)
    f32, bf = jnp.float32, jnp.bfloat16
    order = [lax.rem(pair + o, pairs) for o in range(1, pairs)] + [pair]

    greet(z_peers + p_peers + [partner])
    d3_z = [move.push(d3_ref.at[peer[1]], d3_rx.at[o], peer) for o, peer in enumerate(z_peers)]
    gu_t = [move.push(ggu_ref.at[j * CORES + other], gu_tw.at[o], partner) for o, j in enumerate(order)]
    down_t = [
        move.push(gdown_ref.at[j * CORES + other], down_tw.at[o], partner) for o, j in enumerate(order)
    ]
    gu_p, down_p = [], []
    for o, j in enumerate(order):
        gu_t[o].wait_recv()
        gu_chip[o] = (
            ggu_ref[j * CORES + core].astype(f32) + gu_tw[o].astype(f32)
        ).astype(bf)
        if o < pairs - 1:
            gu_p.append(move.push(gu_chip.at[o], gu_rx.at[o], p_peers[o]))
    for o, j in enumerate(order):
        down_t[o].wait_recv()
        down_chip[o] = (
            gdown_ref[j * CORES + core].astype(f32) + down_tw[o].astype(f32)
        ).astype(bf)
        if o < pairs - 1:
            down_p.append(move.push(down_chip.at[o], down_rx.at[o], p_peers[o]))

    for copy in d3_z:
        copy.wait_recv()
    dact3 = d3_ref[fs].astype(f32)
    for o in range(fs_count - 1):
        dact3 = dact3 + d3_rx[o].astype(f32)
    resid = resid_ref[...]
    scale2 = norm_scale(resid)
    normed2 = resid * scale2
    sm_own[1:2, :] = jnp.sum(dact3 * normed2, axis=0, keepdims=True)
    dnormed = dact3 * gains_ref[1:2, :]
    dresid = cot_ref[...].astype(f32) + scale2 * (
        dnormed - normed2 * jnp.mean(dnormed * normed2, axis=-1, keepdims=True)
    )
    gx_o[...] = dresid
    dres_all[dp, 0:tokens] = dresid.astype(bf)
    mine = dres_all.at[dp, pl.ds(0, tokens)]
    edge = dres_all.at[dp, pl.ds(tokens, HALO)]
    halo_z = move.push(dres_all.at[dp, pl.ds(0, HALO)], edge, z_peers[-1])
    dres_out = [move.push(mine, mine, peer) for peer in p_peers]
    dres_twin = [move.push(mine, mine, partner)]
    dn_z = [move.push(dn_ref.at[peer[1]], dn_rx.at[o], peer) for o, peer in enumerate(z_peers)]
    halo_z.wait_recv()
    edge_out = [move.push(edge, edge, peer) for peer in p_peers]
    dres_twin.append(move.push(edge, edge, partner))
    for o, source in enumerate(p_from):
        src = source * CORES + core
        dres_out[o].wait_recv()
        edge_out[o].wait_recv()
        dres_twin.append(move.push(dres_all.at[src], dres_all.at[src], partner))
    for copy in dres_twin:
        copy.wait_recv()

    taps_acc[...] = jnp.zeros(taps_acc.shape, f32)

    def mixer_step(i, carry):
        dact2 = product_nt(dres_all[i], out_w[...].reshape(feat, width))
        bpart = proj_ref[i, :, 0:feat]
        cpart = proj_ref[i, :, feat : 2 * feat]
        xpart = proj_ref[i, :, 2 * feat :]
        gated = bpart * xpart
        conv = taps_ref[2:3, :] * gated[HALO : HALO + tokens]
        for k in range(1, KW):
            conv = conv + taps_ref[2 + k : 3 + k, :] * gated[HALO - k : HALO - k + tokens]
        dconv = dact2 * cpart[HALO:]
        dcpart = dact2[:tokens] * conv
        dgated = taps_ref[2:3, :] * dconv[:tokens]
        for k in range(1, KW):
            dgated = dgated + taps_ref[2 + k : 3 + k, :] * dconv[k : k + tokens]
        for k in range(KW):
            taps_acc[k : k + 1, :] += jnp.sum(
                dconv[:tokens] * gated[HALO - k : HALO - k + tokens], axis=0, keepdims=True
            )
        dproj[i, :, 0:feat] = (dgated * xpart[HALO : HALO + tokens]).astype(bf)
        dproj[i, :, feat : 2 * feat] = dcpart.astype(bf)
        dproj[i, :, 2 * feat :] = (dgated * bpart[HALO : HALO + tokens]).astype(bf)
        return carry

    lax.fori_loop(0, count, mixer_step, 0)

    def in_partial(dest):
        return product_nt(dproj[dest], in_w[...].reshape(width, 3 * feat))

    share_tw = []
    for o, j in enumerate(order):
        tw_out[o] = in_partial(j * CORES + other).astype(bf)
        share_tw.append(move.push(tw_out.at[o], tw_in.at[o], partner))

    def gin_step(c, carry):
        left = act1_ref[:, pl.ds(HALO, tokens), pl.ds(pl.multiple_of(c * feat, feat), feat)]
        grad = product_tn(
            left.reshape(count * tokens, feat), dproj[...].reshape(count * tokens, 3 * feat)
        )
        gin_p[c] = grad.astype(bf).reshape(fs_count, part, 3 * feat)
        return carry

    lax.fori_loop(0, count, gin_step, 0)
    gin_z = [move.push(gin_p.at[:, peer[1]], gin_rx.at[o], peer) for o, peer in enumerate(z_peers)]

    share_pr = []
    dact1 = None
    for o, j in enumerate(order):
        value = in_partial(j * CORES + core)
        share_tw[o].wait_recv()
        value = value + tw_in[o].astype(f32)
        if o < pairs - 1:
            pr_out[o] = value.astype(bf)
            share_pr.append(move.push(pr_out.at[o], pr_in.at[o], p_peers[o]))
        else:
            dact1 = value
    grad = product_tn(
        act2_ref[...].reshape(count * tokens, feat),
        dres_all[:, 0:tokens].reshape(count * tokens, width),
    )
    gout_p[...] = grad.astype(bf).reshape(fs_count, part, width)
    gout_z = [move.push(gout_p.at[peer[1]], gout_rx.at[o], peer) for o, peer in enumerate(z_peers)]
    taps_z = [move.push(taps_acc, tp_rx.at[o], peer) for o, peer in enumerate(z_peers)]

    for copy in gu_p:
        copy.wait_recv()
    total = gu_chip[pairs - 1].astype(f32)
    for o in range(pairs - 1):
        total = total + gu_rx[o].astype(f32)
    gu_zo[...] = total.astype(bf).reshape(fs_count, part, 2 * hid)
    gu_z = [move.push(gu_zo.at[peer[1]], gu_zi.at[fs], peer) for peer in z_peers]
    gu_zi[fs] = gu_zo[fs]

    for copy in share_pr:
        copy.wait_recv()
    for o in range(pairs - 1):
        dact1 = dact1 + pr_in[o].astype(f32)
    hidden = x_ref[...].astype(f32)
    scale1 = norm_scale(hidden)
    normed1 = hidden * scale1
    sm_own[0:1, :] = jnp.sum(dact1 * normed1, axis=0, keepdims=True)
    sm_own[2:, :] = jnp.zeros((sm_own.shape[0] - 2, width), f32)
    sm_z = [move.push(sm_own, sm_rx.at[o], peer) for o, peer in enumerate(z_peers)]
    dnormed = dact1 * gains_ref[0:1, :]
    gx_o[...] += scale1 * (dnormed - normed1 * jnp.mean(dnormed * normed1, axis=-1, keepdims=True))

    for copy in gin_z:
        copy.wait_recv()
    for d in range(count):
        total = gin_p[d, fs].astype(f32)
        for o in range(fs_count - 1):
            total = total + gin_rx[o, d].astype(f32)
        gin_own[d % CORES, d // CORES] = total.astype(bf)
    gin_t = move.push(gin_own.at[other], gin_stage, partner)
    gin_out = [
        move.push(gin_own.at[core, peer[0] // CORES], gin_fin.at[dp], peer) for peer in p_peers
    ]
    gin_fin[dp] = gin_own[core, pair]
    gin_t.wait_recv()
    gin_via = [
        move.push(gin_stage.at[peer[0] // CORES], gin_fin.at[twin_dp], peer) for peer in p_peers
    ]
    gin_fin[twin_dp] = gin_stage[pair]

    for copy in sm_z:
        copy.wait_recv()
    total = sm_own[...]
    for o in range(fs_count - 1):
        total = total + sm_rx[o]
    for d in range(count):
        sm_p[d % CORES, d // CORES] = total[:, d * feat : (d + 1) * feat]
    sm_t = move.push(sm_p.at[other], sm_tw, partner)

    for copy in down_p:
        copy.wait_recv()
    total = down_chip[pairs - 1].astype(f32)
    for o in range(pairs - 1):
        total = total + down_rx[o].astype(f32)
    gdown_o[...] = total
    for copy in dn_z:
        copy.wait_recv()
    total = resid_ref[...] + dn_ref[fs].astype(f32)
    for o in range(fs_count - 1):
        total = total + dn_rx[o].astype(f32)
    out_o[...] = total.astype(bf)
    sm_t.wait_recv()
    for j in range(pairs):
        sm_tw[j] = sm_tw[j] + sm_p[core, j]
    sm_pair = [
        move.push(sm_tw.at[peer[0] // CORES], sm_pr.at[o], peer) for o, peer in enumerate(p_peers)
    ]
    for copy in gout_z + taps_z:
        copy.wait_recv()
    total = gout_p[fs].astype(f32)
    for o in range(fs_count - 1):
        total = total + gout_rx[o].astype(f32)
    gout_o[...] = total
    for copy in gu_z:
        copy.wait_recv()
    for which, ref in enumerate((ggate_o, gup_o)):
        pieces = []
        wide = [gu_zi[f, :, which * hid : (which + 1) * hid].astype(f32) for f in range(fs_count)]
        for d in range(count):
            for f in range(fs_count):
                pieces.append(wide[f][:, d * inner : (d + 1) * inner])
        ref[...] = jnp.concatenate(pieces, axis=1)
    for copy in gin_out + gin_via:
        copy.wait_recv()
    for d in range(count):
        for k in range(3):
            gin_o[:, k * width + d * feat : k * width + (d + 1) * feat] = gin_fin[
                d, :, k * feat : (k + 1) * feat
            ].astype(f32)
    for copy in sm_pair:
        copy.wait_recv()
    total = sm_tw[pair]
    for o in range(pairs - 1):
        total = total + sm_pr[o]
    taps = taps_acc[...]
    for o in range(fs_count - 1):
        taps = taps + tp_rx[o]
    small_o[0] = total
    small_o[1] = taps
    move.finish()


def mixer_backward(x, cot, gains, taps, resid, act1, proj, act2, in_w, out_w, d3, dn, ggu, gdown, part, wide_in, wide_ff):
    dp_count, fs_count = lax.axis_size("dp"), lax.axis_size("fsdp")
    pairs = dp_count // CORES
    tokens, width = x.shape
    feat = width // dp_count
    hid2 = ggu.shape[2]
    rows_down = gdown.shape[1]
    bf, f32 = jnp.bfloat16, jnp.float32
    shape = jax.ShapeDtypeStruct
    outs = [
        shape((tokens, width), bf),
        shape((tokens, width), f32),
        shape((part, wide_in), f32),
        shape((part, width), f32),
        shape((part, wide_ff), f32),
        shape((part, wide_ff), f32),
        shape((rows_down, width), f32),
        shape((2, 8, feat), f32),
    ]
    slots = 12 * fs_count + 20 * pairs + 40
    scratch = [
        ((fs_count - 1, tokens, width), bf),
        ((fs_count - 1, tokens, width), bf),
        ((pairs, feat, hid2), bf),
        ((pairs, rows_down, width), bf),
        ((pairs, feat, hid2), bf),
        ((pairs, rows_down, width), bf),
        ((pairs - 1, feat, hid2), bf),
        ((pairs - 1, rows_down, width), bf),
        ((fs_count, part, hid2), bf),
        ((fs_count, part, hid2), bf),
        ((dp_count, tokens + HALO, width), bf),
        ((dp_count, tokens, 3 * feat), bf),
        ((8, feat), f32),
        ((dp_count, fs_count, part, 3 * feat), bf),
        ((fs_count - 1, dp_count, part, 3 * feat), bf),
        ((fs_count, part, width), bf),
        ((fs_count - 1, part, width), bf),
        ((CORES, pairs, part, 3 * feat), bf),
        ((pairs, part, 3 * feat), bf),
        ((dp_count, part, 3 * feat), bf),
        ((pairs, tokens, width), bf),
        ((pairs, tokens, width), bf),
        ((pairs - 1, tokens, width), bf),
        ((pairs - 1, tokens, width), bf),
        ((8, width), f32),
        ((fs_count - 1, 8, width), f32),
        ((fs_count - 1, 8, feat), f32),
        ((CORES, pairs, 8, feat), f32),
        ((pairs, 8, feat), f32),
        ((pairs - 1, 8, feat), f32),
    ]
    return pl.pallas_call(
        functools.partial(mixer_backward_kernel, pairs, fs_count),
        out_shape=outs,
        in_specs=[pl.BlockSpec(memory_space=pltpu.VMEM)] * 14,
        out_specs=[pl.BlockSpec(memory_space=pltpu.VMEM)] * len(outs),
        scratch_shapes=[pltpu.VMEM(s, d) for s, d in scratch]
        + [pltpu.SemaphoreType.DMA((slots,)), pltpu.SemaphoreType.DMA((slots,))],
        compiler_params=pltpu.CompilerParams(
            collective_id=9, has_side_effects=True, vmem_limit_bytes=58 * 1024 * 1024
        ),
        name="mixer_backward",
    )(x, cot, gains, taps, resid, act1, proj, act2, in_w, out_w, d3, dn, ggu, gdown)


def split_tokens(
    inputs,
    gain_mixer,
    weight_in,
    conv_taps,
    weight_out,
    gain_ffn,
    weight_gate,
    weight_up,
    weight_down,
    cotangent,
):
    dp_count, fs_count = lax.axis_size("dp"), lax.axis_size("fsdp")
    fs = lax.axis_index("fsdp")
    tokens, width = inputs.shape[1:]
    part = weight_out.shape[0]
    hid = weight_gate.shape[1] // fs_count
    bf = jnp.bfloat16
    x, cot = inputs[0], cotangent[0]
    small = jnp.concatenate([gain_mixer[None], gain_ffn[None], conv_taps], axis=0)
    small = jnp.tile(jnp.pad(small, ((0, 16 - small.shape[0]), (0, 0))), (1, fs_count))
    lanes = lax.broadcasted_iota(jnp.int32, small.shape, 1)
    mine = (lanes >= fs * part) & (lanes < (fs + 1) * part)
    small = jnp.where(mine, small, jnp.zeros_like(small))
    (act1, proj, act2, in_w, out_w, gains, taps, resid, act3_all, cot_all, gu_cols, down_rows) = mixer_forward(
        x, cot, small, weight_in, weight_gate, weight_up, weight_out, weight_down
    )
    act3_all = act3_all.reshape(-1, width)
    grad_all = cot_all.reshape(-1, width)
    gu_cols = gu_cols.reshape(width, 2 * hid)
    down_rows = down_rows.reshape(hid, width)
    gate_up = product(act3_all, gu_cols)
    gate, upval = gate_up[:, :hid], gate_up[:, hid:]
    sig = jax.nn.sigmoid(gate)
    act4 = (gate * sig * upval).astype(bf)
    dact4 = product_nt(grad_all, down_rows)
    dgate = (dact4 * upval * sig * (1.0 + gate * (1.0 - sig))).astype(bf)
    dupval = (dact4 * gate * sig).astype(bf)
    dgu = jnp.concatenate([dgate, dupval], axis=1)
    d3 = token_pieces(product_nt(dgu, gu_cols))
    dn = token_pieces(product(act4, down_rows))
    ggu = product_tn(act3_all, dgu).astype(bf).reshape(dp_count, width // dp_count, 2 * hid)
    gdown = product_tn(act4, grad_all).astype(bf).reshape((dp_count,) + weight_down.shape)
    outputs, gx, gin, gout, ggate, gup, gdn, small_g = mixer_backward(
        x, cot, gains, taps, resid, act1, proj, act2, in_w, out_w, d3, dn, ggu, gdown,
        part, weight_in.shape[1], weight_gate.shape[1],
    )
    small_g = lax.dynamic_slice_in_dim(small_g, fs * part, part, axis=2)
    return (
        outputs[None], gx[None], small_g[0, 0], gin, small_g[1, :KW], gout, small_g[0, 1], ggate, gup, gdn,
    )


def fits_tokens(inputs, weight_out, weight_gate):
    dp_count, fs_count = lax.axis_size("dp"), lax.axis_size("fsdp")
    tokens, width = inputs.shape[1:]
    return (
        dp_count % CORES == 0
        and dp_count > CORES
        and fs_count > 1
        and (width // dp_count) % 128 == 0
        and (weight_gate.shape[1] // fs_count) % 128 == 0
        and weight_out.shape[0] % 16 == 0
        and tokens % 16 == 0
        and inputs.shape[0] == 1
    )


def on_device(
    inputs,
    gain_mixer,
    weight_in,
    conv_taps,
    weight_out,
    gain_ffn,
    weight_gate,
    weight_up,
    weight_down,
    cotangent,
):
    form = split_tokens if fits_tokens(inputs, weight_out, weight_gate) else split_features
    return form(
        inputs,
        gain_mixer,
        weight_in,
        conv_taps,
        weight_out,
        gain_ffn,
        weight_gate,
        weight_up,
        weight_down,
        cotangent,
    )


def solution(mesh):
    in_specs = (
        P("dp", "fsdp", None),
        P(("dp", "fsdp")),
        P(("dp", "fsdp"), None),
        P(None, ("dp", "fsdp")),
        P(("dp", "fsdp"), None),
        P(("dp", "fsdp")),
        P(("dp", "fsdp"), None),
        P(("dp", "fsdp"), None),
        P(("dp", "fsdp"), None),
        P("dp", "fsdp", None),
    )
    out_specs = (
        P("dp", "fsdp", None),
        P("dp", "fsdp", None),
        P(("dp", "fsdp")),
        P(("dp", "fsdp"), None),
        P(None, ("dp", "fsdp")),
        P(("dp", "fsdp"), None),
        P(("dp", "fsdp")),
        P(("dp", "fsdp"), None),
        P(("dp", "fsdp"), None),
        P(("dp", "fsdp"), None),
    )
    return jax.shard_map(
        on_device, mesh=mesh, in_specs=in_specs, out_specs=out_specs, check_vma=False
    )
```

```python
import functools

import jax
import jax.numpy as jnp
from jax import lax
from jax.experimental import pallas as pl
from jax.experimental.pallas import tpu as pltpu
from jax.sharding import PartitionSpec as P

KW = 3


EPS = 1e-05

CORES = 2
MESH = pl.DeviceIdType.MESH


def product(left, right):
    return jnp.dot(left, right, preferred_element_type=jnp.float32)


def product_tn(left, right):
    return lax.dot_general(
        left, right, (((0,), (0,)), ((), ())), preferred_element_type=jnp.float32
    )


def product_nt(left, right):
    return lax.dot_general(
        left, right, (((1,), (1,)), ((), ())), preferred_element_type=jnp.float32
    )


def norm_forward(hidden, gain):
    scale = lax.rsqrt(jnp.mean(hidden * hidden, axis=-1, keepdims=True) + EPS)
    normed = hidden * scale
    return (normed, scale, normed * gain.astype(jnp.float32))


def norm_backward(dact, normed, scale, gain):
    dnormed = dact * gain.astype(jnp.float32)
    dhidden = scale * (dnormed - normed * jnp.mean(dnormed * normed, axis=-1, keepdims=True))
    return (dhidden, jnp.sum(dact * normed, axis=0))


def lagged(values, offset):
    zeros = jnp.zeros((offset, values.shape[1]), values.dtype)
    return jnp.concatenate([zeros, values[: values.shape[0] - offset]], axis=0)


def leading(values, offset):
    zeros = jnp.zeros((offset, values.shape[1]), values.dtype)
    return jnp.concatenate([values[offset:], zeros], axis=0)


def column_blocks(shard, lead, dp_count, fs_count):
    rows, columns = shard.shape
    inner = columns // (lead * dp_count * fs_count)
    pieces = shard.reshape(rows, lead, dp_count, fs_count, inner).transpose(3, 0, 1, 2, 4)
    return pieces.reshape(fs_count, rows, lead * dp_count * inner)


def column_join(blocks, lead, dp_count, fs_count):
    _, rows, columns = blocks.shape
    inner = columns // (lead * dp_count)
    pieces = blocks.reshape(fs_count, rows, lead, dp_count, inner).transpose(1, 2, 3, 0, 4)
    return pieces.reshape(rows, lead * dp_count * fs_count * inner)


def greet(peers):
    barrier = pltpu.get_barrier_semaphore()
    for peer in peers:
        pl.semaphore_signal(barrier, inc=1, device_id=peer, device_id_type=MESH)
    pl.semaphore_wait(barrier, len(peers))


def push(src, dst, sends, recvs, index, peer):
    copy = pltpu.make_async_remote_copy(
        src_ref=src,
        dst_ref=dst,
        send_sem=sends.at[index],
        recv_sem=recvs.at[index],
        device_id=peer,
        device_id_type=MESH,
    )
    copy.start()
    return copy


def place():
    dp, fs = lax.axis_index("dp"), lax.axis_index("fsdp")
    pair, core = dp // CORES, lax.rem(dp, CORES)
    return dp, fs, pair, core, (pair * CORES + 1 - core, fs)


def gather_kernel(
    pairs, fs_count,
    x_ref, cot_ref, small_ref, in_ref, gu_ref, out_ref, down_ref,
    x_all, cot_all, small_all, in_all, gu_all, out_all, down_all,
    local_sem, z_send, z_recv, p_send, p_recv, c_send, c_recv,
):
    dp, fs, pair, core, partner = place()
    z_peers = [(dp, lax.rem(fs + o, fs_count)) for o in range(1, fs_count)]
    p_peers = [(lax.rem(pair + o, pairs) * CORES + core, fs) for o in range(1, pairs)]
    p_from = [lax.rem(pair + pairs - o, pairs) * CORES + core for o in range(1, pairs)]
    greet(z_peers + p_peers + [partner])
    spread = [small_all, in_all, gu_all, out_all, down_all]

    across = [[None] * len(p_peers) for _ in spread]
    twins = [[None] * pairs for _ in spread]

    def spread_own(kind, src):
        dst = spread[kind].at[dp]
        for o, peer in enumerate(p_peers):
            across[kind][o] = push(src, dst, p_send, p_recv, (kind, o), peer)
        twins[kind][0] = push(src, dst, c_send, c_recv, (kind, 0), partner)

    along = [[], [], [], [], []]
    for o, peer in enumerate(z_peers):
        to = peer[1]
        along[0].append(push(small_ref, small_all.at[dp, fs], z_send, z_recv, (0, o), peer))
        along[1].append(push(in_ref.at[to], in_all.at[dp, fs], z_send, z_recv, (1, o), peer))
    for o, peer in enumerate(z_peers):
        to = peer[1]
        along[2].append(push(gu_ref.at[to], gu_all.at[dp, fs], z_send, z_recv, (2, o), peer))
    for o, peer in enumerate(z_peers):
        along[3].append(push(x_ref, x_all.at[fs], z_send, z_recv, (3, o), peer))
    for o, peer in enumerate(z_peers):
        along[4].append(push(cot_ref, cot_all.at[fs], z_send, z_recv, (4, o), peer))
    spread_own(3, out_ref)
    spread_own(4, down_ref)
    local = []
    for index, (src, dst) in enumerate(
        [
            (small_ref, small_all.at[dp, fs]),
            (in_ref.at[fs], in_all.at[dp, fs]),
            (gu_ref.at[fs], gu_all.at[dp, fs]),
            (x_ref, x_all.at[fs]),
            (cot_ref, cot_all.at[fs]),
            (out_ref, out_all.at[dp]),
            (down_ref, down_all.at[dp]),
        ]
    ):
        copy = pltpu.make_async_copy(src, dst, local_sem.at[index])
        copy.start()
        local.append(copy)
    for kind in range(3):
        local[kind].wait()
        for copy in along[kind]:
            copy.wait_recv()
        spread_own(kind, spread[kind].at[dp])
    for kind in (3, 0, 1, 4, 2):
        for o, source in enumerate(p_from):
            across[kind][o].wait_recv()
            block = spread[kind].at[source]
            twins[kind][o + 1] = push(block, block, c_send, c_recv, (kind, o + 1), partner)
    for copy in local[3:]:
        copy.wait()
    for copy in along[3] + along[4]:
        copy.wait_recv()
    for row in along + across:
        for copy in row:
            copy.wait_send()
    for row in twins:
        for copy in row:
            copy.wait()


def gather_all(x, cot, small, in_blocks, gu_blocks, out_shard, down_shard):
    dp_count, fs_count = lax.axis_size("dp"), lax.axis_size("fsdp")
    pairs = dp_count // CORES
    arrays = (x, cot, small, in_blocks, gu_blocks, out_shard, down_shard)
    shapes = (
        (fs_count,) + x.shape,
        (fs_count,) + cot.shape,
        (dp_count, fs_count) + small.shape,
        (dp_count,) + in_blocks.shape,
        (dp_count,) + gu_blocks.shape,
        (dp_count,) + out_shard.shape,
        (dp_count,) + down_shard.shape,
    )
    return pl.pallas_call(
        functools.partial(gather_kernel, pairs, fs_count),
        out_shape=[jax.ShapeDtypeStruct(shape, x.dtype) for shape in shapes],
        in_specs=[pl.BlockSpec(memory_space=pltpu.VMEM)] * len(arrays),
        out_specs=[pl.BlockSpec(memory_space=pl.ANY)] * len(shapes),
        scratch_shapes=[
            pltpu.SemaphoreType.DMA((7,)),
            pltpu.SemaphoreType.DMA((5, fs_count - 1)),
            pltpu.SemaphoreType.DMA((5, fs_count - 1)),
            pltpu.SemaphoreType.DMA((5, pairs - 1)),
            pltpu.SemaphoreType.DMA((5, pairs - 1)),
            pltpu.SemaphoreType.DMA((5, pairs)),
            pltpu.SemaphoreType.DMA((5, pairs)),
        ],
        compiler_params=pltpu.CompilerParams(collective_id=0, has_side_effects=True),
        name="gather_all",
    )(*arrays)


def line_kernel(count, fs_count, whole, *refs):
    sources, landed = refs[:count], refs[count : 2 * count]
    local_sem, sends, recvs = refs[2 * count :]
    dp, fs, _, _, _ = place()
    targets = [lax.rem(fs + o, fs_count) for o in range(1, fs_count)]
    greet([(dp, to) for to in targets])
    copies = [
        push(src if whole else src.at[to], dst.at[fs], sends, recvs, (k, o), (dp, to))
        for k, (src, dst) in enumerate(zip(sources, landed))
        for o, to in enumerate(targets)
    ]
    local = []
    for k, (src, dst) in enumerate(zip(sources, landed)):
        copy = pltpu.make_async_copy(src if whole else src.at[fs], dst.at[fs], local_sem.at[k])
        copy.start()
        local.append(copy)
    for copy in local + copies:
        copy.wait()


def along_line(arrays, whole, collective_id, name):
    fs_count = lax.axis_size("fsdp")
    count = len(arrays)
    return pl.pallas_call(
        functools.partial(line_kernel, count, fs_count, whole),
        out_shape=[
            jax.ShapeDtypeStruct(((fs_count,) + a.shape) if whole else a.shape, a.dtype)
            for a in arrays
        ],
        in_specs=[pl.BlockSpec(memory_space=pltpu.VMEM)] * count,
        out_specs=[pl.BlockSpec(memory_space=pl.ANY)] * count,
        scratch_shapes=[
            pltpu.SemaphoreType.DMA((count,)),
            pltpu.SemaphoreType.DMA((count, fs_count - 1)),
            pltpu.SemaphoreType.DMA((count, fs_count - 1)),
        ],
        compiler_params=pltpu.CompilerParams(collective_id=collective_id, has_side_effects=True),
        name=name,
    )(*arrays)


def whole_sequence(rows, collective_id, name):
    (received,) = along_line([rows], True, collective_id, name)
    return received.reshape(-1, rows.shape[1])


def token_pieces(partial_value):
    fs_count = lax.axis_size("fsdp")
    rows, columns = partial_value.shape
    return partial_value.astype(jnp.bfloat16).reshape(fs_count, rows // fs_count, columns)


def token_share(partial_value, collective_id, name):
    (received,) = along_line([token_pieces(partial_value)], False, collective_id, name)
    return jnp.sum(received.astype(jnp.float32), axis=0)


def token_share_async(partial_value):
    received = lax.all_to_all(
        token_pieces(partial_value), "fsdp", split_axis=0, concat_axis=0, tiled=True
    )
    return jnp.sum(received.astype(jnp.float32), axis=0)


def twin_kernel(count, pairs, *refs):
    partials, received = refs[:count], refs[count : 2 * count]
    sends, recvs = refs[2 * count :]
    _, _, _, core, partner = place()
    greet([partner])
    copies = [
        push(partial.at[j, 1 - core], landed.at[j], sends, recvs, (k, j), partner)
        for k, (partial, landed) in enumerate(zip(partials, received))
        for j in range(pairs)
    ]
    for copy in copies:
        copy.wait()


def pair_kernel(count, pairs, fs_count, *refs):
    partials, pieces = refs[:count], refs[count]
    received, pieces_in = refs[count + 1 : 2 * count + 1], refs[2 * count + 1]
    sends, recvs, z_sends, z_recvs = refs[2 * count + 2 :]
    dp, fs, pair, core, _ = place()
    targets = [lax.rem(pair + o, pairs) for o in range(1, pairs)]
    peers = [(to * CORES + core, fs) for to in targets]
    z_targets = [lax.rem(fs + o, fs_count) for o in range(1, fs_count)]
    greet(peers + [(dp, to) for to in z_targets])
    copies = [
        push(partial.at[to], landed.at[o], sends, recvs, (k, o), peer)
        for k, (partial, landed) in enumerate(zip(partials, received))
        for o, (to, peer) in enumerate(zip(targets, peers))
    ]
    copies += [
        push(pieces.at[to], pieces_in.at[o], z_sends, z_recvs, o, (dp, to))
        for o, to in enumerate(z_targets)
    ]
    for copy in copies:
        copy.wait()


def twin_exchange(partials):
    count = len(partials)
    pairs = lax.axis_size("dp") // CORES
    return pl.pallas_call(
        functools.partial(twin_kernel, count, pairs),
        out_shape=[jax.ShapeDtypeStruct((pairs,) + p.shape[-2:], p.dtype) for p in partials],
        in_specs=[pl.BlockSpec(memory_space=pl.ANY)] * count,
        out_specs=[pl.BlockSpec(memory_space=pl.ANY)] * count,
        scratch_shapes=[pltpu.SemaphoreType.DMA((count, pairs))] * 2,
        compiler_params=pltpu.CompilerParams(collective_id=1, has_side_effects=True),
        name="twin_exchange",
    )(*partials)


def pair_exchange(partials, pieces):
    count = len(partials)
    pairs, fs_count = lax.axis_size("dp") // CORES, lax.axis_size("fsdp")
    slots = [(pairs - 1, p) for p in partials] + [(fs_count - 1, pieces)]
    return pl.pallas_call(
        functools.partial(pair_kernel, count, pairs, fs_count),
        out_shape=[jax.ShapeDtypeStruct((n,) + p.shape[-2:], p.dtype) for n, p in slots],
        in_specs=[pl.BlockSpec(memory_space=pl.ANY)] * len(slots),
        out_specs=[pl.BlockSpec(memory_space=pl.ANY)] * len(slots),
        scratch_shapes=[
            pltpu.SemaphoreType.DMA((count, pairs - 1)),
            pltpu.SemaphoreType.DMA((count, pairs - 1)),
            pltpu.SemaphoreType.DMA((fs_count - 1,)),
            pltpu.SemaphoreType.DMA((fs_count - 1,)),
        ],
        compiler_params=pltpu.CompilerParams(collective_id=2, has_side_effects=True),
        name="pair_exchange",
    )(*partials, pieces)


def reduce_all(partials, pieces):
    dp_count = lax.axis_size("dp")
    pairs = dp_count // CORES
    dp = lax.axis_index("dp")
    core, pair = lax.rem(dp, CORES), dp // CORES
    split = [
        p.reshape(pairs, CORES, p.shape[0] // dp_count, p.shape[1])
        for p in partials
    ]
    landed = twin_exchange(split)
    chip = [
        (
            lax.dynamic_index_in_dim(p, core, axis=1, keepdims=False).astype(jnp.float32)
            + r.astype(jnp.float32)
        ).astype(p.dtype)
        for p, r in zip(split, landed)
    ]
    *others, pieces_in = pair_exchange(chip, pieces)
    own_piece = lax.dynamic_index_in_dim(pieces, lax.axis_index("fsdp"), axis=0, keepdims=False)
    tokens = own_piece.astype(jnp.float32) + jnp.sum(pieces_in.astype(jnp.float32), axis=0)
    return tokens, [
        lax.dynamic_index_in_dim(p, pair, axis=0, keepdims=False).astype(jnp.float32)
        + jnp.sum(r.astype(jnp.float32), axis=0)
        for p, r in zip(chip, others)
    ]


def split_features(
    inputs,
    gain_mixer,
    weight_in,
    conv_taps,
    weight_out,
    gain_ffn,
    weight_gate,
    weight_up,
    weight_down,
    cotangent,
):
    dp_count = lax.axis_size("dp")
    fs_count = lax.axis_size("fsdp")
    width = weight_out.shape[1]
    part = weight_out.shape[0]
    quarter = dp_count * part
    hid = dp_count * weight_down.shape[0]

    small = jnp.concatenate([gain_mixer[None], gain_ffn[None], conv_taps], axis=0)
    lanes = max(128, part)
    small = jnp.pad(small, ((0, 8 - small.shape[0]), (0, lanes - part)))
    gu_blocks = jnp.concatenate(
        [
            column_blocks(weight_gate, 1, dp_count, fs_count),
            column_blocks(weight_up, 1, dp_count, fs_count),
        ],
        axis=2,
    )
    grad_out = cotangent[0]
    x_all, grad_all, small_all, in_cols, gu_cols, out_rows, down_rows = gather_all(
        inputs[0],
        grad_out,
        small,
        column_blocks(weight_in, 3, dp_count, fs_count),
        gu_blocks,
        weight_out,
        weight_down,
    )
    x_all = x_all.reshape(-1, width)
    grad_all = grad_all.reshape(-1, width)
    in_cols = in_cols.reshape(width, 3 * quarter)
    gu_cols = gu_cols.reshape(width, 2 * hid)
    out_rows = out_rows.reshape(quarter, width)
    down_rows = down_rows.reshape(hid, width)
    small_all = small_all[:, :, : KW + 2, :part]
    gain1 = small_all[:, :, 0].reshape(width)
    gain2 = small_all[:, :, 1].reshape(width)
    taps32 = (
        lax.dynamic_index_in_dim(small_all, lax.axis_index("fsdp"), axis=1, keepdims=False)[:, 2:]
        .transpose(1, 0, 2)
        .reshape(KW, quarter)
        .astype(jnp.float32)
    )

    _, _, pre1_all = norm_forward(x_all.astype(jnp.float32), gain1)
    act1_all = pre1_all.astype(jnp.bfloat16)
    projected = product(act1_all, in_cols)
    bpart = projected[:, :quarter]
    cpart = projected[:, quarter : 2 * quarter]
    xpart = projected[:, 2 * quarter :]
    gated = bpart * xpart
    lagged_rows = [lagged(gated, offset) for offset in range(KW)]
    conv = taps32[0] * lagged_rows[0]
    for offset in range(1, KW):
        conv = conv + taps32[offset] * lagged_rows[offset]
    act2 = (cpart * conv).astype(jnp.bfloat16)
    hidden = inputs[0].astype(jnp.float32)
    normed1, scale1, _ = norm_forward(hidden, gain1)
    resid = hidden + token_share(product(act2, out_rows), 3, "share_out")
    normed2, scale2, pre2 = norm_forward(resid, gain2)
    act3_all = whole_sequence(pre2.astype(jnp.bfloat16), 4, "gather_ffn")
    gate_up = product(act3_all, gu_cols)
    gate, upval = gate_up[:, :hid], gate_up[:, hid:]
    sig = jax.nn.sigmoid(gate)
    act4 = (gate * sig * upval).astype(jnp.bfloat16)
    dact4 = product_nt(grad_all, down_rows)
    dgate = (dact4 * upval * sig * (1.0 + gate * (1.0 - sig))).astype(jnp.bfloat16)
    dupval = (dact4 * gate * sig).astype(jnp.bfloat16)
    dgu = jnp.concatenate([dgate, dupval], axis=1)
    dact3 = token_share(product_nt(dgu, gu_cols), 5, "share_ffn")
    down_pieces = token_pieces(product(act4, down_rows))
    dnorm2, g_gain2 = norm_backward(dact3, normed2, scale2, gain2)
    dresid = grad_out.astype(jnp.float32) + dnorm2
    dres_all = whole_sequence(dresid.astype(jnp.bfloat16), 6, "gather_dres")
    dact2 = product_nt(dres_all, out_rows)
    dcpart = dact2 * conv
    dconv = dact2 * cpart
    g_taps = jnp.stack(
        [jnp.sum(dconv * lagged_rows[offset], axis=0) for offset in range(KW)], axis=0
    )
    dgated = taps32[0] * dconv
    for offset in range(1, KW):
        dgated = dgated + taps32[offset] * leading(dconv, offset)
    dproj = jnp.concatenate([dgated * xpart, dcpart, dgated * bpart], axis=1).astype(jnp.bfloat16)
    dact1 = token_share_async(product_nt(dproj, in_cols))
    dnorm1, g_gain1 = norm_backward(dact1, normed1, scale1, gain1)
    grad_inputs = dresid + dnorm1

    own_column = (jnp.arange(fs_count) == lax.axis_index("fsdp"))[None, None, :, None]
    taps_spread = jnp.where(own_column, g_taps.reshape(KW, dp_count, 1, part), 0.0).reshape(KW, width)
    small_grad = jnp.concatenate([g_gain1[None], g_gain2[None], taps_spread], axis=0)
    small_grad = jnp.pad(small_grad, ((0, 8 - small_grad.shape[0]), (0, 0)))
    small_grad = small_grad.reshape(8, dp_count, fs_count, part).transpose(1, 2, 0, 3)
    small_grad = jnp.pad(small_grad, ((0, 0), (0, 0), (0, 0), (0, lanes - part)))
    down_sum, (g_small, g_gu, g_down, g_in, g_out) = reduce_all(
        [small_grad.reshape(dp_count * fs_count * 8, lanes)]
        + [
            grad.astype(jnp.bfloat16)
            for grad in (
                product_tn(act3_all, dgu),
                product_tn(act4, grad_all),
                product_tn(act1_all, dproj),
                product_tn(act2, dres_all),
            )
        ],
        down_pieces,
    )
    outputs = (resid + down_sum).astype(jnp.bfloat16)
    moved = jnp.concatenate([g_in, g_gu], axis=1).astype(jnp.bfloat16)
    moved, small_parts = along_line(
        [
            moved.reshape(fs_count, part, 3 * quarter + 2 * hid),
            g_small.reshape(fs_count, 8, lanes),
        ],
        False,
        7,
        "owner_exchange",
    )
    moved = moved.astype(jnp.float32)
    g_in_owned = moved[:, :, : 3 * quarter]
    g_gu_owned = moved[:, :, 3 * quarter :]
    small_owned = jnp.sum(small_parts, axis=0)[: KW + 2, :part]
    return (
        outputs[None],
        grad_inputs[None],
        small_owned[0],
        column_join(g_in_owned, 3, dp_count, fs_count),
        small_owned[2:],
        g_out,
        small_owned[1],
        column_join(g_gu_owned[:, :, :hid], 1, dp_count, fs_count),
        column_join(g_gu_owned[:, :, hid:], 1, dp_count, fs_count),
        g_down,
    )

HALO = 16


class Mover:
    def __init__(self, sends, recvs, locals_):
        self.sends, self.recvs, self.locals = sends, recvs, locals_
        self.count = 0
        self.local_count = 0
        self.open = []

    def push(self, src, dst, peer):
        copy = push(src, dst, self.sends, self.recvs, self.count, peer)
        self.count += 1
        self.open.append(copy)
        return copy

    def local(self, src, dst):
        copy = pltpu.make_async_copy(src, dst, self.locals.at[self.local_count])
        self.local_count += 1
        copy.start()
        return copy

    def finish(self):
        for copy in self.open:
            copy.wait_send()


class Line:
    def __init__(self, move, slot, dp, fs, fs_count):
        self.move, self.slot, self.dp, self.fs, self.size = move, slot, dp, fs, fs_count
        self.base = move.count
        move.count += CORES * fs_count

    def copy(self, source, up):
        index = self.base + CORES * source + (1 if up else 0)
        to = lax.rem(self.fs + (1 if up else self.size - 1), self.size)
        return pltpu.make_async_remote_copy(
            src_ref=self.slot(source),
            dst_ref=self.slot(source),
            send_sem=self.move.sends.at[index],
            recv_sem=self.move.recvs.at[index],
            device_id=(self.dp, to),
            device_id_type=MESH,
        )

    def start(self):
        @pl.when(self.fs < self.size - 1)
        def _():
            self.copy(self.fs, True).start()

        @pl.when(self.fs > 0)
        def _():
            self.copy(self.fs, False).start()

    def step(self, hop):
        below, above = self.fs - hop, self.fs + hop

        @pl.when(below >= 0)
        def _():
            self.copy(below, True).wait_recv()

            @pl.when(self.fs < self.size - 1)
            def _():
                self.copy(below, True).start()

        @pl.when(above < self.size)
        def _():
            self.copy(above, False).wait_recv()

            @pl.when(self.fs > 0)
            def _():
                self.copy(above, False).start()

    def finish(self):
        for hop in range(self.size):

            @pl.when((self.fs - hop >= 0) & (self.fs < self.size - 1))
            def _():
                self.copy(self.fs - hop, True).wait_send()

            @pl.when((self.fs + hop < self.size) & (self.fs > 0))
            def _():
                self.copy(self.fs + hop, False).wait_send()


def seats(pairs, fs_count):
    dp, fs, pair, core, partner = place()
    z_peers = [(dp, lax.rem(fs + o, fs_count)) for o in range(1, fs_count)]
    p_peers = [(lax.rem(pair + o, pairs) * CORES + core, fs) for o in range(1, pairs)]
    p_from = [lax.rem(pair + pairs - o, pairs) for o in range(1, pairs)]
    return dp, fs, pair, core, partner, z_peers, p_peers, p_from


def norm_scale(hidden):
    return lax.rsqrt(jnp.mean(hidden * hidden, axis=-1, keepdims=True) + EPS)


def mixer_forward_kernel(
    pairs, fs_count,
    x_ref, cot_ref, small_ref, in_hbm, gate_hbm, up_hbm, out_ref, down_ref,
    act1_o, proj_o, act2_o, in_all, out_all, gains_o, taps_o, resid_o,
    act3_all, cot_all, gu_all, down_all,
    x_all, halo_all, small_all, in_ref, gate_ref, up_ref, in_blk, in_stage, gu_blk,
    tw_out, tw_in, pr_out, pr_in, local_sem, sends, recvs,
):
    dp, fs, pair, core, partner, z_peers, p_peers, p_from = seats(pairs, fs_count)
    count = pairs * CORES
    tokens, width = x_ref.shape
    part = in_ref.shape[0]
    feat = width // count
    inner = gate_ref.shape[1] // (count * fs_count)
    hid = inner * count
    other = 1 - core
    move = Mover(sends, recvs, local_sem)
    f32 = jnp.float32

    in_local = move.local(in_hbm, in_ref)
    x_local = move.local(x_ref, x_all.at[dp])
    gate_local = move.local(gate_hbm, gate_ref)
    up_local = move.local(up_hbm, up_ref)
    out_local = move.local(out_ref, out_all.at[fs])
    cot_local = move.local(cot_ref, cot_all.at[fs])
    down_local = move.local(down_ref, down_all.at[dp])
    greet(z_peers + p_peers + [partner])
    small_z = [move.push(small_ref, small_all.at[dp, fs], peer) for peer in z_peers]
    halo_next = move.push(x_ref.at[pl.ds(tokens - HALO, HALO)], halo_all.at[dp, pl.ds(0, HALO)], z_peers[0])
    halo_prev = move.push(x_ref.at[pl.ds(0, HALO)], halo_all.at[dp, pl.ds(HALO, HALO)], z_peers[-1])
    in_local.wait()
    for to in range(count):
        for k in range(3):
            in_blk[to % CORES, to // CORES, :, k * feat : (k + 1) * feat] = in_ref[
                :, k * width + to * feat : k * width + (to + 1) * feat
            ]
    in_twin = move.push(in_blk.at[other], in_stage, partner)
    in_out = [move.push(in_blk.at[core, peer[0] // CORES], in_all.at[dp, fs], peer) for peer in p_peers]
    x_out = [move.push(x_ref, x_all.at[dp], peer) for peer in p_peers]
    x_twin = move.push(x_ref, x_all.at[dp], partner)
    small_all[dp, fs] = small_ref[...]
    in_all[dp, fs] = in_blk[core, pair]
    in_twin.wait_recv()
    twin_dp = pair * CORES + other
    in_all[twin_dp, fs] = in_stage[pair]
    in_via = [
        move.push(in_stage.at[peer[0] // CORES], in_all.at[twin_dp, fs], peer) for peer in p_peers
    ]
    for copy in small_z:
        copy.wait_recv()
    small_out = [move.push(small_all.at[dp], small_all.at[dp], peer) for peer in p_peers]
    small_twin = [move.push(small_all.at[dp], small_all.at[dp], partner)]
    halo_next.wait_recv()
    halo_prev.wait_recv()
    halo_out = [move.push(halo_all.at[dp], halo_all.at[dp], peer) for peer in p_peers]
    halo_twin = [move.push(halo_all.at[dp], halo_all.at[dp], partner)]
    for copy in in_out + in_via:
        copy.wait_recv()
    in_line = Line(move, lambda f: in_all.at[:, f], dp, fs, fs_count)
    out_line = Line(move, lambda f: out_all.at[f], dp, fs, fs_count)
    cot_line = Line(move, lambda f: cot_all.at[f], dp, fs, fs_count)
    act3_line = Line(move, lambda f: act3_all.at[f], dp, fs, fs_count)
    in_line.start()
    out_local.wait()
    out_line.start()
    down_out = [move.push(down_ref, down_all.at[dp], peer) for peer in p_peers]
    down_twin = [move.push(down_ref, down_all.at[dp], partner)]
    gate_local.wait()
    up_local.wait()
    for which, ref in enumerate((gate_ref, up_ref)):
        wide = ref[...].astype(f32)
        for to in range(fs_count):
            pieces = [
                wide[:, (d * fs_count + to) * inner : (d * fs_count + to + 1) * inner]
                for d in range(count)
            ]
            gu_blk[to, :, which * hid : (which + 1) * hid] = jnp.concatenate(pieces, axis=1).astype(
                jnp.bfloat16
            )
    gu_local = move.local(gu_blk.at[fs], gu_all.at[dp, fs])
    in_line.step(1)
    out_line.step(1)

    small_rel, x_rel = [], []
    for o, source in enumerate(p_from):
        src = source * CORES + core
        small_out[o].wait_recv()
        halo_out[o].wait_recv()
        x_out[o].wait_recv()
        small_rel.append(move.push(small_all.at[src], small_all.at[src], partner))
        x_rel.append(move.push(halo_all.at[src], halo_all.at[src], partner))
        x_rel.append(move.push(x_all.at[src], x_all.at[src], partner))
    in_line.step(2)
    out_line.step(2)
    gu_z = [move.push(gu_blk.at[peer[1]], gu_all.at[dp, fs], peer) for peer in z_peers]
    for copy in small_twin + small_rel + [x_twin] + halo_twin + x_rel:
        copy.wait_recv()
    x_local.wait()

    for d in range(count):
        total = small_all[d, 0].astype(f32)
        for f in range(1, fs_count):
            total = total + small_all[d, f].astype(f32)
        gains_o[:, d * feat : (d + 1) * feat] = total
    total = small_all[dp, 0].astype(f32)
    for f in range(1, fs_count):
        total = total + small_all[dp, f].astype(f32)
    taps_o[...] = total
    has_prev, has_next = fs > 0, fs < fs_count - 1

    def norm_step(i, carry):
        gain = gains_o[0:1, :]
        rows = x_all[i].astype(f32)
        act1_o[i, HALO : HALO + tokens] = (rows * norm_scale(rows) * gain).astype(jnp.bfloat16)
        edge = halo_all[i].astype(f32)
        edge = edge * norm_scale(edge) * gain
        act1_o[i, 0:HALO] = jnp.where(has_prev, edge[:HALO], 0.0).astype(jnp.bfloat16)
        act1_o[i, HALO + tokens :] = jnp.where(has_next, edge[HALO:], 0.0).astype(jnp.bfloat16)
        return carry

    lax.fori_loop(0, count, norm_step, 0)
    for hop in range(3, fs_count):
        in_line.step(hop)

    def project_step(i, carry):
        proj_o[i] = product(act1_o[i], in_all[...].reshape(width, 3 * feat))
        gated = proj_o[i, :, 0:feat] * proj_o[i, :, 2 * feat :]
        conv = taps_o[2:3, :] * gated[HALO : HALO + tokens]
        for k in range(1, KW):
            conv = conv + taps_o[2 + k : 3 + k, :] * gated[HALO - k : HALO - k + tokens]
        act2_o[i] = (proj_o[i, HALO : HALO + tokens, feat : 2 * feat] * conv).astype(jnp.bfloat16)
        return carry

    lax.fori_loop(0, count, project_step, 0)
    for hop in range(3, fs_count):
        out_line.step(hop)

    def out_partial(dest):
        return product(act2_o[dest], out_all[...].reshape(feat, width))

    order = [lax.rem(pair + o, pairs) for o in range(1, pairs)] + [pair]
    share_tw = []
    for o, j in enumerate(order):
        tw_out[o] = out_partial(j * CORES + other).astype(jnp.bfloat16)
        share_tw.append(move.push(tw_out.at[o], tw_in.at[o], partner))
    share_pr = []
    for o, j in enumerate(order):
        value = out_partial(j * CORES + core)
        share_tw[o].wait_recv()
        value = value + tw_in[o].astype(f32)
        if o < pairs - 1:
            pr_out[o] = value.astype(jnp.bfloat16)
            share_pr.append(move.push(pr_out.at[o], pr_in.at[o], p_peers[o]))
        else:
            resid_o[...] = value + x_all[dp].astype(f32)
    cot_local.wait()
    cot_line.start()
    for copy in gu_z:
        copy.wait_recv()
    gu_local.wait()
    gu_out = [move.push(gu_all.at[dp], gu_all.at[dp], peer) for peer in p_peers]
    gu_twin = [move.push(gu_all.at[dp], gu_all.at[dp], partner)]
    for copy in share_pr:
        copy.wait_recv()
    resid = resid_o[...]
    for o in range(pairs - 1):
        resid = resid + pr_in[o].astype(f32)
    resid_o[...] = resid
    act3_all[fs] = (resid * norm_scale(resid) * gains_o[1:2, :]).astype(jnp.bfloat16)
    act3_line.start()
    cot_line.step(1)
    for o, source in enumerate(p_from):
        src = source * CORES + core
        down_out[o].wait_recv()
        down_twin.append(move.push(down_all.at[src], down_all.at[src], partner))
    for hop in range(1, fs_count):
        act3_line.step(hop)
        if hop + 1 < fs_count:
            cot_line.step(hop + 1)
    for o, source in enumerate(p_from):
        src = source * CORES + core
        gu_out[o].wait_recv()
        gu_twin.append(move.push(gu_all.at[src], gu_all.at[src], partner))
    for copy in down_twin + gu_twin:
        copy.wait_recv()
    down_local.wait()
    move.finish()
    for line in (in_line, out_line, cot_line, act3_line):
        line.finish()


def mixer_forward(x, cot, small, w_in, w_gate, w_up, w_out, w_down):
    dp_count, fs_count = lax.axis_size("dp"), lax.axis_size("fsdp")
    pairs = dp_count // CORES
    tokens, width = x.shape
    part = w_in.shape[0]
    feat = width // dp_count
    hid = w_gate.shape[1] // fs_count
    bf, f32 = jnp.bfloat16, jnp.float32
    shape = jax.ShapeDtypeStruct
    long = tokens + 2 * HALO
    in_vmem = [
        shape((dp_count, long, width), bf),
        shape((dp_count, long, 3 * feat), f32),
        shape((dp_count, tokens, feat), bf),
        shape((dp_count, fs_count, part, 3 * feat), bf),
        shape((fs_count, part, width), bf),
        shape((small.shape[0], width), f32),
        shape((small.shape[0], feat), f32),
        shape((tokens, width), f32),
    ]
    in_vmem += [shape((fs_count, tokens, width), bf)] * 2
    anywhere = [
        shape((dp_count, fs_count, part, 2 * hid), bf),
        shape((dp_count,) + w_down.shape, bf),
    ]
    slots = 20 * fs_count + 20 * pairs + 40
    return pl.pallas_call(
        functools.partial(mixer_forward_kernel, pairs, fs_count),
        out_shape=in_vmem + anywhere,
        in_specs=[
            pl.BlockSpec(memory_space=pltpu.VMEM if index == 2 else pltpu.HBM) for index in range(8)
        ],
        out_specs=[pl.BlockSpec(memory_space=pltpu.VMEM)] * len(in_vmem)
        + [pl.BlockSpec(memory_space=pl.ANY)] * len(anywhere),
        scratch_shapes=[
            pltpu.VMEM((dp_count, tokens, width), bf),
            pltpu.VMEM((dp_count, 2 * HALO, width), bf),
            pltpu.VMEM((dp_count, fs_count) + small.shape, bf),
            pltpu.VMEM(w_in.shape, bf),
            pltpu.VMEM(w_gate.shape, bf),
            pltpu.VMEM(w_up.shape, bf),
            pltpu.VMEM((CORES, pairs, part, 3 * feat), bf),
            pltpu.VMEM((pairs, part, 3 * feat), bf),
            pltpu.VMEM((fs_count, part, 2 * hid), bf),
            pltpu.VMEM((pairs, tokens, width), bf),
            pltpu.VMEM((pairs, tokens, width), bf),
            pltpu.VMEM((pairs - 1, tokens, width), bf),
            pltpu.VMEM((pairs - 1, tokens, width), bf),
            pltpu.SemaphoreType.DMA((8,)),
            pltpu.SemaphoreType.DMA((slots,)),
            pltpu.SemaphoreType.DMA((slots,)),
        ],
        compiler_params=pltpu.CompilerParams(
            collective_id=8, has_side_effects=True, vmem_limit_bytes=40 * 1024 * 1024
        ),
        name="mixer_forward",
    )(x, cot, small, w_in, w_gate, w_up, w_out, w_down)


def mixer_backward_kernel(
    pairs, fs_count,
    x_ref, gains_ref, taps_ref, resid_ref, act1_ref, proj_ref, act2_ref, in_w, out_w,
    d3_ref, act3_ref, dgu_ref, act4_ref, cot_ref, down_ref,
    out_o, gx_o, gin_fin, gout_o, gu_zi, gdown_o, small_o,
    d3_rx, dn_ref, dn_rx, ggu_two, gd_all, gu_tw, down_tw, gu_chip, down_chip, gu_rx, down_rx, gu_zo,
    dres_all, dproj, taps_acc, gin_p, gin_rx, gout_p, gout_rx, gin_own, gin_stage,
    tw_out, tw_in, pr_out, pr_in, sm_own, sm_rx, tp_rx, sm_p, sm_tw, sm_pr,
    sends, recvs,
):
    dp, fs, pair, core, partner, z_peers, p_peers, p_from = seats(pairs, fs_count)
    count = pairs * CORES
    tokens, width = x_ref.shape
    feat = width // count
    part = feat // fs_count
    hid = act4_ref.shape[1]
    inner = hid // count
    other = 1 - core
    twin_dp = pair * CORES + other
    move = Mover(sends, recvs, None)
    f32, bf = jnp.float32, jnp.bfloat16
    order = [lax.rem(pair + o, pairs) for o in range(1, pairs)] + [pair]

    greet(z_peers + p_peers + [partner])
    d3_z = [move.push(d3_ref.at[peer[1]], d3_rx.at[o], peer) for o, peer in enumerate(z_peers)]

    def gu_partial(dest):
        left = act3_ref[:, :, pl.ds(pl.multiple_of(dest * feat, feat), feat)]
        return product_tn(left.reshape(fs_count * tokens, feat), dgu_ref[...])

    def down_slot(dest):
        return pl.ds(pl.multiple_of(dest * inner, inner), inner)

    gu_t, gu_p = [], []
    for o, j in enumerate(order):
        ggu_two[o] = gu_partial(j * CORES + other).astype(bf)
        gu_t.append(move.push(ggu_two.at[o], gu_tw.at[o], partner))
    for o, j in enumerate(order):
        value = gu_partial(j * CORES + core)
        gu_t[o].wait_recv()
        gu_chip[o] = (value + gu_tw[o].astype(f32)).astype(bf)
        if o < pairs - 1:
            gu_p.append(move.push(gu_chip.at[o], gu_rx.at[o], p_peers[o]))
    chunk = 3 * 128 if hid % (3 * 128) == 0 else 128

    def down_step(c, carry):
        at = pl.ds(pl.multiple_of(c * chunk, chunk), chunk)
        gd_all[at, :] = product_tn(
            act4_ref[:, at], cot_ref[...].reshape(fs_count * tokens, width)
        ).astype(bf)
        return carry

    lax.fori_loop(0, hid // chunk, down_step, 0)
    down_t = [
        move.push(gd_all.at[down_slot(j * CORES + other)], down_tw.at[o], partner)
        for o, j in enumerate(order)
    ]

    def dn_step(f, carry):
        at = pl.ds(pl.multiple_of(f * tokens, tokens), tokens)
        dn_ref[f] = product(act4_ref[at, :], down_ref[...].reshape(hid, width)).astype(bf)
        return carry

    lax.fori_loop(0, fs_count, dn_step, 0)

    for copy in d3_z:
        copy.wait_recv()
    dact3 = d3_ref[fs].astype(f32)
    for o in range(fs_count - 1):
        dact3 = dact3 + d3_rx[o].astype(f32)
    resid = resid_ref[...]
    scale2 = norm_scale(resid)
    normed2 = resid * scale2
    sm_own[1:2, :] = jnp.sum(dact3 * normed2, axis=0, keepdims=True)
    dnormed = dact3 * gains_ref[1:2, :]
    dresid = cot_ref[fs].astype(f32) + scale2 * (
        dnormed - normed2 * jnp.mean(dnormed * normed2, axis=-1, keepdims=True)
    )
    gx_o[...] = dresid
    dres_all[dp, 0:tokens] = dresid.astype(bf)
    mine = dres_all.at[dp, pl.ds(0, tokens)]
    edge = dres_all.at[dp, pl.ds(tokens, HALO)]
    halo_z = move.push(dres_all.at[dp, pl.ds(0, HALO)], edge, z_peers[-1])
    dres_out = [move.push(mine, mine, peer) for peer in p_peers]
    dres_twin = [move.push(mine, mine, partner)]
    dn_z = [move.push(dn_ref.at[peer[1]], dn_rx.at[o], peer) for o, peer in enumerate(z_peers)]
    down_p = []
    for o, j in enumerate(order):
        down_t[o].wait_recv()
        down_chip[o] = (
            gd_all[down_slot(j * CORES + core), :].astype(f32) + down_tw[o].astype(f32)
        ).astype(bf)
    halo_z.wait_recv()
    edge_out = [move.push(edge, edge, peer) for peer in p_peers]
    dres_twin.append(move.push(edge, edge, partner))
    for o, source in enumerate(p_from):
        src = source * CORES + core
        dres_out[o].wait_recv()
        edge_out[o].wait_recv()
        dres_twin.append(move.push(dres_all.at[src], dres_all.at[src], partner))
    for o, peer in enumerate(p_peers):
        down_p.append(move.push(down_chip.at[o], down_rx.at[o], peer))
    for copy in dres_twin:
        copy.wait_recv()

    taps_acc[...] = jnp.zeros(taps_acc.shape, f32)

    def mixer_step(i, carry):
        dact2 = product_nt(dres_all[i], out_w[...].reshape(feat, width))
        bpart = proj_ref[i, :, 0:feat]
        cpart = proj_ref[i, :, feat : 2 * feat]
        xpart = proj_ref[i, :, 2 * feat :]
        gated = bpart * xpart
        conv = taps_ref[2:3, :] * gated[HALO : HALO + tokens]
        for k in range(1, KW):
            conv = conv + taps_ref[2 + k : 3 + k, :] * gated[HALO - k : HALO - k + tokens]
        dconv = dact2 * cpart[HALO:]
        dcpart = dact2[:tokens] * conv
        dgated = taps_ref[2:3, :] * dconv[:tokens]
        for k in range(1, KW):
            dgated = dgated + taps_ref[2 + k : 3 + k, :] * dconv[k : k + tokens]
        for k in range(KW):
            taps_acc[k : k + 1, :] += jnp.sum(
                dconv[:tokens] * gated[HALO - k : HALO - k + tokens], axis=0, keepdims=True
            )
        dproj[i, :, 0:feat] = (dgated * xpart[HALO : HALO + tokens]).astype(bf)
        dproj[i, :, feat : 2 * feat] = dcpart.astype(bf)
        dproj[i, :, 2 * feat :] = (dgated * bpart[HALO : HALO + tokens]).astype(bf)
        return carry

    lax.fori_loop(0, count, mixer_step, 0)

    def in_partial(dest):
        return product_nt(dproj[dest], in_w[...].reshape(width, 3 * feat))

    share_tw = []
    for o, j in enumerate(order):
        tw_out[o] = in_partial(j * CORES + other).astype(bf)
        share_tw.append(move.push(tw_out.at[o], tw_in.at[o], partner))

    def gin_step(c, carry):
        left = act1_ref[:, pl.ds(HALO, tokens), pl.ds(pl.multiple_of(c * feat, feat), feat)]
        grad = product_tn(
            left.reshape(count * tokens, feat), dproj[...].reshape(count * tokens, 3 * feat)
        )
        gin_p[c] = grad.astype(bf).reshape(fs_count, part, 3 * feat)
        return carry

    lax.fori_loop(0, count, gin_step, 0)
    gin_z = [move.push(gin_p.at[:, peer[1]], gin_rx.at[o], peer) for o, peer in enumerate(z_peers)]

    share_pr = []
    dact1 = None
    for o, j in enumerate(order):
        value = in_partial(j * CORES + core)
        share_tw[o].wait_recv()
        value = value + tw_in[o].astype(f32)
        if o < pairs - 1:
            pr_out[o] = value.astype(bf)
            share_pr.append(move.push(pr_out.at[o], pr_in.at[o], p_peers[o]))
        else:
            dact1 = value
    grad = product_tn(
        act2_ref[...].reshape(count * tokens, feat),
        dres_all[:, 0:tokens].reshape(count * tokens, width),
    )
    gout_p[...] = grad.astype(bf).reshape(fs_count, part, width)
    gout_z = [move.push(gout_p.at[peer[1]], gout_rx.at[o], peer) for o, peer in enumerate(z_peers)]
    taps_z = [move.push(taps_acc, tp_rx.at[o], peer) for o, peer in enumerate(z_peers)]

    for copy in gu_p:
        copy.wait_recv()
    total = gu_chip[pairs - 1].astype(f32)
    for o in range(pairs - 1):
        total = total + gu_rx[o].astype(f32)
    gu_zo[...] = total.astype(bf).reshape(fs_count, part, 2 * hid)
    gu_z = [move.push(gu_zo.at[peer[1]], gu_zi.at[fs], peer) for peer in z_peers]
    gu_zi[fs] = gu_zo[fs]

    for copy in share_pr:
        copy.wait_recv()
    for o in range(pairs - 1):
        dact1 = dact1 + pr_in[o].astype(f32)
    hidden = x_ref[...].astype(f32)
    scale1 = norm_scale(hidden)
    normed1 = hidden * scale1
    sm_own[0:1, :] = jnp.sum(dact1 * normed1, axis=0, keepdims=True)
    sm_own[2:, :] = jnp.zeros((sm_own.shape[0] - 2, width), f32)
    sm_z = [move.push(sm_own, sm_rx.at[o], peer) for o, peer in enumerate(z_peers)]
    dnormed = dact1 * gains_ref[0:1, :]
    gx_o[...] += scale1 * (dnormed - normed1 * jnp.mean(dnormed * normed1, axis=-1, keepdims=True))

    for copy in gin_z:
        copy.wait_recv()
    for d in range(count):
        total = gin_p[d, fs].astype(f32)
        for o in range(fs_count - 1):
            total = total + gin_rx[o, d].astype(f32)
        gin_own[d % CORES, d // CORES] = total.astype(bf)
    gin_t = move.push(gin_own.at[other], gin_stage, partner)
    gin_out = [
        move.push(gin_own.at[core, peer[0] // CORES], gin_fin.at[dp], peer) for peer in p_peers
    ]
    gin_fin[dp] = gin_own[core, pair]
    gin_t.wait_recv()
    gin_via = [
        move.push(gin_stage.at[peer[0] // CORES], gin_fin.at[twin_dp], peer) for peer in p_peers
    ]
    gin_fin[twin_dp] = gin_stage[pair]

    for copy in sm_z:
        copy.wait_recv()
    total = sm_own[...]
    for o in range(fs_count - 1):
        total = total + sm_rx[o]
    for d in range(count):
        sm_p[d % CORES, d // CORES] = total[:, d * feat : (d + 1) * feat]
    sm_t = move.push(sm_p.at[other], sm_tw, partner)

    for copy in down_p:
        copy.wait_recv()
    total = down_chip[pairs - 1].astype(f32)
    for o in range(pairs - 1):
        total = total + down_rx[o].astype(f32)
    gdown_o[...] = total
    for copy in dn_z:
        copy.wait_recv()
    total = resid_ref[...] + dn_ref[fs].astype(f32)
    for o in range(fs_count - 1):
        total = total + dn_rx[o].astype(f32)
    out_o[...] = total.astype(bf)
    sm_t.wait_recv()
    for j in range(pairs):
        sm_tw[j] = sm_tw[j] + sm_p[core, j]
    sm_pair = [
        move.push(sm_tw.at[peer[0] // CORES], sm_pr.at[o], peer) for o, peer in enumerate(p_peers)
    ]
    for copy in gout_z + taps_z:
        copy.wait_recv()
    total = gout_p[fs].astype(f32)
    for o in range(fs_count - 1):
        total = total + gout_rx[o].astype(f32)
    gout_o[...] = total
    for copy in gu_z:
        copy.wait_recv()
    for copy in gin_out + gin_via:
        copy.wait_recv()
    for copy in sm_pair:
        copy.wait_recv()
    total = sm_tw[pair]
    for o in range(pairs - 1):
        total = total + sm_pr[o]
    taps = taps_acc[...]
    for o in range(fs_count - 1):
        taps = taps + tp_rx[o]
    small_o[0] = total
    small_o[1] = taps
    move.finish()


def mixer_backward(x, gains, taps, resid, act1, proj, act2, in_w, out_w, d3, act3, dgu, act4, cot, down):
    dp_count, fs_count = lax.axis_size("dp"), lax.axis_size("fsdp")
    pairs = dp_count // CORES
    tokens, width = x.shape
    feat = width // dp_count
    part = feat // fs_count
    hid2 = dgu.shape[1]
    rows_down = down.shape[1]
    bf, f32 = jnp.bfloat16, jnp.float32
    shape = jax.ShapeDtypeStruct
    outs = [
        shape((tokens, width), bf),
        shape((tokens, width), f32),
        shape((dp_count, part, 3 * feat), bf),
        shape((part, width), f32),
        shape((fs_count, part, hid2), bf),
        shape((rows_down, width), f32),
        shape((2, 8, feat), f32),
    ]
    slots = 12 * fs_count + 20 * pairs + 40
    scratch = [
        ((fs_count - 1, tokens, width), bf),
        ((fs_count, tokens, width), bf),
        ((fs_count - 1, tokens, width), bf),
        ((pairs, feat, hid2), bf),
        ((hid2 // 2, width), bf),
        ((pairs, feat, hid2), bf),
        ((pairs, rows_down, width), bf),
        ((pairs, feat, hid2), bf),
        ((pairs, rows_down, width), bf),
        ((pairs - 1, feat, hid2), bf),
        ((pairs - 1, rows_down, width), bf),
        ((fs_count, part, hid2), bf),
        ((dp_count, tokens + HALO, width), bf),
        ((dp_count, tokens, 3 * feat), bf),
        ((8, feat), f32),
        ((dp_count, fs_count, part, 3 * feat), bf),
        ((fs_count - 1, dp_count, part, 3 * feat), bf),
        ((fs_count, part, width), bf),
        ((fs_count - 1, part, width), bf),
        ((CORES, pairs, part, 3 * feat), bf),
        ((pairs, part, 3 * feat), bf),
        ((pairs, tokens, width), bf),
        ((pairs, tokens, width), bf),
        ((pairs - 1, tokens, width), bf),
        ((pairs - 1, tokens, width), bf),
        ((8, width), f32),
        ((fs_count - 1, 8, width), f32),
        ((fs_count - 1, 8, feat), f32),
        ((CORES, pairs, 8, feat), f32),
        ((pairs, 8, feat), f32),
        ((pairs - 1, 8, feat), f32),
    ]
    return pl.pallas_call(
        functools.partial(mixer_backward_kernel, pairs, fs_count),
        out_shape=outs,
        in_specs=[pl.BlockSpec(memory_space=pltpu.VMEM)] * 15,
        out_specs=[pl.BlockSpec(memory_space=pltpu.VMEM)] * len(outs),
        scratch_shapes=[pltpu.VMEM(s, d) for s, d in scratch]
        + [pltpu.SemaphoreType.DMA((slots,)), pltpu.SemaphoreType.DMA((slots,))],
        compiler_params=pltpu.CompilerParams(
            collective_id=9, has_side_effects=True, vmem_limit_bytes=58 * 1024 * 1024
        ),
        name="mixer_backward",
    )(x, gains, taps, resid, act1, proj, act2, in_w, out_w, d3, act3, dgu, act4, cot, down)


def finish_kernel(
    fs_count, count,
    out_i, gx_i, gin_fin, gout_i, gu_zi, gdown_i, small_i,
    out_o, gx_o, gin_o, gout_o, ggate_o, gup_o, gdown_o, gain1_o, gain2_o, taps_o,
    gin_v, gate_v, up_v, sems,
):
    part, feat = gout_i.shape[0], gin_fin.shape[2] // 3
    width, hid = gout_i.shape[1], gu_zi.shape[2] // 2
    inner = hid // count
    f32 = jnp.float32
    copies = []

    def send(src, dst):
        copy = pltpu.make_async_copy(src, dst, sems.at[len(copies)])
        copy.start()
        copies.append(copy)

    send(gx_i, gx_o)
    send(gdown_i, gdown_o)
    send(out_i, out_o)
    send(gout_i, gout_o)
    for d in range(count):
        for k in range(3):
            gin_v[:, k * width + d * feat : k * width + (d + 1) * feat] = gin_fin[
                d, :, k * feat : (k + 1) * feat
            ].astype(f32)
    send(gin_v, gin_o)
    for which, (ref, dst) in enumerate(((gate_v, ggate_o), (up_v, gup_o))):
        wide = [gu_zi[f, :, which * hid : (which + 1) * hid].astype(f32) for f in range(fs_count)]
        pieces = [
            wide[f][:, d * inner : (d + 1) * inner] for d in range(count) for f in range(fs_count)
        ]
        ref[...] = jnp.concatenate(pieces, axis=1)
        send(ref, dst)
    fs = lax.axis_index("fsdp")
    small = small_i[...]
    mine = small[:, :, 0:part]
    for f in range(1, fs_count):
        mine = jnp.where(fs == f, small[:, :, f * part : (f + 1) * part], mine)
    gain1_o[...] = mine[0, 0:1]
    gain2_o[...] = mine[0, 1:2]
    taps_o[...] = mine[1, 0:KW]
    for copy in copies:
        copy.wait()


def finish(out, gx, gin, gout, gu, gdown, small, wide_in, wide_ff):
    dp_count, fs_count = lax.axis_size("dp"), lax.axis_size("fsdp")
    part = gout.shape[0]
    f32 = jnp.float32
    shape = jax.ShapeDtypeStruct
    outs = [
        shape(out.shape, out.dtype),
        shape(gx.shape, f32),
        shape((part, wide_in), f32),
        shape(gout.shape, f32),
        shape((part, wide_ff), f32),
        shape((part, wide_ff), f32),
        shape(gdown.shape, f32),
        shape((1, part), f32),
        shape((1, part), f32),
        shape((KW, part), f32),
    ]
    return pl.pallas_call(
        functools.partial(finish_kernel, fs_count, dp_count),
        out_shape=outs,
        in_specs=[pl.BlockSpec(memory_space=pltpu.VMEM)] * 7,
        out_specs=[pl.BlockSpec(memory_space=pltpu.HBM)] * 7
        + [pl.BlockSpec(memory_space=pltpu.VMEM)] * 3,
        scratch_shapes=[
            pltpu.VMEM((part, wide_in), f32),
            pltpu.VMEM((part, wide_ff), f32),
            pltpu.VMEM((part, wide_ff), f32),
            pltpu.SemaphoreType.DMA((7,)),
        ],
        compiler_params=pltpu.CompilerParams(vmem_limit_bytes=16 * 1024 * 1024),
        name="finish",
    )(out, gx, gin, gout, gu, gdown, small)


def split_tokens(
    inputs,
    gain_mixer,
    weight_in,
    conv_taps,
    weight_out,
    gain_ffn,
    weight_gate,
    weight_up,
    weight_down,
    cotangent,
):
    dp_count, fs_count = lax.axis_size("dp"), lax.axis_size("fsdp")
    fs = lax.axis_index("fsdp")
    tokens, width = inputs.shape[1:]
    part = weight_out.shape[0]
    hid = weight_gate.shape[1] // fs_count
    bf = jnp.bfloat16
    x, cot = inputs[0], cotangent[0]
    small = jnp.concatenate([gain_mixer[None], gain_ffn[None], conv_taps], axis=0)
    small = jnp.tile(jnp.pad(small, ((0, 16 - small.shape[0]), (0, 0))), (1, fs_count))
    lanes = lax.broadcasted_iota(jnp.int32, small.shape, 1)
    mine = (lanes >= fs * part) & (lanes < (fs + 1) * part)
    small = jnp.where(mine, small, jnp.zeros_like(small))
    (act1, proj, act2, in_w, out_w, gains, taps, resid, act3_all, cot_all, gu_cols, down_rows) = mixer_forward(
        x, cot, small, weight_in, weight_gate, weight_up, weight_out, weight_down
    )
    gu_cols = gu_cols.reshape(width, 2 * hid)
    gate_up = product(act3_all.reshape(-1, width), gu_cols)
    gate, upval = gate_up[:, :hid], gate_up[:, hid:]
    sig = jax.nn.sigmoid(gate)
    act4 = (gate * sig * upval).astype(bf)
    dact4 = product_nt(cot_all.reshape(-1, width), down_rows.reshape(hid, width))
    dgate = (dact4 * upval * sig * (1.0 + gate * (1.0 - sig))).astype(bf)
    dupval = (dact4 * gate * sig).astype(bf)
    dgu = jnp.concatenate([dgate, dupval], axis=1)
    d3 = token_pieces(product_nt(dgu, gu_cols))
    parts = mixer_backward(
        x, gains, taps, resid, act1, proj, act2, in_w, out_w, d3, act3_all, dgu, act4, cot_all, down_rows
    )
    outputs, gx, gin, gout, ggate, gup, gdown, gain1, gain2, g_taps = finish(
        *parts, weight_in.shape[1], weight_gate.shape[1]
    )
    return (
        outputs[None], gx[None], gain1[0], gin, g_taps, gout, gain2[0], ggate, gup, gdown,
    )


def fits_tokens(inputs, weight_out, weight_gate):
    dp_count, fs_count = lax.axis_size("dp"), lax.axis_size("fsdp")
    tokens, width = inputs.shape[1:]
    return (
        dp_count % CORES == 0
        and dp_count > CORES
        and fs_count > 1
        and (width // dp_count) % 128 == 0
        and (weight_gate.shape[1] // fs_count) % 128 == 0
        and weight_out.shape[0] % 16 == 0
        and tokens % 16 == 0
        and inputs.shape[0] == 1
    )


def on_device(
    inputs,
    gain_mixer,
    weight_in,
    conv_taps,
    weight_out,
    gain_ffn,
    weight_gate,
    weight_up,
    weight_down,
    cotangent,
):
    form = split_tokens if fits_tokens(inputs, weight_out, weight_gate) else split_features
    return form(
        inputs,
        gain_mixer,
        weight_in,
        conv_taps,
        weight_out,
        gain_ffn,
        weight_gate,
        weight_up,
        weight_down,
        cotangent,
    )


def solution(mesh):
    in_specs = (
        P("dp", "fsdp", None),
        P(("dp", "fsdp")),
        P(("dp", "fsdp"), None),
        P(None, ("dp", "fsdp")),
        P(("dp", "fsdp"), None),
        P(("dp", "fsdp")),
        P(("dp", "fsdp"), None),
        P(("dp", "fsdp"), None),
        P(("dp", "fsdp"), None),
        P("dp", "fsdp", None),
    )
    out_specs = (
        P("dp", "fsdp", None),
        P("dp", "fsdp", None),
        P(("dp", "fsdp")),
        P(("dp", "fsdp"), None),
        P(None, ("dp", "fsdp")),
        P(("dp", "fsdp"), None),
        P(("dp", "fsdp")),
        P(("dp", "fsdp"), None),
        P(("dp", "fsdp"), None),
        P(("dp", "fsdp"), None),
    )
    return jax.shard_map(
        on_device, mesh=mesh, in_specs=in_specs, out_specs=out_specs, check_vma=False
    )
```

```python
import functools

import jax
import jax.numpy as jnp
from jax import lax
from jax.experimental import pallas as pl
from jax.experimental.pallas import tpu as pltpu
from jax.sharding import PartitionSpec as P

KW = 3


EPS = 1e-05

CORES = 2
MESH = pl.DeviceIdType.MESH


def product(left, right):
    return jnp.dot(left, right, preferred_element_type=jnp.float32)


def product_tn(left, right):
    return lax.dot_general(
        left, right, (((0,), (0,)), ((), ())), preferred_element_type=jnp.float32
    )


def product_nt(left, right):
    return lax.dot_general(
        left, right, (((1,), (1,)), ((), ())), preferred_element_type=jnp.float32
    )


def norm_forward(hidden, gain):
    scale = lax.rsqrt(jnp.mean(hidden * hidden, axis=-1, keepdims=True) + EPS)
    normed = hidden * scale
    return (normed, scale, normed * gain.astype(jnp.float32))


def norm_backward(dact, normed, scale, gain):
    dnormed = dact * gain.astype(jnp.float32)
    dhidden = scale * (dnormed - normed * jnp.mean(dnormed * normed, axis=-1, keepdims=True))
    return (dhidden, jnp.sum(dact * normed, axis=0))


def lagged(values, offset):
    zeros = jnp.zeros((offset, values.shape[1]), values.dtype)
    return jnp.concatenate([zeros, values[: values.shape[0] - offset]], axis=0)


def leading(values, offset):
    zeros = jnp.zeros((offset, values.shape[1]), values.dtype)
    return jnp.concatenate([values[offset:], zeros], axis=0)


def column_blocks(shard, lead, dp_count, fs_count):
    rows, columns = shard.shape
    inner = columns // (lead * dp_count * fs_count)
    pieces = shard.reshape(rows, lead, dp_count, fs_count, inner).transpose(3, 0, 1, 2, 4)
    return pieces.reshape(fs_count, rows, lead * dp_count * inner)


def column_join(blocks, lead, dp_count, fs_count):
    _, rows, columns = blocks.shape
    inner = columns // (lead * dp_count)
    pieces = blocks.reshape(fs_count, rows, lead, dp_count, inner).transpose(1, 2, 3, 0, 4)
    return pieces.reshape(rows, lead * dp_count * fs_count * inner)


def greet(peers):
    barrier = pltpu.get_barrier_semaphore()
    for peer in peers:
        pl.semaphore_signal(barrier, inc=1, device_id=peer, device_id_type=MESH)
    pl.semaphore_wait(barrier, len(peers))


def push(src, dst, sends, recvs, index, peer):
    copy = pltpu.make_async_remote_copy(
        src_ref=src,
        dst_ref=dst,
        send_sem=sends.at[index],
        recv_sem=recvs.at[index],
        device_id=peer,
        device_id_type=MESH,
    )
    copy.start()
    return copy


def place():
    dp, fs = lax.axis_index("dp"), lax.axis_index("fsdp")
    pair, core = dp // CORES, lax.rem(dp, CORES)
    return dp, fs, pair, core, (pair * CORES + 1 - core, fs)


def gather_kernel(
    pairs, fs_count,
    x_ref, cot_ref, small_ref, in_ref, gu_ref, out_ref, down_ref,
    x_all, cot_all, small_all, in_all, gu_all, out_all, down_all,
    local_sem, z_send, z_recv, p_send, p_recv, c_send, c_recv,
):
    dp, fs, pair, core, partner = place()
    z_peers = [(dp, lax.rem(fs + o, fs_count)) for o in range(1, fs_count)]
    p_peers = [(lax.rem(pair + o, pairs) * CORES + core, fs) for o in range(1, pairs)]
    p_from = [lax.rem(pair + pairs - o, pairs) * CORES + core for o in range(1, pairs)]
    greet(z_peers + p_peers + [partner])
    spread = [small_all, in_all, gu_all, out_all, down_all]

    across = [[None] * len(p_peers) for _ in spread]
    twins = [[None] * pairs for _ in spread]

    def spread_own(kind, src):
        dst = spread[kind].at[dp]
        for o, peer in enumerate(p_peers):
            across[kind][o] = push(src, dst, p_send, p_recv, (kind, o), peer)
        twins[kind][0] = push(src, dst, c_send, c_recv, (kind, 0), partner)

    along = [[], [], [], [], []]
    for o, peer in enumerate(z_peers):
        to = peer[1]
        along[0].append(push(small_ref, small_all.at[dp, fs], z_send, z_recv, (0, o), peer))
        along[1].append(push(in_ref.at[to], in_all.at[dp, fs], z_send, z_recv, (1, o), peer))
    for o, peer in enumerate(z_peers):
        to = peer[1]
        along[2].append(push(gu_ref.at[to], gu_all.at[dp, fs], z_send, z_recv, (2, o), peer))
    for o, peer in enumerate(z_peers):
        along[3].append(push(x_ref, x_all.at[fs], z_send, z_recv, (3, o), peer))
    for o, peer in enumerate(z_peers):
        along[4].append(push(cot_ref, cot_all.at[fs], z_send, z_recv, (4, o), peer))
    spread_own(3, out_ref)
    spread_own(4, down_ref)
    local = []
    for index, (src, dst) in enumerate(
        [
            (small_ref, small_all.at[dp, fs]),
            (in_ref.at[fs], in_all.at[dp, fs]),
            (gu_ref.at[fs], gu_all.at[dp, fs]),
            (x_ref, x_all.at[fs]),
            (cot_ref, cot_all.at[fs]),
            (out_ref, out_all.at[dp]),
            (down_ref, down_all.at[dp]),
        ]
    ):
        copy = pltpu.make_async_copy(src, dst, local_sem.at[index])
        copy.start()
        local.append(copy)
    for kind in range(3):
        local[kind].wait()
        for copy in along[kind]:
            copy.wait_recv()
        spread_own(kind, spread[kind].at[dp])
    for kind in (3, 0, 1, 4, 2):
        for o, source in enumerate(p_from):
            across[kind][o].wait_recv()
            block = spread[kind].at[source]
            twins[kind][o + 1] = push(block, block, c_send, c_recv, (kind, o + 1), partner)
    for copy in local[3:]:
        copy.wait()
    for copy in along[3] + along[4]:
        copy.wait_recv()
    for row in along + across:
        for copy in row:
            copy.wait_send()
    for row in twins:
        for copy in row:
            copy.wait()


def gather_all(x, cot, small, in_blocks, gu_blocks, out_shard, down_shard):
    dp_count, fs_count = lax.axis_size("dp"), lax.axis_size("fsdp")
    pairs = dp_count // CORES
    arrays = (x, cot, small, in_blocks, gu_blocks, out_shard, down_shard)
    shapes = (
        (fs_count,) + x.shape,
        (fs_count,) + cot.shape,
        (dp_count, fs_count) + small.shape,
        (dp_count,) + in_blocks.shape,
        (dp_count,) + gu_blocks.shape,
        (dp_count,) + out_shard.shape,
        (dp_count,) + down_shard.shape,
    )
    return pl.pallas_call(
        functools.partial(gather_kernel, pairs, fs_count),
        out_shape=[jax.ShapeDtypeStruct(shape, x.dtype) for shape in shapes],
        in_specs=[pl.BlockSpec(memory_space=pltpu.VMEM)] * len(arrays),
        out_specs=[pl.BlockSpec(memory_space=pl.ANY)] * len(shapes),
        scratch_shapes=[
            pltpu.SemaphoreType.DMA((7,)),
            pltpu.SemaphoreType.DMA((5, fs_count - 1)),
            pltpu.SemaphoreType.DMA((5, fs_count - 1)),
            pltpu.SemaphoreType.DMA((5, pairs - 1)),
            pltpu.SemaphoreType.DMA((5, pairs - 1)),
            pltpu.SemaphoreType.DMA((5, pairs)),
            pltpu.SemaphoreType.DMA((5, pairs)),
        ],
        compiler_params=pltpu.CompilerParams(collective_id=0, has_side_effects=True),
        name="gather_all",
    )(*arrays)


def line_kernel(count, fs_count, whole, *refs):
    sources, landed = refs[:count], refs[count : 2 * count]
    local_sem, sends, recvs = refs[2 * count :]
    dp, fs, _, _, _ = place()
    targets = [lax.rem(fs + o, fs_count) for o in range(1, fs_count)]
    greet([(dp, to) for to in targets])
    copies = [
        push(src if whole else src.at[to], dst.at[fs], sends, recvs, (k, o), (dp, to))
        for k, (src, dst) in enumerate(zip(sources, landed))
        for o, to in enumerate(targets)
    ]
    local = []
    for k, (src, dst) in enumerate(zip(sources, landed)):
        copy = pltpu.make_async_copy(src if whole else src.at[fs], dst.at[fs], local_sem.at[k])
        copy.start()
        local.append(copy)
    for copy in local + copies:
        copy.wait()


def along_line(arrays, whole, collective_id, name):
    fs_count = lax.axis_size("fsdp")
    count = len(arrays)
    return pl.pallas_call(
        functools.partial(line_kernel, count, fs_count, whole),
        out_shape=[
            jax.ShapeDtypeStruct(((fs_count,) + a.shape) if whole else a.shape, a.dtype)
            for a in arrays
        ],
        in_specs=[pl.BlockSpec(memory_space=pltpu.VMEM)] * count,
        out_specs=[pl.BlockSpec(memory_space=pl.ANY)] * count,
        scratch_shapes=[
            pltpu.SemaphoreType.DMA((count,)),
            pltpu.SemaphoreType.DMA((count, fs_count - 1)),
            pltpu.SemaphoreType.DMA((count, fs_count - 1)),
        ],
        compiler_params=pltpu.CompilerParams(collective_id=collective_id, has_side_effects=True),
        name=name,
    )(*arrays)


def whole_sequence(rows, collective_id, name):
    (received,) = along_line([rows], True, collective_id, name)
    return received.reshape(-1, rows.shape[1])


def token_pieces(partial_value):
    fs_count = lax.axis_size("fsdp")
    rows, columns = partial_value.shape
    return partial_value.astype(jnp.bfloat16).reshape(fs_count, rows // fs_count, columns)


def token_share(partial_value, collective_id, name):
    (received,) = along_line([token_pieces(partial_value)], False, collective_id, name)
    return jnp.sum(received.astype(jnp.float32), axis=0)


def token_share_async(partial_value):
    received = lax.all_to_all(
        token_pieces(partial_value), "fsdp", split_axis=0, concat_axis=0, tiled=True
    )
    return jnp.sum(received.astype(jnp.float32), axis=0)


def twin_kernel(count, pairs, *refs):
    partials, received = refs[:count], refs[count : 2 * count]
    sends, recvs = refs[2 * count :]
    _, _, _, core, partner = place()
    greet([partner])
    copies = [
        push(partial.at[j, 1 - core], landed.at[j], sends, recvs, (k, j), partner)
        for k, (partial, landed) in enumerate(zip(partials, received))
        for j in range(pairs)
    ]
    for copy in copies:
        copy.wait()


def pair_kernel(count, pairs, fs_count, *refs):
    partials, pieces = refs[:count], refs[count]
    received, pieces_in = refs[count + 1 : 2 * count + 1], refs[2 * count + 1]
    sends, recvs, z_sends, z_recvs = refs[2 * count + 2 :]
    dp, fs, pair, core, _ = place()
    targets = [lax.rem(pair + o, pairs) for o in range(1, pairs)]
    peers = [(to * CORES + core, fs) for to in targets]
    z_targets = [lax.rem(fs + o, fs_count) for o in range(1, fs_count)]
    greet(peers + [(dp, to) for to in z_targets])
    copies = [
        push(partial.at[to], landed.at[o], sends, recvs, (k, o), peer)
        for k, (partial, landed) in enumerate(zip(partials, received))
        for o, (to, peer) in enumerate(zip(targets, peers))
    ]
    copies += [
        push(pieces.at[to], pieces_in.at[o], z_sends, z_recvs, o, (dp, to))
        for o, to in enumerate(z_targets)
    ]
    for copy in copies:
        copy.wait()


def twin_exchange(partials):
    count = len(partials)
    pairs = lax.axis_size("dp") // CORES
    return pl.pallas_call(
        functools.partial(twin_kernel, count, pairs),
        out_shape=[jax.ShapeDtypeStruct((pairs,) + p.shape[-2:], p.dtype) for p in partials],
        in_specs=[pl.BlockSpec(memory_space=pl.ANY)] * count,
        out_specs=[pl.BlockSpec(memory_space=pl.ANY)] * count,
        scratch_shapes=[pltpu.SemaphoreType.DMA((count, pairs))] * 2,
        compiler_params=pltpu.CompilerParams(collective_id=1, has_side_effects=True),
        name="twin_exchange",
    )(*partials)


def pair_exchange(partials, pieces):
    count = len(partials)
    pairs, fs_count = lax.axis_size("dp") // CORES, lax.axis_size("fsdp")
    slots = [(pairs - 1, p) for p in partials] + [(fs_count - 1, pieces)]
    return pl.pallas_call(
        functools.partial(pair_kernel, count, pairs, fs_count),
        out_shape=[jax.ShapeDtypeStruct((n,) + p.shape[-2:], p.dtype) for n, p in slots],
        in_specs=[pl.BlockSpec(memory_space=pl.ANY)] * len(slots),
        out_specs=[pl.BlockSpec(memory_space=pl.ANY)] * len(slots),
        scratch_shapes=[
            pltpu.SemaphoreType.DMA((count, pairs - 1)),
            pltpu.SemaphoreType.DMA((count, pairs - 1)),
            pltpu.SemaphoreType.DMA((fs_count - 1,)),
            pltpu.SemaphoreType.DMA((fs_count - 1,)),
        ],
        compiler_params=pltpu.CompilerParams(collective_id=2, has_side_effects=True),
        name="pair_exchange",
    )(*partials, pieces)


def reduce_all(partials, pieces):
    dp_count = lax.axis_size("dp")
    pairs = dp_count // CORES
    dp = lax.axis_index("dp")
    core, pair = lax.rem(dp, CORES), dp // CORES
    split = [
        p.reshape(pairs, CORES, p.shape[0] // dp_count, p.shape[1])
        for p in partials
    ]
    landed = twin_exchange(split)
    chip = [
        (
            lax.dynamic_index_in_dim(p, core, axis=1, keepdims=False).astype(jnp.float32)
            + r.astype(jnp.float32)
        ).astype(p.dtype)
        for p, r in zip(split, landed)
    ]
    *others, pieces_in = pair_exchange(chip, pieces)
    own_piece = lax.dynamic_index_in_dim(pieces, lax.axis_index("fsdp"), axis=0, keepdims=False)
    tokens = own_piece.astype(jnp.float32) + jnp.sum(pieces_in.astype(jnp.float32), axis=0)
    return tokens, [
        lax.dynamic_index_in_dim(p, pair, axis=0, keepdims=False).astype(jnp.float32)
        + jnp.sum(r.astype(jnp.float32), axis=0)
        for p, r in zip(chip, others)
    ]


def split_features(
    inputs,
    gain_mixer,
    weight_in,
    conv_taps,
    weight_out,
    gain_ffn,
    weight_gate,
    weight_up,
    weight_down,
    cotangent,
):
    dp_count = lax.axis_size("dp")
    fs_count = lax.axis_size("fsdp")
    width = weight_out.shape[1]
    part = weight_out.shape[0]
    quarter = dp_count * part
    hid = dp_count * weight_down.shape[0]

    small = jnp.concatenate([gain_mixer[None], gain_ffn[None], conv_taps], axis=0)
    lanes = max(128, part)
    small = jnp.pad(small, ((0, 8 - small.shape[0]), (0, lanes - part)))
    gu_blocks = jnp.concatenate(
        [
            column_blocks(weight_gate, 1, dp_count, fs_count),
            column_blocks(weight_up, 1, dp_count, fs_count),
        ],
        axis=2,
    )
    grad_out = cotangent[0]
    x_all, grad_all, small_all, in_cols, gu_cols, out_rows, down_rows = gather_all(
        inputs[0],
        grad_out,
        small,
        column_blocks(weight_in, 3, dp_count, fs_count),
        gu_blocks,
        weight_out,
        weight_down,
    )
    x_all = x_all.reshape(-1, width)
    grad_all = grad_all.reshape(-1, width)
    in_cols = in_cols.reshape(width, 3 * quarter)
    gu_cols = gu_cols.reshape(width, 2 * hid)
    out_rows = out_rows.reshape(quarter, width)
    down_rows = down_rows.reshape(hid, width)
    small_all = small_all[:, :, : KW + 2, :part]
    gain1 = small_all[:, :, 0].reshape(width)
    gain2 = small_all[:, :, 1].reshape(width)
    taps32 = (
        lax.dynamic_index_in_dim(small_all, lax.axis_index("fsdp"), axis=1, keepdims=False)[:, 2:]
        .transpose(1, 0, 2)
        .reshape(KW, quarter)
        .astype(jnp.float32)
    )

    _, _, pre1_all = norm_forward(x_all.astype(jnp.float32), gain1)
    act1_all = pre1_all.astype(jnp.bfloat16)
    projected = product(act1_all, in_cols)
    bpart = projected[:, :quarter]
    cpart = projected[:, quarter : 2 * quarter]
    xpart = projected[:, 2 * quarter :]
    gated = bpart * xpart
    lagged_rows = [lagged(gated, offset) for offset in range(KW)]
    conv = taps32[0] * lagged_rows[0]
    for offset in range(1, KW):
        conv = conv + taps32[offset] * lagged_rows[offset]
    act2 = (cpart * conv).astype(jnp.bfloat16)
    hidden = inputs[0].astype(jnp.float32)
    normed1, scale1, _ = norm_forward(hidden, gain1)
    resid = hidden + token_share(product(act2, out_rows), 3, "share_out")
    normed2, scale2, pre2 = norm_forward(resid, gain2)
    act3_all = whole_sequence(pre2.astype(jnp.bfloat16), 4, "gather_ffn")
    gate_up = product(act3_all, gu_cols)
    gate, upval = gate_up[:, :hid], gate_up[:, hid:]
    sig = jax.nn.sigmoid(gate)
    act4 = (gate * sig * upval).astype(jnp.bfloat16)
    dact4 = product_nt(grad_all, down_rows)
    dgate = (dact4 * upval * sig * (1.0 + gate * (1.0 - sig))).astype(jnp.bfloat16)
    dupval = (dact4 * gate * sig).astype(jnp.bfloat16)
    dgu = jnp.concatenate([dgate, dupval], axis=1)
    dact3 = token_share(product_nt(dgu, gu_cols), 5, "share_ffn")
    down_pieces = token_pieces(product(act4, down_rows))
    dnorm2, g_gain2 = norm_backward(dact3, normed2, scale2, gain2)
    dresid = grad_out.astype(jnp.float32) + dnorm2
    dres_all = whole_sequence(dresid.astype(jnp.bfloat16), 6, "gather_dres")
    dact2 = product_nt(dres_all, out_rows)
    dcpart = dact2 * conv
    dconv = dact2 * cpart
    g_taps = jnp.stack(
        [jnp.sum(dconv * lagged_rows[offset], axis=0) for offset in range(KW)], axis=0
    )
    dgated = taps32[0] * dconv
    for offset in range(1, KW):
        dgated = dgated + taps32[offset] * leading(dconv, offset)
    dproj = jnp.concatenate([dgated * xpart, dcpart, dgated * bpart], axis=1).astype(jnp.bfloat16)
    dact1 = token_share_async(product_nt(dproj, in_cols))
    dnorm1, g_gain1 = norm_backward(dact1, normed1, scale1, gain1)
    grad_inputs = dresid + dnorm1

    own_column = (jnp.arange(fs_count) == lax.axis_index("fsdp"))[None, None, :, None]
    taps_spread = jnp.where(own_column, g_taps.reshape(KW, dp_count, 1, part), 0.0).reshape(KW, width)
    small_grad = jnp.concatenate([g_gain1[None], g_gain2[None], taps_spread], axis=0)
    small_grad = jnp.pad(small_grad, ((0, 8 - small_grad.shape[0]), (0, 0)))
    small_grad = small_grad.reshape(8, dp_count, fs_count, part).transpose(1, 2, 0, 3)
    small_grad = jnp.pad(small_grad, ((0, 0), (0, 0), (0, 0), (0, lanes - part)))
    down_sum, (g_small, g_gu, g_down, g_in, g_out) = reduce_all(
        [small_grad.reshape(dp_count * fs_count * 8, lanes)]
        + [
            grad.astype(jnp.bfloat16)
            for grad in (
                product_tn(act3_all, dgu),
                product_tn(act4, grad_all),
                product_tn(act1_all, dproj),
                product_tn(act2, dres_all),
            )
        ],
        down_pieces,
    )
    outputs = (resid + down_sum).astype(jnp.bfloat16)
    moved = jnp.concatenate([g_in, g_gu], axis=1).astype(jnp.bfloat16)
    moved, small_parts = along_line(
        [
            moved.reshape(fs_count, part, 3 * quarter + 2 * hid),
            g_small.reshape(fs_count, 8, lanes),
        ],
        False,
        7,
        "owner_exchange",
    )
    moved = moved.astype(jnp.float32)
    g_in_owned = moved[:, :, : 3 * quarter]
    g_gu_owned = moved[:, :, 3 * quarter :]
    small_owned = jnp.sum(small_parts, axis=0)[: KW + 2, :part]
    return (
        outputs[None],
        grad_inputs[None],
        small_owned[0],
        column_join(g_in_owned, 3, dp_count, fs_count),
        small_owned[2:],
        g_out,
        small_owned[1],
        column_join(g_gu_owned[:, :, :hid], 1, dp_count, fs_count),
        column_join(g_gu_owned[:, :, hid:], 1, dp_count, fs_count),
        g_down,
    )

HALO = 16


class Mover:
    def __init__(self, sends, recvs, locals_):
        self.sends, self.recvs, self.locals = sends, recvs, locals_
        self.count = 0
        self.local_count = 0
        self.open = []

    def push(self, src, dst, peer):
        copy = push(src, dst, self.sends, self.recvs, self.count, peer)
        self.count += 1
        self.open.append(copy)
        return copy

    def local(self, src, dst):
        copy = pltpu.make_async_copy(src, dst, self.locals.at[self.local_count])
        self.local_count += 1
        copy.start()
        return copy

    def finish(self):
        for copy in self.open:
            copy.wait_send()


class Line:
    def __init__(self, move, slot, dp, fs, fs_count):
        self.move, self.slot, self.dp, self.fs, self.size = move, slot, dp, fs, fs_count
        self.base = move.count
        move.count += CORES * fs_count

    def copy(self, source, up):
        index = self.base + CORES * source + (1 if up else 0)
        to = lax.rem(self.fs + (1 if up else self.size - 1), self.size)
        return pltpu.make_async_remote_copy(
            src_ref=self.slot(source),
            dst_ref=self.slot(source),
            send_sem=self.move.sends.at[index],
            recv_sem=self.move.recvs.at[index],
            device_id=(self.dp, to),
            device_id_type=MESH,
        )

    def start(self):
        @pl.when(self.fs < self.size - 1)
        def _():
            self.copy(self.fs, True).start()

        @pl.when(self.fs > 0)
        def _():
            self.copy(self.fs, False).start()

    def step(self, hop):
        below, above = self.fs - hop, self.fs + hop

        @pl.when(below >= 0)
        def _():
            self.copy(below, True).wait_recv()

            @pl.when(self.fs < self.size - 1)
            def _():
                self.copy(below, True).start()

        @pl.when(above < self.size)
        def _():
            self.copy(above, False).wait_recv()

            @pl.when(self.fs > 0)
            def _():
                self.copy(above, False).start()

    def finish(self):
        for hop in range(self.size):

            @pl.when((self.fs - hop >= 0) & (self.fs < self.size - 1))
            def _():
                self.copy(self.fs - hop, True).wait_send()

            @pl.when((self.fs + hop < self.size) & (self.fs > 0))
            def _():
                self.copy(self.fs + hop, False).wait_send()


class LineSum:
    def __init__(self, move, own, send, land, dp, fs, fs_count):
        self.move, self.own, self.send, self.land = move, own, send, land
        self.dp, self.fs, self.size = dp, fs, fs_count
        self.base = move.count
        move.count += CORES * fs_count

    def copy(self, dest, up, holder):
        index = self.base + CORES * dest + (1 if up else 0)
        to = lax.rem(holder + (1 if up else self.size - 1), self.size)
        slot = dest if up else jnp.where(dest == to, self.size, dest)
        return pltpu.make_async_remote_copy(
            src_ref=self.send.at[dest],
            dst_ref=self.land.at[slot],
            send_sem=self.move.sends.at[index],
            recv_sem=self.move.recvs.at[index],
            device_id=(self.dp, to),
            device_id_type=MESH,
        )

    def source(self, dest, up):
        return self.copy(dest, up, lax.rem(self.fs + (self.size - 1 if up else 1), self.size))

    def start(self):
        last = self.size - 1
        for far in range(last):

            @pl.when(self.fs == 0)
            def _():
                self.send[last - far] = self.own(last - far).astype(jnp.bfloat16)
                self.copy(last - far, True, self.fs).start()

            @pl.when(self.fs == last)
            def _():
                self.send[far] = self.own(far).astype(jnp.bfloat16)
                self.copy(far, False, self.fs).start()

    def relay(self, dest, up):
        self.source(dest, up).wait_recv()
        total = self.own(dest).astype(jnp.float32) + self.land[dest].astype(jnp.float32)
        self.send[dest] = total.astype(jnp.bfloat16)
        self.copy(dest, up, self.fs).start()

    def step(self, hop):
        last = self.size - 1
        if hop < last:

            @pl.when((self.fs >= 1) & (self.fs <= hop))
            def _():
                self.relay(self.fs + last - hop, True)

            @pl.when((self.fs < last) & (last - self.fs <= hop))
            def _():
                self.relay(self.fs + hop - last, False)

    def total(self, out):
        out[...] = self.own(self.fs).astype(jnp.float32)

        @pl.when(self.fs > 0)
        def _():
            self.source(self.fs, True).wait_recv()
            out[...] += self.land[self.fs].astype(jnp.float32)

        @pl.when(self.fs < self.size - 1)
        def _():
            self.source(self.fs, False).wait_recv()
            out[...] += self.land[self.size].astype(jnp.float32)

    def finish(self):
        for dest in range(self.size):

            @pl.when(self.fs < dest)
            def _():
                self.copy(dest, True, self.fs).wait_send()

            @pl.when(self.fs > dest)
            def _():
                self.copy(dest, False, self.fs).wait_send()


def seats(pairs, fs_count):
    dp, fs, pair, core, partner = place()
    z_peers = [(dp, lax.rem(fs + o, fs_count)) for o in range(1, fs_count)]
    p_peers = [(lax.rem(pair + o, pairs) * CORES + core, fs) for o in range(1, pairs)]
    p_from = [lax.rem(pair + pairs - o, pairs) for o in range(1, pairs)]
    return dp, fs, pair, core, partner, z_peers, p_peers, p_from


def norm_scale(hidden):
    return lax.rsqrt(jnp.mean(hidden * hidden, axis=-1, keepdims=True) + EPS)


def mixer_forward_kernel(
    pairs, fs_count,
    x_ref, cot_ref, small_ref, in_hbm, gate_hbm, up_hbm, out_ref, down_ref,
    act1_out, proj_out, act2_out, in_out_o, out_out, gains_out, taps_out, resid_out,
    act3_out, cot_out, gu_all, down_all,
    act1_o, proj_o, act2_o, in_all, out_all, gains_o, taps_o, resid_o, act3_all, cot_all,
    x_all, halo_all, small_all, in_ref, gate_ref, up_ref, in_blk, gu_blk,
    tw_out, tw_in, pr_out, pr_in, local_sem, sends, recvs,
):
    dp, fs, pair, core, partner, z_peers, p_peers, p_from = seats(pairs, fs_count)
    count = pairs * CORES
    tokens, width = x_ref.shape
    part = in_ref.shape[0]
    feat = width // count
    inner = gate_ref.shape[1] // (count * fs_count)
    hid = inner * count
    other = 1 - core
    move = Mover(sends, recvs, local_sem)
    f32 = jnp.float32

    in_local = move.local(in_hbm, in_ref)
    x_local = move.local(x_ref, x_all.at[dp])
    gate_local = move.local(gate_hbm, gate_ref)
    up_local = move.local(up_hbm, up_ref)
    out_local = move.local(out_ref, out_all.at[fs])
    cot_local = move.local(cot_ref, cot_all.at[fs])
    down_local = move.local(down_ref, down_all.at[dp])
    crossed = [(peer[0] + other - core, fs) for peer in p_peers]
    greet(z_peers + p_peers + crossed + [partner])
    small_z = [move.push(small_ref, small_all.at[dp, fs], peer) for peer in z_peers]
    halo_next = move.push(x_ref.at[pl.ds(tokens - HALO, HALO)], halo_all.at[dp, pl.ds(0, HALO)], z_peers[0])
    halo_prev = move.push(x_ref.at[pl.ds(0, HALO)], halo_all.at[dp, pl.ds(HALO, HALO)], z_peers[-1])
    in_local.wait()
    for to in range(count):
        for k in range(3):
            in_blk[to % CORES, to // CORES, :, k * feat : (k + 1) * feat] = in_ref[
                :, k * width + to * feat : k * width + (to + 1) * feat
            ]
    in_twin = move.push(in_blk.at[other, pair], in_all.at[dp, fs], partner)
    in_via = [
        move.push(in_blk.at[other, peer[0] // CORES], in_all.at[dp, fs], peer) for peer in crossed
    ]
    in_out = [move.push(in_blk.at[core, peer[0] // CORES], in_all.at[dp, fs], peer) for peer in p_peers]
    x_out = [move.push(x_ref, x_all.at[dp], peer) for peer in p_peers]
    x_twin = move.push(x_ref, x_all.at[dp], partner)
    small_all[dp, fs] = small_ref[...]
    in_all[dp, fs] = in_blk[core, pair]
    gate_local.wait()
    up_local.wait()
    for which, ref in enumerate((gate_ref, up_ref)):
        wide = ref[...].astype(f32)
        for to in range(fs_count):
            pieces = [
                wide[:, (d * fs_count + to) * inner : (d * fs_count + to + 1) * inner]
                for d in range(count)
            ]
            gu_blk[to, :, which * hid : (which + 1) * hid] = jnp.concatenate(pieces, axis=1).astype(
                jnp.bfloat16
            )
    gu_local = move.local(gu_blk.at[fs], gu_all.at[dp, fs])
    for copy in small_z:
        copy.wait_recv()
    small_out = [move.push(small_all.at[dp], small_all.at[dp], peer) for peer in p_peers]
    small_twin = [move.push(small_all.at[dp], small_all.at[dp], partner)]
    halo_next.wait_recv()
    halo_prev.wait_recv()
    halo_out = [move.push(halo_all.at[dp], halo_all.at[dp], peer) for peer in p_peers]
    halo_twin = [move.push(halo_all.at[dp], halo_all.at[dp], partner)]
    for copy in in_out + in_via + [in_twin]:
        copy.wait_recv()
    in_line = Line(move, lambda f: in_all.at[:, f], dp, fs, fs_count)
    out_line = Line(move, lambda f: out_all.at[f], dp, fs, fs_count)
    cot_line = Line(move, lambda f: cot_all.at[f], dp, fs, fs_count)
    act3_line = Line(move, lambda f: act3_all.at[f], dp, fs, fs_count)
    in_line.start()
    out_local.wait()
    out_line.start()
    down_out = [move.push(down_ref, down_all.at[dp], peer) for peer in p_peers]
    down_twin = [move.push(down_ref, down_all.at[dp], partner)]
    in_line.step(1)
    out_line.step(1)

    small_rel, x_rel = [], []
    for o, source in enumerate(p_from):
        src = source * CORES + core
        small_out[o].wait_recv()
        halo_out[o].wait_recv()
        x_out[o].wait_recv()
        small_rel.append(move.push(small_all.at[src], small_all.at[src], partner))
        x_rel.append(move.push(halo_all.at[src], halo_all.at[src], partner))
        x_rel.append(move.push(x_all.at[src], x_all.at[src], partner))
    in_line.step(2)
    out_line.step(2)
    gu_z = [move.push(gu_blk.at[peer[1]], gu_all.at[dp, fs], peer) for peer in z_peers]
    for copy in small_twin + small_rel + [x_twin] + halo_twin + x_rel:
        copy.wait_recv()
    x_local.wait()

    for d in range(count):
        total = small_all[d, 0].astype(f32)
        for f in range(1, fs_count):
            total = total + small_all[d, f].astype(f32)
        gains_o[:, d * feat : (d + 1) * feat] = total
    total = small_all[dp, 0].astype(f32)
    for f in range(1, fs_count):
        total = total + small_all[dp, f].astype(f32)
    taps_o[...] = total
    has_prev, has_next = fs > 0, fs < fs_count - 1

    def norm_step(i, carry):
        gain = gains_o[0:1, :]
        rows = x_all[i].astype(f32)
        act1_o[i, HALO : HALO + tokens] = (rows * norm_scale(rows) * gain).astype(jnp.bfloat16)
        edge = halo_all[i].astype(f32)
        edge = edge * norm_scale(edge) * gain
        act1_o[i, 0:HALO] = jnp.where(has_prev, edge[:HALO], 0.0).astype(jnp.bfloat16)
        act1_o[i, HALO + tokens :] = jnp.where(has_next, edge[HALO:], 0.0).astype(jnp.bfloat16)
        return carry

    lax.fori_loop(0, count, norm_step, 0)
    kept = [
        move.local(act1_o, act1_out), move.local(gains_o, gains_out), move.local(taps_o, taps_out)
    ]
    for hop in range(3, fs_count):
        in_line.step(hop)

    def project_step(i, carry):
        proj_o[i] = product(act1_o[i], in_all[...].reshape(width, 3 * feat))
        gated = proj_o[i, :, 0:feat] * proj_o[i, :, 2 * feat :]
        conv = taps_o[2:3, :] * gated[HALO : HALO + tokens]
        for k in range(1, KW):
            conv = conv + taps_o[2 + k : 3 + k, :] * gated[HALO - k : HALO - k + tokens]
        act2_o[i] = (proj_o[i, HALO : HALO + tokens, feat : 2 * feat] * conv).astype(jnp.bfloat16)
        return carry

    lax.fori_loop(0, count, project_step, 0)
    kept += [
        move.local(proj_o, proj_out), move.local(act2_o, act2_out), move.local(in_all, in_out_o)
    ]
    for hop in range(3, fs_count):
        out_line.step(hop)
    kept.append(move.local(out_all, out_out))

    def out_partial(dest):
        return product(act2_o[dest], out_all[...].reshape(feat, width))

    order = [lax.rem(pair + o, pairs) for o in range(1, pairs)] + [pair]
    share_tw = []
    for o, j in enumerate(order):
        tw_out[o] = out_partial(j * CORES + other).astype(jnp.bfloat16)
        share_tw.append(move.push(tw_out.at[o], tw_in.at[o], partner))
    share_pr = []
    for o, j in enumerate(order):
        value = out_partial(j * CORES + core)
        share_tw[o].wait_recv()
        value = value + tw_in[o].astype(f32)
        if o < pairs - 1:
            pr_out[o] = value.astype(jnp.bfloat16)
            share_pr.append(move.push(pr_out.at[o], pr_in.at[o], p_peers[o]))
        else:
            resid_o[...] = value + x_all[dp].astype(f32)
    cot_local.wait()
    cot_line.start()
    for copy in gu_z:
        copy.wait_recv()
    gu_local.wait()
    gu_out = [move.push(gu_all.at[dp], gu_all.at[dp], peer) for peer in p_peers]
    gu_twin = [move.push(gu_all.at[dp], gu_all.at[dp], partner)]
    for copy in share_pr:
        copy.wait_recv()
    resid = resid_o[...]
    for o in range(pairs - 1):
        resid = resid + pr_in[o].astype(f32)
    resid_o[...] = resid
    act3_all[fs] = (resid * norm_scale(resid) * gains_o[1:2, :]).astype(jnp.bfloat16)
    act3_line.start()
    kept.append(move.local(resid_o, resid_out))
    cot_line.step(1)
    for o, source in enumerate(p_from):
        src = source * CORES + core
        down_out[o].wait_recv()
        down_twin.append(move.push(down_all.at[src], down_all.at[src], partner))
    for hop in range(1, fs_count):
        act3_line.step(hop)
        if hop + 1 < fs_count:
            cot_line.step(hop + 1)
    kept += [move.local(act3_all, act3_out), move.local(cot_all, cot_out)]
    for o, source in enumerate(p_from):
        src = source * CORES + core
        gu_out[o].wait_recv()
        gu_twin.append(move.push(gu_all.at[src], gu_all.at[src], partner))
    for copy in down_twin + gu_twin:
        copy.wait_recv()
    down_local.wait()
    for copy in kept:
        copy.wait()
    move.finish()
    for line in (in_line, out_line, cot_line, act3_line):
        line.finish()


def mixer_forward(x, cot, small, w_in, w_gate, w_up, w_out, w_down):
    dp_count, fs_count = lax.axis_size("dp"), lax.axis_size("fsdp")
    pairs = dp_count // CORES
    tokens, width = x.shape
    part = w_in.shape[0]
    feat = width // dp_count
    hid = w_gate.shape[1] // fs_count
    bf, f32 = jnp.bfloat16, jnp.float32
    shape = jax.ShapeDtypeStruct
    long = tokens + 2 * HALO
    in_vmem = [
        shape((dp_count, long, width), bf),
        shape((dp_count, long, 3 * feat), f32),
        shape((dp_count, tokens, feat), bf),
        shape((dp_count, fs_count, part, 3 * feat), bf),
        shape((fs_count, part, width), bf),
        shape((small.shape[0], width), f32),
        shape((small.shape[0], feat), f32),
        shape((tokens, width), f32),
    ]
    in_vmem += [shape((fs_count, tokens, width), bf)] * 2
    anywhere = [
        shape((dp_count, fs_count, part, 2 * hid), bf),
        shape((dp_count,) + w_down.shape, bf),
    ]
    slots = 20 * fs_count + 20 * pairs + 40
    return pl.pallas_call(
        functools.partial(mixer_forward_kernel, pairs, fs_count),
        out_shape=in_vmem + anywhere,
        in_specs=[
            pl.BlockSpec(memory_space=pltpu.VMEM if index == 2 else pltpu.HBM) for index in range(8)
        ],
        out_specs=[pl.BlockSpec(memory_space=pltpu.HBM)] * (len(in_vmem) + len(anywhere)),
        scratch_shapes=[pltpu.VMEM(item.shape, item.dtype) for item in in_vmem]
        + [
            pltpu.VMEM((dp_count, tokens, width), bf),
            pltpu.VMEM((dp_count, 2 * HALO, width), bf),
            pltpu.VMEM((dp_count, fs_count) + small.shape, bf),
            pltpu.VMEM(w_in.shape, bf),
            pltpu.VMEM(w_gate.shape, bf),
            pltpu.VMEM(w_up.shape, bf),
            pltpu.VMEM((CORES, pairs, part, 3 * feat), bf),
            pltpu.VMEM((fs_count, part, 2 * hid), bf),
            pltpu.VMEM((pairs, tokens, width), bf),
            pltpu.VMEM((pairs, tokens, width), bf),
            pltpu.VMEM((pairs - 1, tokens, width), bf),
            pltpu.VMEM((pairs - 1, tokens, width), bf),
            pltpu.SemaphoreType.DMA((24,)),
            pltpu.SemaphoreType.DMA((slots,)),
            pltpu.SemaphoreType.DMA((slots,)),
        ],
        compiler_params=pltpu.CompilerParams(
            collective_id=8, has_side_effects=True, vmem_limit_bytes=60 * 1024 * 1024
        ),
        name="mixer_forward",
    )(x, cot, small, w_in, w_gate, w_up, w_out, w_down)


def mixer_backward_kernel(
    pairs, fs_count,
    x_h, gains_ref, taps_ref, resid_h, act1_h, proj_h, act2_h, in_h, out_h,
    gu_h, act3_h, dgu_h, act4_h, cot_h, down_h,
    out_o, gx_o, gin_fin, gout_o, gu_zi, gdown_o, small_o,
    x_ref, resid_ref, act1_ref, proj_ref, act2_ref, in_w, out_w,
    gu_ref, act3_ref, dgu_ref, act4_ref, cot_ref, down_ref,
    d3_own, d3_rx, dn_ref, dn_tx, dn_rx, acc, gin_acc,
    ggu_two, gd_all, gu_tw, down_tw, gu_chip, down_chip, gu_rx, down_rx, gu_zo,
    dres_all, dproj, taps_acc, gin_p, gin_tx, gin_rx, gout_p, gout_tx, gout_rx, gin_own, gin_stage,
    tw_out, tw_in, pr_out, pr_in, sm_own, sm_rx, tp_rx, sm_p, sm_tw, sm_pr,
    local_sem, sends, recvs,
):
    dp, fs, pair, core, partner, z_peers, p_peers, p_from = seats(pairs, fs_count)
    count = pairs * CORES
    tokens, width = x_ref.shape
    feat = width // count
    part = feat // fs_count
    hid = act4_ref.shape[1]
    inner = hid // count
    other = 1 - core
    twin_dp = pair * CORES + other
    move = Mover(sends, recvs, local_sem)
    f32, bf = jnp.float32, jnp.bfloat16
    order = [lax.rem(pair + o, pairs) for o in range(1, pairs)] + [pair]

    dgu_l = move.local(dgu_h, dgu_ref)
    gu_l = move.local(gu_h, gu_ref)
    act3_l = move.local(act3_h, act3_ref)
    act4_l = move.local(act4_h, act4_ref)
    cot_l = move.local(cot_h, cot_ref)
    down_l = move.local(down_h, down_ref)
    late = [
        move.local(src, dst)
        for src, dst in (
            (x_h, x_ref), (resid_h, resid_ref), (out_h, out_w), (proj_h, proj_ref),
            (in_h, in_w), (act1_h, act1_ref), (act2_h, act2_ref),
        )
    ]
    greet(z_peers + p_peers + [partner])
    dgu_l.wait()
    gu_l.wait()

    d3_z = []
    for o, peer in enumerate(z_peers + [(dp, fs)]):
        at = pl.ds(pl.multiple_of(peer[1] * tokens, tokens), tokens)
        d3_own[o] = product_nt(dgu_ref[at, :], gu_ref[...].reshape(width, 2 * hid)).astype(bf)
        if o < fs_count - 1:
            d3_z.append(move.push(d3_own.at[o], d3_rx.at[o], peer))
    dn = LineSum(move, lambda f: dn_ref[f], dn_tx, dn_rx, dp, fs, fs_count)
    gin_line = LineSum(move, lambda f: gin_p[:, f], gin_tx, gin_rx, dp, fs, fs_count)
    gout_line = LineSum(move, lambda f: gout_p[f], gout_tx, gout_rx, dp, fs, fs_count)
    act3_l.wait()

    def gu_partial(dest):
        left = act3_ref[:, :, pl.ds(pl.multiple_of(dest * feat, feat), feat)]
        return product_tn(left.reshape(fs_count * tokens, feat), dgu_ref[...])

    def down_slot(dest):
        return pl.ds(pl.multiple_of(dest * inner, inner), inner)

    gu_t, gu_p = [], []
    for o, j in enumerate(order):
        ggu_two[o] = gu_partial(j * CORES + other).astype(bf)
        gu_t.append(move.push(ggu_two.at[o], gu_tw.at[o], partner))
    for o, j in enumerate(order):
        value = gu_partial(j * CORES + core)
        gu_t[o].wait_recv()
        gu_chip[o] = (value + gu_tw[o].astype(f32)).astype(bf)
        if o < pairs - 1:
            gu_p.append(move.push(gu_chip.at[o], gu_rx.at[o], p_peers[o]))
    act4_l.wait()
    cot_l.wait()
    down_l.wait()
    chunk = 3 * 128 if hid % (3 * 128) == 0 else 128

    def down_step(c, carry):
        at = pl.ds(pl.multiple_of(c * chunk, chunk), chunk)
        gd_all[at, :] = product_tn(
            act4_ref[:, at], cot_ref[...].reshape(fs_count * tokens, width)
        ).astype(bf)
        return carry

    lax.fori_loop(0, hid // chunk, down_step, 0)
    down_t = [
        move.push(gd_all.at[down_slot(j * CORES + other)], down_tw.at[o], partner)
        for o, j in enumerate(order)
    ]

    def dn_step(f, carry):
        at = pl.ds(pl.multiple_of(f * tokens, tokens), tokens)
        dn_ref[f] = product(act4_ref[at, :], down_ref[...].reshape(hid, width)).astype(bf)
        return carry

    lax.fori_loop(0, fs_count, dn_step, 0)
    for copy in late:
        copy.wait()

    for copy in d3_z:
        copy.wait_recv()
    dact3 = d3_own[fs_count - 1].astype(f32)
    for o in range(fs_count - 1):
        dact3 = dact3 + d3_rx[o].astype(f32)
    resid = resid_ref[...]
    scale2 = norm_scale(resid)
    normed2 = resid * scale2
    sm_own[1:2, :] = jnp.sum(dact3 * normed2, axis=0, keepdims=True)
    dnormed = dact3 * gains_ref[1:2, :]
    dresid = cot_ref[fs].astype(f32) + scale2 * (
        dnormed - normed2 * jnp.mean(dnormed * normed2, axis=-1, keepdims=True)
    )
    gx_o[...] = dresid
    dres_all[dp, 0:tokens] = dresid.astype(bf)
    mine = dres_all.at[dp, pl.ds(0, tokens)]
    edge = dres_all.at[dp, pl.ds(tokens, HALO)]
    halo_z = move.push(dres_all.at[dp, pl.ds(0, HALO)], edge, z_peers[-1])
    dres_out = [move.push(mine, mine, peer) for peer in p_peers]
    dres_twin = [move.push(mine, mine, partner)]
    dn.start()
    down_p = []
    for o, j in enumerate(order):
        down_t[o].wait_recv()
        down_chip[o] = (
            gd_all[down_slot(j * CORES + core), :].astype(f32) + down_tw[o].astype(f32)
        ).astype(bf)
    halo_z.wait_recv()
    edge_out = [move.push(edge, edge, peer) for peer in p_peers]
    dres_twin.append(move.push(edge, edge, partner))
    for o, source in enumerate(p_from):
        src = source * CORES + core
        dres_out[o].wait_recv()
        edge_out[o].wait_recv()
        dres_twin.append(move.push(dres_all.at[src], dres_all.at[src], partner))
    for o, peer in enumerate(p_peers):
        down_p.append(move.push(down_chip.at[o], down_rx.at[o], peer))
    dn.step(1)
    for copy in dres_twin:
        copy.wait_recv()

    taps_acc[...] = jnp.zeros(taps_acc.shape, f32)

    def mixer_step(i, carry):
        dact2 = product_nt(dres_all[i], out_w[...].reshape(feat, width))
        bpart = proj_ref[i, :, 0:feat]
        cpart = proj_ref[i, :, feat : 2 * feat]
        xpart = proj_ref[i, :, 2 * feat :]
        gated = bpart * xpart
        conv = taps_ref[2:3, :] * gated[HALO : HALO + tokens]
        for k in range(1, KW):
            conv = conv + taps_ref[2 + k : 3 + k, :] * gated[HALO - k : HALO - k + tokens]
        dconv = dact2 * cpart[HALO:]
        dcpart = dact2[:tokens] * conv
        dgated = taps_ref[2:3, :] * dconv[:tokens]
        for k in range(1, KW):
            dgated = dgated + taps_ref[2 + k : 3 + k, :] * dconv[k : k + tokens]
        for k in range(KW):
            taps_acc[k : k + 1, :] += jnp.sum(
                dconv[:tokens] * gated[HALO - k : HALO - k + tokens], axis=0, keepdims=True
            )
        dproj[i, :, 0:feat] = (dgated * xpart[HALO : HALO + tokens]).astype(bf)
        dproj[i, :, feat : 2 * feat] = dcpart.astype(bf)
        dproj[i, :, 2 * feat :] = (dgated * bpart[HALO : HALO + tokens]).astype(bf)
        return carry

    lax.fori_loop(0, count, mixer_step, 0)

    sm_own[0:1, :] = jnp.zeros((1, width), f32)
    sm_own[2:, :] = jnp.zeros((sm_own.shape[0] - 2, width), f32)

    def in_partial(dest):
        value = product_nt(dproj[dest], in_w[...].reshape(width, 3 * feat))
        left = act1_ref[dest, pl.ds(HALO, tokens), :].astype(f32)
        sm_own[0:1, :] += jnp.sum(value * left, axis=0, keepdims=True)
        return value

    share_tw = []
    for o, j in enumerate(order):
        tw_out[o] = in_partial(j * CORES + other).astype(bf)
        share_tw.append(move.push(tw_out.at[o], tw_in.at[o], partner))

    def gin_step(c, carry):
        left = act1_ref[:, pl.ds(HALO, tokens), pl.ds(pl.multiple_of(c * feat, feat), feat)]
        grad = product_tn(
            left.reshape(count * tokens, feat), dproj[...].reshape(count * tokens, 3 * feat)
        )
        gin_p[c] = grad.astype(bf).reshape(fs_count, part, 3 * feat)
        return carry

    lax.fori_loop(0, count, gin_step, 0)
    dn.step(2)
    gin_line.start()

    share_pr = []
    dact1 = None
    for o, j in enumerate(order):
        value = in_partial(j * CORES + core)
        share_tw[o].wait_recv()
        value = value + tw_in[o].astype(f32)
        if o < pairs - 1:
            pr_out[o] = value.astype(bf)
            share_pr.append(move.push(pr_out.at[o], pr_in.at[o], p_peers[o]))
        else:
            dact1 = value
    sm_own[0:1, :] = sm_own[0:1, :] / gains_ref[0:1, :]
    sm_z = [move.push(sm_own, sm_rx.at[o], peer) for o, peer in enumerate(z_peers)]
    taps_z = [move.push(taps_acc, tp_rx.at[o], peer) for o, peer in enumerate(z_peers)]
    grad = product_tn(
        act2_ref[...].reshape(count * tokens, feat),
        dres_all[:, 0:tokens].reshape(count * tokens, width),
    )
    gout_p[...] = grad.astype(bf).reshape(fs_count, part, width)
    gout_line.start()
    gin_line.step(1)
    for hop in range(3, fs_count):
        dn.step(hop)

    for copy in gu_p:
        copy.wait_recv()
    total = gu_chip[pairs - 1].astype(f32)
    for o in range(pairs - 1):
        total = total + gu_rx[o].astype(f32)
    gu_zo[...] = total.astype(bf).reshape(fs_count, part, 2 * hid)
    gu_z = [move.push(gu_zo.at[peer[1]], gu_zi.at[fs], peer) for peer in z_peers]
    gu_zi[fs] = gu_zo[fs]
    gout_line.step(1)
    gin_line.step(2)
    gout_line.step(2)

    for copy in sm_z:
        copy.wait_recv()
    small_sum = sm_own[...]
    for o in range(fs_count - 1):
        small_sum = small_sum + sm_rx[o]
    for d in range(count):
        sm_p[d % CORES, d // CORES] = small_sum[:, d * feat : (d + 1) * feat]
    sm_t = move.push(sm_p.at[other], sm_tw, partner)

    for copy in share_pr:
        copy.wait_recv()
    for o in range(pairs - 1):
        dact1 = dact1 + pr_in[o].astype(f32)
    hidden = x_ref[...].astype(f32)
    scale1 = norm_scale(hidden)
    normed1 = hidden * scale1
    dnormed = dact1 * gains_ref[0:1, :]
    gx_o[...] += scale1 * (dnormed - normed1 * jnp.mean(dnormed * normed1, axis=-1, keepdims=True))

    sm_t.wait_recv()
    for j in range(pairs):
        sm_tw[j] = sm_tw[j] + sm_p[core, j]
    sm_pair = [
        move.push(sm_tw.at[peer[0] // CORES], sm_pr.at[o], peer) for o, peer in enumerate(p_peers)
    ]
    for hop in range(3, fs_count):
        gin_line.step(hop)
        gout_line.step(hop)
    gin_line.total(gin_acc)
    for d in range(count):
        gin_own[d % CORES, d // CORES] = gin_acc[d].astype(bf)
    gin_t = move.push(gin_own.at[other], gin_stage, partner)
    gin_out = [
        move.push(gin_own.at[core, peer[0] // CORES], gin_fin.at[dp], peer) for peer in p_peers
    ]
    gin_fin[dp] = gin_own[core, pair]
    gin_t.wait_recv()
    gin_via = [
        move.push(gin_stage.at[peer[0] // CORES], gin_fin.at[twin_dp], peer) for peer in p_peers
    ]
    gin_fin[twin_dp] = gin_stage[pair]

    for copy in down_p:
        copy.wait_recv()
    total = down_chip[pairs - 1].astype(f32)
    for o in range(pairs - 1):
        total = total + down_rx[o].astype(f32)
    gdown_o[...] = total
    dn.total(acc)
    out_o[...] = (resid_ref[...] + acc[...]).astype(bf)
    for copy in taps_z:
        copy.wait_recv()
    gout_line.total(gout_o)
    for copy in gu_z:
        copy.wait_recv()
    for copy in gin_out + gin_via:
        copy.wait_recv()
    for copy in sm_pair:
        copy.wait_recv()
    total = sm_tw[pair]
    for o in range(pairs - 1):
        total = total + sm_pr[o]
    taps = taps_acc[...]
    for o in range(fs_count - 1):
        taps = taps + tp_rx[o]
    small_o[0] = total
    small_o[1] = taps
    move.finish()
    for line in (dn, gin_line, gout_line):
        line.finish()


def mixer_backward(x, gains, taps, resid, act1, proj, act2, in_w, out_w, gu, act3, dgu, act4, cot, down):
    dp_count, fs_count = lax.axis_size("dp"), lax.axis_size("fsdp")
    pairs = dp_count // CORES
    tokens, width = x.shape
    feat = width // dp_count
    part = feat // fs_count
    hid2 = dgu.shape[1]
    rows_down = down.shape[1]
    bf, f32 = jnp.bfloat16, jnp.float32
    shape = jax.ShapeDtypeStruct
    outs = [
        shape((tokens, width), bf),
        shape((tokens, width), f32),
        shape((dp_count, part, 3 * feat), bf),
        shape((part, width), f32),
        shape((fs_count, part, hid2), bf),
        shape((rows_down, width), f32),
        shape((2, 8, feat), f32),
    ]
    slots = 24 * fs_count + 20 * pairs + 40
    loaded = (x, resid, act1, proj, act2, in_w, out_w, gu, act3, dgu, act4, cot, down)
    scratch = [(item.shape, item.dtype) for item in loaded] + [
        ((fs_count, tokens, width), bf),
        ((fs_count - 1, tokens, width), bf),
        ((fs_count, tokens, width), bf),
        ((fs_count, tokens, width), bf),
        ((fs_count + 1, tokens, width), bf),
        ((tokens, width), f32),
        ((dp_count, part, 3 * feat), f32),
        ((pairs, feat, hid2), bf),
        ((hid2 // 2, width), bf),
        ((pairs, feat, hid2), bf),
        ((pairs, rows_down, width), bf),
        ((pairs, feat, hid2), bf),
        ((pairs, rows_down, width), bf),
        ((pairs - 1, feat, hid2), bf),
        ((pairs - 1, rows_down, width), bf),
        ((fs_count, part, hid2), bf),
        ((dp_count, tokens + HALO, width), bf),
        ((dp_count, tokens, 3 * feat), bf),
        ((8, feat), f32),
        ((dp_count, fs_count, part, 3 * feat), bf),
        ((fs_count, dp_count, part, 3 * feat), bf),
        ((fs_count + 1, dp_count, part, 3 * feat), bf),
        ((fs_count, part, width), bf),
        ((fs_count, part, width), bf),
        ((fs_count + 1, part, width), bf),
        ((CORES, pairs, part, 3 * feat), bf),
        ((pairs, part, 3 * feat), bf),
        ((pairs, tokens, width), bf),
        ((pairs, tokens, width), bf),
        ((pairs - 1, tokens, width), bf),
        ((pairs - 1, tokens, width), bf),
        ((8, width), f32),
        ((fs_count - 1, 8, width), f32),
        ((fs_count - 1, 8, feat), f32),
        ((CORES, pairs, 8, feat), f32),
        ((pairs, 8, feat), f32),
        ((pairs - 1, 8, feat), f32),
    ]
    return pl.pallas_call(
        functools.partial(mixer_backward_kernel, pairs, fs_count),
        out_shape=outs,
        in_specs=[
            pl.BlockSpec(memory_space=pltpu.VMEM if index in (1, 2) else pltpu.HBM)
            for index in range(15)
        ],
        out_specs=[pl.BlockSpec(memory_space=pltpu.VMEM)] * len(outs),
        scratch_shapes=[pltpu.VMEM(s, d) for s, d in scratch]
        + [pltpu.SemaphoreType.DMA((n,)) for n in (len(loaded), slots, slots)],
        compiler_params=pltpu.CompilerParams(
            collective_id=9, has_side_effects=True, vmem_limit_bytes=60 * 1024 * 1024
        ),
        name="mixer_backward",
    )(x, gains, taps, resid, act1, proj, act2, in_w, out_w, gu, act3, dgu, act4, cot, down)


def finish_kernel(
    fs_count, count,
    out_i, gx_i, gin_h, gout_i, gu_h, gdown_i, small_i,
    out_o, gx_o, gin_o, gout_o, ggate_o, gup_o, gdown_o, gain1_o, gain2_o, taps_o,
    gin_fin, gu_zi, gin_v, gate_v, up_v, out_v, gx_v, gout_v, gdown_v, sems,
):
    part, feat = gout_i.shape[0], gin_fin.shape[2] // 3
    width, hid = gout_i.shape[1], gu_zi.shape[2] // 2
    inner = hid // count
    f32 = jnp.float32
    copies = []

    def send(src, dst):
        copy = pltpu.make_async_copy(src, dst, sems.at[len(copies)])
        copy.start()
        copies.append(copy)

    send(gin_h, gin_fin)
    send(gu_h, gu_zi)
    through = ((gx_i, gx_v, gx_o), (gdown_i, gdown_v, gdown_o), (out_i, out_v, out_o), (gout_i, gout_v, gout_o))
    for src, held, dst in through:
        send(src, held)
    gin_in, gu_in, *held_in = copies
    gin_count = len(copies)
    for copy, (src, held, dst) in zip(held_in, through):
        copy.wait()
        send(held, dst)
    gin_in.wait()
    for d in range(count):
        for k in range(3):
            gin_v[:, k * width + d * feat : k * width + (d + 1) * feat] = gin_fin[
                d, :, k * feat : (k + 1) * feat
            ].astype(f32)
    send(gin_v, gin_o)
    gu_in.wait()
    for which, (ref, dst) in enumerate(((gate_v, ggate_o), (up_v, gup_o))):
        wide = [gu_zi[f, :, which * hid : (which + 1) * hid].astype(f32) for f in range(fs_count)]
        pieces = [
            wide[f][:, d * inner : (d + 1) * inner] for d in range(count) for f in range(fs_count)
        ]
        ref[...] = jnp.concatenate(pieces, axis=1)
        send(ref, dst)
    fs = lax.axis_index("fsdp")
    small = small_i[...]
    mine = small[:, :, 0:part]
    for f in range(1, fs_count):
        mine = jnp.where(fs == f, small[:, :, f * part : (f + 1) * part], mine)
    gain1_o[...] = mine[0, 0:1]
    gain2_o[...] = mine[0, 1:2]
    taps_o[...] = mine[1, 0:KW]
    for copy in copies[gin_count:]:
        copy.wait()


def finish(out, gx, gin, gout, gu, gdown, small, wide_in, wide_ff):
    dp_count, fs_count = lax.axis_size("dp"), lax.axis_size("fsdp")
    part = gout.shape[0]
    f32 = jnp.float32
    shape = jax.ShapeDtypeStruct
    outs = [
        shape(out.shape, out.dtype),
        shape(gx.shape, f32),
        shape((part, wide_in), f32),
        shape(gout.shape, f32),
        shape((part, wide_ff), f32),
        shape((part, wide_ff), f32),
        shape(gdown.shape, f32),
        shape((1, part), f32),
        shape((1, part), f32),
        shape((KW, part), f32),
    ]
    return pl.pallas_call(
        functools.partial(finish_kernel, fs_count, dp_count),
        out_shape=outs,
        in_specs=[pl.BlockSpec(memory_space=pltpu.HBM)] * 6
        + [pl.BlockSpec(memory_space=pltpu.VMEM)],
        out_specs=[pl.BlockSpec(memory_space=pltpu.HBM)] * 7
        + [pl.BlockSpec(memory_space=pltpu.VMEM)] * 3,
        scratch_shapes=[
            pltpu.VMEM(gin.shape, gin.dtype),
            pltpu.VMEM(gu.shape, gu.dtype),
            pltpu.VMEM((part, wide_in), f32),
            pltpu.VMEM((part, wide_ff), f32),
            pltpu.VMEM((part, wide_ff), f32),
            pltpu.VMEM(out.shape, out.dtype),
            pltpu.VMEM(gx.shape, f32),
            pltpu.VMEM(gout.shape, f32),
            pltpu.VMEM(gdown.shape, f32),
            pltpu.SemaphoreType.DMA((13,)),
        ],
        compiler_params=pltpu.CompilerParams(vmem_limit_bytes=60 * 1024 * 1024),
        name="finish",
    )(out, gx, gin, gout, gu, gdown, small)


def split_tokens(
    inputs,
    gain_mixer,
    weight_in,
    conv_taps,
    weight_out,
    gain_ffn,
    weight_gate,
    weight_up,
    weight_down,
    cotangent,
):
    dp_count, fs_count = lax.axis_size("dp"), lax.axis_size("fsdp")
    fs = lax.axis_index("fsdp")
    tokens, width = inputs.shape[1:]
    part = weight_out.shape[0]
    hid = weight_gate.shape[1] // fs_count
    bf = jnp.bfloat16
    x, cot = inputs[0], cotangent[0]
    small = jnp.concatenate([gain_mixer[None], gain_ffn[None], conv_taps], axis=0)
    small = jnp.tile(jnp.pad(small, ((0, 16 - small.shape[0]), (0, 0))), (1, fs_count))
    lanes = lax.broadcasted_iota(jnp.int32, small.shape, 1)
    mine = (lanes >= fs * part) & (lanes < (fs + 1) * part)
    small = jnp.where(mine, small, jnp.zeros_like(small))
    (act1, proj, act2, in_w, out_w, gains, taps, resid, act3_all, cot_all, gu_all, down_rows) = mixer_forward(
        x, cot, small, weight_in, weight_gate, weight_up, weight_out, weight_down
    )
    gu_cols = gu_all.reshape(width, 2 * hid)
    gate_up = product(act3_all.reshape(-1, width), gu_cols)
    gate, upval = gate_up[:, :hid], gate_up[:, hid:]
    sig = jax.nn.sigmoid(gate)
    act4 = (gate * sig * upval).astype(bf)
    dact4 = product_nt(cot_all.reshape(-1, width), down_rows.reshape(hid, width))
    dgate = (dact4 * upval * sig * (1.0 + gate * (1.0 - sig))).astype(bf)
    dupval = (dact4 * gate * sig).astype(bf)
    dgu = jnp.concatenate([dgate, dupval], axis=1)
    parts = mixer_backward(
        x, gains, taps, resid, act1, proj, act2, in_w, out_w, gu_all, act3_all, dgu, act4, cot_all, down_rows
    )
    outputs, gx, gin, gout, ggate, gup, gdown, gain1, gain2, g_taps = finish(
        *parts, weight_in.shape[1], weight_gate.shape[1]
    )
    return (
        outputs[None], gx[None], gain1[0], gin, g_taps, gout, gain2[0], ggate, gup, gdown,
    )


def fits_tokens(inputs, weight_out, weight_gate):
    dp_count, fs_count = lax.axis_size("dp"), lax.axis_size("fsdp")
    tokens, width = inputs.shape[1:]
    return (
        dp_count % CORES == 0
        and dp_count > CORES
        and fs_count > 1
        and (width // dp_count) % 128 == 0
        and (weight_gate.shape[1] // fs_count) % 128 == 0
        and weight_out.shape[0] % 16 == 0
        and tokens % 16 == 0
        and inputs.shape[0] == 1
    )


def on_device(
    inputs,
    gain_mixer,
    weight_in,
    conv_taps,
    weight_out,
    gain_ffn,
    weight_gate,
    weight_up,
    weight_down,
    cotangent,
):
    form = split_tokens if fits_tokens(inputs, weight_out, weight_gate) else split_features
    return form(
        inputs,
        gain_mixer,
        weight_in,
        conv_taps,
        weight_out,
        gain_ffn,
        weight_gate,
        weight_up,
        weight_down,
        cotangent,
    )


def solution(mesh):
    in_specs = (
        P("dp", "fsdp", None),
        P(("dp", "fsdp")),
        P(("dp", "fsdp"), None),
        P(None, ("dp", "fsdp")),
        P(("dp", "fsdp"), None),
        P(("dp", "fsdp")),
        P(("dp", "fsdp"), None),
        P(("dp", "fsdp"), None),
        P(("dp", "fsdp"), None),
        P("dp", "fsdp", None),
    )
    out_specs = (
        P("dp", "fsdp", None),
        P("dp", "fsdp", None),
        P(("dp", "fsdp")),
        P(("dp", "fsdp"), None),
        P(None, ("dp", "fsdp")),
        P(("dp", "fsdp"), None),
        P(("dp", "fsdp")),
        P(("dp", "fsdp"), None),
        P(("dp", "fsdp"), None),
        P(("dp", "fsdp"), None),
    )
    return jax.shard_map(
        on_device, mesh=mesh, in_specs=in_specs, out_specs=out_specs, check_vma=False
    )
```

```python
import functools

import jax
import jax.numpy as jnp
from jax import lax
from jax.experimental import pallas as pl
from jax.experimental.pallas import tpu as pltpu
from jax.sharding import PartitionSpec as P

KW = 3


EPS = 1e-05

CORES = 2
MESH = pl.DeviceIdType.MESH


def product(left, right):
    return jnp.dot(left, right, preferred_element_type=jnp.float32)


def product_tn(left, right):
    return lax.dot_general(
        left, right, (((0,), (0,)), ((), ())), preferred_element_type=jnp.float32
    )


def product_nt(left, right):
    return lax.dot_general(
        left, right, (((1,), (1,)), ((), ())), preferred_element_type=jnp.float32
    )


def norm_forward(hidden, gain):
    scale = lax.rsqrt(jnp.mean(hidden * hidden, axis=-1, keepdims=True) + EPS)
    normed = hidden * scale
    return (normed, scale, normed * gain.astype(jnp.float32))


def norm_backward(dact, normed, scale, gain):
    dnormed = dact * gain.astype(jnp.float32)
    dhidden = scale * (dnormed - normed * jnp.mean(dnormed * normed, axis=-1, keepdims=True))
    return (dhidden, jnp.sum(dact * normed, axis=0))


def lagged(values, offset):
    zeros = jnp.zeros((offset, values.shape[1]), values.dtype)
    return jnp.concatenate([zeros, values[: values.shape[0] - offset]], axis=0)


def leading(values, offset):
    zeros = jnp.zeros((offset, values.shape[1]), values.dtype)
    return jnp.concatenate([values[offset:], zeros], axis=0)


def column_blocks(shard, lead, dp_count, fs_count):
    rows, columns = shard.shape
    inner = columns // (lead * dp_count * fs_count)
    pieces = shard.reshape(rows, lead, dp_count, fs_count, inner).transpose(3, 0, 1, 2, 4)
    return pieces.reshape(fs_count, rows, lead * dp_count * inner)


def column_join(blocks, lead, dp_count, fs_count):
    _, rows, columns = blocks.shape
    inner = columns // (lead * dp_count)
    pieces = blocks.reshape(fs_count, rows, lead, dp_count, inner).transpose(1, 2, 3, 0, 4)
    return pieces.reshape(rows, lead * dp_count * fs_count * inner)


def greet(peers):
    barrier = pltpu.get_barrier_semaphore()
    for peer in peers:
        pl.semaphore_signal(barrier, inc=1, device_id=peer, device_id_type=MESH)
    pl.semaphore_wait(barrier, len(peers))


def push(src, dst, sends, recvs, index, peer):
    copy = pltpu.make_async_remote_copy(
        src_ref=src,
        dst_ref=dst,
        send_sem=sends.at[index],
        recv_sem=recvs.at[index],
        device_id=peer,
        device_id_type=MESH,
    )
    copy.start()
    return copy


def place():
    dp, fs = lax.axis_index("dp"), lax.axis_index("fsdp")
    pair, core = dp // CORES, lax.rem(dp, CORES)
    return dp, fs, pair, core, (pair * CORES + 1 - core, fs)


def gather_kernel(
    pairs, fs_count,
    x_ref, cot_ref, small_ref, in_ref, gu_ref, out_ref, down_ref,
    x_all, cot_all, small_all, in_all, gu_all, out_all, down_all,
    local_sem, z_send, z_recv, p_send, p_recv, c_send, c_recv,
):
    dp, fs, pair, core, partner = place()
    z_peers = [(dp, lax.rem(fs + o, fs_count)) for o in range(1, fs_count)]
    p_peers = [(lax.rem(pair + o, pairs) * CORES + core, fs) for o in range(1, pairs)]
    p_from = [lax.rem(pair + pairs - o, pairs) * CORES + core for o in range(1, pairs)]
    greet(z_peers + p_peers + [partner])
    spread = [small_all, in_all, gu_all, out_all, down_all]

    across = [[None] * len(p_peers) for _ in spread]
    twins = [[None] * pairs for _ in spread]

    def spread_own(kind, src):
        dst = spread[kind].at[dp]
        for o, peer in enumerate(p_peers):
            across[kind][o] = push(src, dst, p_send, p_recv, (kind, o), peer)
        twins[kind][0] = push(src, dst, c_send, c_recv, (kind, 0), partner)

    along = [[], [], [], [], []]
    for o, peer in enumerate(z_peers):
        to = peer[1]
        along[0].append(push(small_ref, small_all.at[dp, fs], z_send, z_recv, (0, o), peer))
        along[1].append(push(in_ref.at[to], in_all.at[dp, fs], z_send, z_recv, (1, o), peer))
    for o, peer in enumerate(z_peers):
        to = peer[1]
        along[2].append(push(gu_ref.at[to], gu_all.at[dp, fs], z_send, z_recv, (2, o), peer))
    for o, peer in enumerate(z_peers):
        along[3].append(push(x_ref, x_all.at[fs], z_send, z_recv, (3, o), peer))
    for o, peer in enumerate(z_peers):
        along[4].append(push(cot_ref, cot_all.at[fs], z_send, z_recv, (4, o), peer))
    spread_own(3, out_ref)
    spread_own(4, down_ref)
    local = []
    for index, (src, dst) in enumerate(
        [
            (small_ref, small_all.at[dp, fs]),
            (in_ref.at[fs], in_all.at[dp, fs]),
            (gu_ref.at[fs], gu_all.at[dp, fs]),
            (x_ref, x_all.at[fs]),
            (cot_ref, cot_all.at[fs]),
            (out_ref, out_all.at[dp]),
            (down_ref, down_all.at[dp]),
        ]
    ):
        copy = pltpu.make_async_copy(src, dst, local_sem.at[index])
        copy.start()
        local.append(copy)
    for kind in range(3):
        local[kind].wait()
        for copy in along[kind]:
            copy.wait_recv()
        spread_own(kind, spread[kind].at[dp])
    for kind in (3, 0, 1, 4, 2):
        for o, source in enumerate(p_from):
            across[kind][o].wait_recv()
            block = spread[kind].at[source]
            twins[kind][o + 1] = push(block, block, c_send, c_recv, (kind, o + 1), partner)
    for copy in local[3:]:
        copy.wait()
    for copy in along[3] + along[4]:
        copy.wait_recv()
    for row in along + across:
        for copy in row:
            copy.wait_send()
    for row in twins:
        for copy in row:
            copy.wait()


def gather_all(x, cot, small, in_blocks, gu_blocks, out_shard, down_shard):
    dp_count, fs_count = lax.axis_size("dp"), lax.axis_size("fsdp")
    pairs = dp_count // CORES
    arrays = (x, cot, small, in_blocks, gu_blocks, out_shard, down_shard)
    shapes = (
        (fs_count,) + x.shape,
        (fs_count,) + cot.shape,
        (dp_count, fs_count) + small.shape,
        (dp_count,) + in_blocks.shape,
        (dp_count,) + gu_blocks.shape,
        (dp_count,) + out_shard.shape,
        (dp_count,) + down_shard.shape,
    )
    return pl.pallas_call(
        functools.partial(gather_kernel, pairs, fs_count),
        out_shape=[jax.ShapeDtypeStruct(shape, x.dtype) for shape in shapes],
        in_specs=[pl.BlockSpec(memory_space=pltpu.VMEM)] * len(arrays),
        out_specs=[pl.BlockSpec(memory_space=pl.ANY)] * len(shapes),
        scratch_shapes=[
            pltpu.SemaphoreType.DMA((7,)),
            pltpu.SemaphoreType.DMA((5, fs_count - 1)),
            pltpu.SemaphoreType.DMA((5, fs_count - 1)),
            pltpu.SemaphoreType.DMA((5, pairs - 1)),
            pltpu.SemaphoreType.DMA((5, pairs - 1)),
            pltpu.SemaphoreType.DMA((5, pairs)),
            pltpu.SemaphoreType.DMA((5, pairs)),
        ],
        compiler_params=pltpu.CompilerParams(collective_id=0, has_side_effects=True),
        name="gather_all",
    )(*arrays)


def line_kernel(count, fs_count, whole, *refs):
    sources, landed = refs[:count], refs[count : 2 * count]
    local_sem, sends, recvs = refs[2 * count :]
    dp, fs, _, _, _ = place()
    targets = [lax.rem(fs + o, fs_count) for o in range(1, fs_count)]
    greet([(dp, to) for to in targets])
    copies = [
        push(src if whole else src.at[to], dst.at[fs], sends, recvs, (k, o), (dp, to))
        for k, (src, dst) in enumerate(zip(sources, landed))
        for o, to in enumerate(targets)
    ]
    local = []
    for k, (src, dst) in enumerate(zip(sources, landed)):
        copy = pltpu.make_async_copy(src if whole else src.at[fs], dst.at[fs], local_sem.at[k])
        copy.start()
        local.append(copy)
    for copy in local + copies:
        copy.wait()


def along_line(arrays, whole, collective_id, name):
    fs_count = lax.axis_size("fsdp")
    count = len(arrays)
    return pl.pallas_call(
        functools.partial(line_kernel, count, fs_count, whole),
        out_shape=[
            jax.ShapeDtypeStruct(((fs_count,) + a.shape) if whole else a.shape, a.dtype)
            for a in arrays
        ],
        in_specs=[pl.BlockSpec(memory_space=pltpu.VMEM)] * count,
        out_specs=[pl.BlockSpec(memory_space=pl.ANY)] * count,
        scratch_shapes=[
            pltpu.SemaphoreType.DMA((count,)),
            pltpu.SemaphoreType.DMA((count, fs_count - 1)),
            pltpu.SemaphoreType.DMA((count, fs_count - 1)),
        ],
        compiler_params=pltpu.CompilerParams(collective_id=collective_id, has_side_effects=True),
        name=name,
    )(*arrays)


def whole_sequence(rows, collective_id, name):
    (received,) = along_line([rows], True, collective_id, name)
    return received.reshape(-1, rows.shape[1])


def token_pieces(partial_value):
    fs_count = lax.axis_size("fsdp")
    rows, columns = partial_value.shape
    return partial_value.astype(jnp.bfloat16).reshape(fs_count, rows // fs_count, columns)


def token_share(partial_value, collective_id, name):
    (received,) = along_line([token_pieces(partial_value)], False, collective_id, name)
    return jnp.sum(received.astype(jnp.float32), axis=0)


def token_share_async(partial_value):
    received = lax.all_to_all(
        token_pieces(partial_value), "fsdp", split_axis=0, concat_axis=0, tiled=True
    )
    return jnp.sum(received.astype(jnp.float32), axis=0)


def twin_kernel(count, pairs, *refs):
    partials, received = refs[:count], refs[count : 2 * count]
    sends, recvs = refs[2 * count :]
    _, _, _, core, partner = place()
    greet([partner])
    copies = [
        push(partial.at[j, 1 - core], landed.at[j], sends, recvs, (k, j), partner)
        for k, (partial, landed) in enumerate(zip(partials, received))
        for j in range(pairs)
    ]
    for copy in copies:
        copy.wait()


def pair_kernel(count, pairs, fs_count, *refs):
    partials, pieces = refs[:count], refs[count]
    received, pieces_in = refs[count + 1 : 2 * count + 1], refs[2 * count + 1]
    sends, recvs, z_sends, z_recvs = refs[2 * count + 2 :]
    dp, fs, pair, core, _ = place()
    targets = [lax.rem(pair + o, pairs) for o in range(1, pairs)]
    peers = [(to * CORES + core, fs) for to in targets]
    z_targets = [lax.rem(fs + o, fs_count) for o in range(1, fs_count)]
    greet(peers + [(dp, to) for to in z_targets])
    copies = [
        push(partial.at[to], landed.at[o], sends, recvs, (k, o), peer)
        for k, (partial, landed) in enumerate(zip(partials, received))
        for o, (to, peer) in enumerate(zip(targets, peers))
    ]
    copies += [
        push(pieces.at[to], pieces_in.at[o], z_sends, z_recvs, o, (dp, to))
        for o, to in enumerate(z_targets)
    ]
    for copy in copies:
        copy.wait()


def twin_exchange(partials):
    count = len(partials)
    pairs = lax.axis_size("dp") // CORES
    return pl.pallas_call(
        functools.partial(twin_kernel, count, pairs),
        out_shape=[jax.ShapeDtypeStruct((pairs,) + p.shape[-2:], p.dtype) for p in partials],
        in_specs=[pl.BlockSpec(memory_space=pl.ANY)] * count,
        out_specs=[pl.BlockSpec(memory_space=pl.ANY)] * count,
        scratch_shapes=[pltpu.SemaphoreType.DMA((count, pairs))] * 2,
        compiler_params=pltpu.CompilerParams(collective_id=1, has_side_effects=True),
        name="twin_exchange",
    )(*partials)


def pair_exchange(partials, pieces):
    count = len(partials)
    pairs, fs_count = lax.axis_size("dp") // CORES, lax.axis_size("fsdp")
    slots = [(pairs - 1, p) for p in partials] + [(fs_count - 1, pieces)]
    return pl.pallas_call(
        functools.partial(pair_kernel, count, pairs, fs_count),
        out_shape=[jax.ShapeDtypeStruct((n,) + p.shape[-2:], p.dtype) for n, p in slots],
        in_specs=[pl.BlockSpec(memory_space=pl.ANY)] * len(slots),
        out_specs=[pl.BlockSpec(memory_space=pl.ANY)] * len(slots),
        scratch_shapes=[
            pltpu.SemaphoreType.DMA((count, pairs - 1)),
            pltpu.SemaphoreType.DMA((count, pairs - 1)),
            pltpu.SemaphoreType.DMA((fs_count - 1,)),
            pltpu.SemaphoreType.DMA((fs_count - 1,)),
        ],
        compiler_params=pltpu.CompilerParams(collective_id=2, has_side_effects=True),
        name="pair_exchange",
    )(*partials, pieces)


def reduce_all(partials, pieces):
    dp_count = lax.axis_size("dp")
    pairs = dp_count // CORES
    dp = lax.axis_index("dp")
    core, pair = lax.rem(dp, CORES), dp // CORES
    split = [
        p.reshape(pairs, CORES, p.shape[0] // dp_count, p.shape[1])
        for p in partials
    ]
    landed = twin_exchange(split)
    chip = [
        (
            lax.dynamic_index_in_dim(p, core, axis=1, keepdims=False).astype(jnp.float32)
            + r.astype(jnp.float32)
        ).astype(p.dtype)
        for p, r in zip(split, landed)
    ]
    *others, pieces_in = pair_exchange(chip, pieces)
    own_piece = lax.dynamic_index_in_dim(pieces, lax.axis_index("fsdp"), axis=0, keepdims=False)
    tokens = own_piece.astype(jnp.float32) + jnp.sum(pieces_in.astype(jnp.float32), axis=0)
    return tokens, [
        lax.dynamic_index_in_dim(p, pair, axis=0, keepdims=False).astype(jnp.float32)
        + jnp.sum(r.astype(jnp.float32), axis=0)
        for p, r in zip(chip, others)
    ]


def split_features(
    inputs,
    gain_mixer,
    weight_in,
    conv_taps,
    weight_out,
    gain_ffn,
    weight_gate,
    weight_up,
    weight_down,
    cotangent,
):
    dp_count = lax.axis_size("dp")
    fs_count = lax.axis_size("fsdp")
    width = weight_out.shape[1]
    part = weight_out.shape[0]
    quarter = dp_count * part
    hid = dp_count * weight_down.shape[0]

    small = jnp.concatenate([gain_mixer[None], gain_ffn[None], conv_taps], axis=0)
    lanes = max(128, part)
    small = jnp.pad(small, ((0, 8 - small.shape[0]), (0, lanes - part)))
    gu_blocks = jnp.concatenate(
        [
            column_blocks(weight_gate, 1, dp_count, fs_count),
            column_blocks(weight_up, 1, dp_count, fs_count),
        ],
        axis=2,
    )
    grad_out = cotangent[0]
    x_all, grad_all, small_all, in_cols, gu_cols, out_rows, down_rows = gather_all(
        inputs[0],
        grad_out,
        small,
        column_blocks(weight_in, 3, dp_count, fs_count),
        gu_blocks,
        weight_out,
        weight_down,
    )
    x_all = x_all.reshape(-1, width)
    grad_all = grad_all.reshape(-1, width)
    in_cols = in_cols.reshape(width, 3 * quarter)
    gu_cols = gu_cols.reshape(width, 2 * hid)
    out_rows = out_rows.reshape(quarter, width)
    down_rows = down_rows.reshape(hid, width)
    small_all = small_all[:, :, : KW + 2, :part]
    gain1 = small_all[:, :, 0].reshape(width)
    gain2 = small_all[:, :, 1].reshape(width)
    taps32 = (
        lax.dynamic_index_in_dim(small_all, lax.axis_index("fsdp"), axis=1, keepdims=False)[:, 2:]
        .transpose(1, 0, 2)
        .reshape(KW, quarter)
        .astype(jnp.float32)
    )

    _, _, pre1_all = norm_forward(x_all.astype(jnp.float32), gain1)
    act1_all = pre1_all.astype(jnp.bfloat16)
    projected = product(act1_all, in_cols)
    bpart = projected[:, :quarter]
    cpart = projected[:, quarter : 2 * quarter]
    xpart = projected[:, 2 * quarter :]
    gated = bpart * xpart
    lagged_rows = [lagged(gated, offset) for offset in range(KW)]
    conv = taps32[0] * lagged_rows[0]
    for offset in range(1, KW):
        conv = conv + taps32[offset] * lagged_rows[offset]
    act2 = (cpart * conv).astype(jnp.bfloat16)
    hidden = inputs[0].astype(jnp.float32)
    normed1, scale1, _ = norm_forward(hidden, gain1)
    resid = hidden + token_share(product(act2, out_rows), 3, "share_out")
    normed2, scale2, pre2 = norm_forward(resid, gain2)
    act3_all = whole_sequence(pre2.astype(jnp.bfloat16), 4, "gather_ffn")
    gate_up = product(act3_all, gu_cols)
    gate, upval = gate_up[:, :hid], gate_up[:, hid:]
    sig = jax.nn.sigmoid(gate)
    act4 = (gate * sig * upval).astype(jnp.bfloat16)
    dact4 = product_nt(grad_all, down_rows)
    dgate = (dact4 * upval * sig * (1.0 + gate * (1.0 - sig))).astype(jnp.bfloat16)
    dupval = (dact4 * gate * sig).astype(jnp.bfloat16)
    dgu = jnp.concatenate([dgate, dupval], axis=1)
    dact3 = token_share(product_nt(dgu, gu_cols), 5, "share_ffn")
    down_pieces = token_pieces(product(act4, down_rows))
    dnorm2, g_gain2 = norm_backward(dact3, normed2, scale2, gain2)
    dresid = grad_out.astype(jnp.float32) + dnorm2
    dres_all = whole_sequence(dresid.astype(jnp.bfloat16), 6, "gather_dres")
    dact2 = product_nt(dres_all, out_rows)
    dcpart = dact2 * conv
    dconv = dact2 * cpart
    g_taps = jnp.stack(
        [jnp.sum(dconv * lagged_rows[offset], axis=0) for offset in range(KW)], axis=0
    )
    dgated = taps32[0] * dconv
    for offset in range(1, KW):
        dgated = dgated + taps32[offset] * leading(dconv, offset)
    dproj = jnp.concatenate([dgated * xpart, dcpart, dgated * bpart], axis=1).astype(jnp.bfloat16)
    dact1 = token_share_async(product_nt(dproj, in_cols))
    dnorm1, g_gain1 = norm_backward(dact1, normed1, scale1, gain1)
    grad_inputs = dresid + dnorm1

    own_column = (jnp.arange(fs_count) == lax.axis_index("fsdp"))[None, None, :, None]
    taps_spread = jnp.where(own_column, g_taps.reshape(KW, dp_count, 1, part), 0.0).reshape(KW, width)
    small_grad = jnp.concatenate([g_gain1[None], g_gain2[None], taps_spread], axis=0)
    small_grad = jnp.pad(small_grad, ((0, 8 - small_grad.shape[0]), (0, 0)))
    small_grad = small_grad.reshape(8, dp_count, fs_count, part).transpose(1, 2, 0, 3)
    small_grad = jnp.pad(small_grad, ((0, 0), (0, 0), (0, 0), (0, lanes - part)))
    down_sum, (g_small, g_gu, g_down, g_in, g_out) = reduce_all(
        [small_grad.reshape(dp_count * fs_count * 8, lanes)]
        + [
            grad.astype(jnp.bfloat16)
            for grad in (
                product_tn(act3_all, dgu),
                product_tn(act4, grad_all),
                product_tn(act1_all, dproj),
                product_tn(act2, dres_all),
            )
        ],
        down_pieces,
    )
    outputs = (resid + down_sum).astype(jnp.bfloat16)
    moved = jnp.concatenate([g_in, g_gu], axis=1).astype(jnp.bfloat16)
    moved, small_parts = along_line(
        [
            moved.reshape(fs_count, part, 3 * quarter + 2 * hid),
            g_small.reshape(fs_count, 8, lanes),
        ],
        False,
        7,
        "owner_exchange",
    )
    moved = moved.astype(jnp.float32)
    g_in_owned = moved[:, :, : 3 * quarter]
    g_gu_owned = moved[:, :, 3 * quarter :]
    small_owned = jnp.sum(small_parts, axis=0)[: KW + 2, :part]
    return (
        outputs[None],
        grad_inputs[None],
        small_owned[0],
        column_join(g_in_owned, 3, dp_count, fs_count),
        small_owned[2:],
        g_out,
        small_owned[1],
        column_join(g_gu_owned[:, :, :hid], 1, dp_count, fs_count),
        column_join(g_gu_owned[:, :, hid:], 1, dp_count, fs_count),
        g_down,
    )

HALO = 16


class Mover:
    def __init__(self, sends, recvs, locals_):
        self.sends, self.recvs, self.locals = sends, recvs, locals_
        self.count = 0
        self.local_count = 0
        self.open = []

    def push(self, src, dst, peer):
        copy = push(src, dst, self.sends, self.recvs, self.count, peer)
        self.count += 1
        self.open.append(copy)
        return copy

    def local(self, src, dst):
        copy = pltpu.make_async_copy(src, dst, self.locals.at[self.local_count])
        self.local_count += 1
        copy.start()
        return copy

    def finish(self):
        for copy in self.open:
            copy.wait_send()


class Line:
    def __init__(self, move, slot, dp, fs, fs_count):
        self.move, self.slot, self.dp, self.fs, self.size = move, slot, dp, fs, fs_count
        self.base = move.count
        move.count += CORES * fs_count

    def copy(self, source, up):
        index = self.base + CORES * source + (1 if up else 0)
        to = lax.rem(self.fs + (1 if up else self.size - 1), self.size)
        return pltpu.make_async_remote_copy(
            src_ref=self.slot(source),
            dst_ref=self.slot(source),
            send_sem=self.move.sends.at[index],
            recv_sem=self.move.recvs.at[index],
            device_id=(self.dp, to),
            device_id_type=MESH,
        )

    def start(self):
        @pl.when(self.fs < self.size - 1)
        def _():
            self.copy(self.fs, True).start()

        @pl.when(self.fs > 0)
        def _():
            self.copy(self.fs, False).start()

    def step(self, hop):
        below, above = self.fs - hop, self.fs + hop

        @pl.when(below >= 0)
        def _():
            self.copy(below, True).wait_recv()

            @pl.when(self.fs < self.size - 1)
            def _():
                self.copy(below, True).start()

        @pl.when(above < self.size)
        def _():
            self.copy(above, False).wait_recv()

            @pl.when(self.fs > 0)
            def _():
                self.copy(above, False).start()

    def finish(self):
        for hop in range(self.size):

            @pl.when((self.fs - hop >= 0) & (self.fs < self.size - 1))
            def _():
                self.copy(self.fs - hop, True).wait_send()

            @pl.when((self.fs + hop < self.size) & (self.fs > 0))
            def _():
                self.copy(self.fs + hop, False).wait_send()


class LineSum:
    def __init__(self, move, own, send, land, dp, fs, fs_count):
        self.move, self.own, self.send, self.land = move, own, send, land
        self.dp, self.fs, self.size = dp, fs, fs_count
        self.base = move.count
        move.count += CORES * fs_count

    def copy(self, dest, up, holder):
        index = self.base + CORES * dest + (1 if up else 0)
        to = lax.rem(holder + (1 if up else self.size - 1), self.size)
        slot = dest if up else jnp.where(dest == to, self.size, dest)
        return pltpu.make_async_remote_copy(
            src_ref=self.send.at[dest],
            dst_ref=self.land.at[slot],
            send_sem=self.move.sends.at[index],
            recv_sem=self.move.recvs.at[index],
            device_id=(self.dp, to),
            device_id_type=MESH,
        )

    def source(self, dest, up):
        return self.copy(dest, up, lax.rem(self.fs + (self.size - 1 if up else 1), self.size))

    def start(self):
        last = self.size - 1
        for far in range(last):

            @pl.when(self.fs == 0)
            def _():
                self.send[last - far] = self.own(last - far).astype(jnp.bfloat16)
                self.copy(last - far, True, self.fs).start()

            @pl.when(self.fs == last)
            def _():
                self.send[far] = self.own(far).astype(jnp.bfloat16)
                self.copy(far, False, self.fs).start()

    def relay(self, dest, up):
        self.source(dest, up).wait_recv()
        total = self.own(dest).astype(jnp.float32) + self.land[dest].astype(jnp.float32)
        self.send[dest] = total.astype(jnp.bfloat16)
        self.copy(dest, up, self.fs).start()

    def step(self, hop):
        last = self.size - 1
        if hop < last:

            @pl.when((self.fs >= 1) & (self.fs <= hop))
            def _():
                self.relay(self.fs + last - hop, True)

            @pl.when((self.fs < last) & (last - self.fs <= hop))
            def _():
                self.relay(self.fs + hop - last, False)

    def total(self, out):
        out[...] = self.own(self.fs).astype(jnp.float32)

        @pl.when(self.fs > 0)
        def _():
            self.source(self.fs, True).wait_recv()
            out[...] += self.land[self.fs].astype(jnp.float32)

        @pl.when(self.fs < self.size - 1)
        def _():
            self.source(self.fs, False).wait_recv()
            out[...] += self.land[self.size].astype(jnp.float32)

    def finish(self):
        for dest in range(self.size):

            @pl.when(self.fs < dest)
            def _():
                self.copy(dest, True, self.fs).wait_send()

            @pl.when(self.fs > dest)
            def _():
                self.copy(dest, False, self.fs).wait_send()


def seats(pairs, fs_count):
    dp, fs, pair, core, partner = place()
    z_peers = [(dp, lax.rem(fs + o, fs_count)) for o in range(1, fs_count)]
    p_peers = [(lax.rem(pair + o, pairs) * CORES + core, fs) for o in range(1, pairs)]
    p_from = [lax.rem(pair + pairs - o, pairs) for o in range(1, pairs)]
    return dp, fs, pair, core, partner, z_peers, p_peers, p_from


def norm_scale(hidden):
    return lax.rsqrt(jnp.mean(hidden * hidden, axis=-1, keepdims=True) + EPS)


def mixer_forward_kernel(
    pairs, fs_count,
    x_ref, cot_ref, small_ref, in_hbm, gate_hbm, up_hbm, out_ref, down_ref,
    act1_out, proj_out, act2_out, in_out_o, out_out, gains_out, taps_out, resid_out,
    act3_out, cot_out, gu_all, down_all,
    act1_o, proj_o, act2_o, in_all, out_all, gains_o, taps_o, resid_o, act3_all, cot_all,
    x_all, halo_all, small_all, in_ref, gate_ref, up_ref, in_blk, gu_blk,
    tw_out, tw_in, pr_out, pr_in, local_sem, sends, recvs,
):
    dp, fs, pair, core, partner, z_peers, p_peers, p_from = seats(pairs, fs_count)
    count = pairs * CORES
    tokens, width = x_ref.shape
    part = in_ref.shape[0]
    feat = width // count
    inner = gate_ref.shape[1] // (count * fs_count)
    hid = inner * count
    other = 1 - core
    move = Mover(sends, recvs, local_sem)
    f32 = jnp.float32

    in_local = move.local(in_hbm, in_ref)
    x_local = move.local(x_ref, x_all.at[dp])
    gate_local = move.local(gate_hbm, gate_ref)
    up_local = move.local(up_hbm, up_ref)
    out_local = move.local(out_ref, out_all.at[fs])
    cot_local = move.local(cot_ref, cot_all.at[fs])
    down_local = move.local(down_ref, down_all.at[dp])
    crossed = [(peer[0] + other - core, fs) for peer in p_peers]
    greet(z_peers + p_peers + crossed + [partner])
    small_z = [move.push(small_ref, small_all.at[dp, fs], peer) for peer in z_peers]
    halo_next = move.push(x_ref.at[pl.ds(tokens - HALO, HALO)], halo_all.at[dp, pl.ds(0, HALO)], z_peers[0])
    halo_prev = move.push(x_ref.at[pl.ds(0, HALO)], halo_all.at[dp, pl.ds(HALO, HALO)], z_peers[-1])
    in_local.wait()
    for to in range(count):
        for k in range(3):
            in_blk[to % CORES, to // CORES, :, k * feat : (k + 1) * feat] = in_ref[
                :, k * width + to * feat : k * width + (to + 1) * feat
            ]
    in_twin = move.push(in_blk.at[other, pair], in_all.at[dp, fs], partner)
    in_via = [
        move.push(in_blk.at[other, peer[0] // CORES], in_all.at[dp, fs], peer) for peer in crossed
    ]
    in_out = [move.push(in_blk.at[core, peer[0] // CORES], in_all.at[dp, fs], peer) for peer in p_peers]
    x_out = [move.push(x_ref, x_all.at[dp], peer) for peer in p_peers]
    x_twin = move.push(x_ref, x_all.at[dp], partner)
    small_all[dp, fs] = small_ref[...]
    in_all[dp, fs] = in_blk[core, pair]
    gate_local.wait()
    up_local.wait()
    for which, ref in enumerate((gate_ref, up_ref)):
        wide = ref[...].astype(f32)
        for to in range(fs_count):
            pieces = [
                wide[:, (d * fs_count + to) * inner : (d * fs_count + to + 1) * inner]
                for d in range(count)
            ]
            gu_blk[to, :, which * hid : (which + 1) * hid] = jnp.concatenate(pieces, axis=1).astype(
                jnp.bfloat16
            )
    gu_local = move.local(gu_blk.at[fs], gu_all.at[dp, fs])
    for copy in small_z:
        copy.wait_recv()
    small_out = [move.push(small_all.at[dp], small_all.at[dp], peer) for peer in p_peers]
    small_twin = [move.push(small_all.at[dp], small_all.at[dp], partner)]
    halo_next.wait_recv()
    halo_prev.wait_recv()
    halo_out = [move.push(halo_all.at[dp], halo_all.at[dp], peer) for peer in p_peers]
    halo_twin = [move.push(halo_all.at[dp], halo_all.at[dp], partner)]
    for copy in in_out + in_via + [in_twin]:
        copy.wait_recv()
    in_line = Line(move, lambda f: in_all.at[:, f], dp, fs, fs_count)
    out_line = Line(move, lambda f: out_all.at[f], dp, fs, fs_count)
    cot_line = Line(move, lambda f: cot_all.at[f], dp, fs, fs_count)
    act3_line = Line(move, lambda f: act3_all.at[f], dp, fs, fs_count)
    in_line.start()
    out_local.wait()
    out_line.start()
    down_out = [move.push(down_ref, down_all.at[dp], peer) for peer in p_peers]
    down_twin = [move.push(down_ref, down_all.at[dp], partner)]
    in_line.step(1)
    out_line.step(1)

    small_rel, x_rel = [], []
    for o, source in enumerate(p_from):
        src = source * CORES + core
        small_out[o].wait_recv()
        halo_out[o].wait_recv()
        x_out[o].wait_recv()
        small_rel.append(move.push(small_all.at[src], small_all.at[src], partner))
        x_rel.append(move.push(halo_all.at[src], halo_all.at[src], partner))
        x_rel.append(move.push(x_all.at[src], x_all.at[src], partner))
    in_line.step(2)
    out_line.step(2)
    gu_z = [move.push(gu_blk.at[peer[1]], gu_all.at[dp, fs], peer) for peer in z_peers]
    for copy in small_twin + small_rel + [x_twin] + halo_twin + x_rel:
        copy.wait_recv()
    x_local.wait()

    for d in range(count):
        total = small_all[d, 0].astype(f32)
        for f in range(1, fs_count):
            total = total + small_all[d, f].astype(f32)
        gains_o[:, d * feat : (d + 1) * feat] = total
    total = small_all[dp, 0].astype(f32)
    for f in range(1, fs_count):
        total = total + small_all[dp, f].astype(f32)
    taps_o[...] = total
    has_prev, has_next = fs > 0, fs < fs_count - 1

    def norm_step(i, carry):
        gain = gains_o[0:1, :]
        rows = x_all[i].astype(f32)
        act1_o[i, HALO : HALO + tokens] = (rows * norm_scale(rows) * gain).astype(jnp.bfloat16)
        edge = halo_all[i].astype(f32)
        edge = edge * norm_scale(edge) * gain
        act1_o[i, 0:HALO] = jnp.where(has_prev, edge[:HALO], 0.0).astype(jnp.bfloat16)
        act1_o[i, HALO + tokens :] = jnp.where(has_next, edge[HALO:], 0.0).astype(jnp.bfloat16)
        return carry

    lax.fori_loop(0, count, norm_step, 0)
    kept = [
        move.local(act1_o, act1_out), move.local(gains_o, gains_out), move.local(taps_o, taps_out)
    ]
    for hop in range(3, fs_count):
        in_line.step(hop)

    def project_step(i, carry):
        proj_o[i] = product(act1_o[i], in_all[...].reshape(width, 3 * feat))
        gated = proj_o[i, :, 0:feat] * proj_o[i, :, 2 * feat :]
        conv = taps_o[2:3, :] * gated[HALO : HALO + tokens]
        for k in range(1, KW):
            conv = conv + taps_o[2 + k : 3 + k, :] * gated[HALO - k : HALO - k + tokens]
        act2_o[i] = (proj_o[i, HALO : HALO + tokens, feat : 2 * feat] * conv).astype(jnp.bfloat16)
        return carry

    lax.fori_loop(0, count, project_step, 0)
    cot_local.wait()
    cot_line.start()
    kept += [
        move.local(proj_o, proj_out), move.local(act2_o, act2_out), move.local(in_all, in_out_o)
    ]
    for hop in range(3, fs_count):
        out_line.step(hop)
    kept.append(move.local(out_all, out_out))

    def out_partial(dest):
        return product(act2_o[dest], out_all[...].reshape(feat, width))

    order = [lax.rem(pair + o, pairs) for o in range(1, pairs)] + [pair]
    share_tw = []
    for o, j in enumerate(order):
        tw_out[o] = out_partial(j * CORES + other).astype(jnp.bfloat16)
        share_tw.append(move.push(tw_out.at[o], tw_in.at[o], partner))
    share_pr = []
    for o, j in enumerate(order):
        value = out_partial(j * CORES + core)
        share_tw[o].wait_recv()
        value = value + tw_in[o].astype(f32)
        if o < pairs - 1:
            pr_out[o] = value.astype(jnp.bfloat16)
            share_pr.append(move.push(pr_out.at[o], pr_in.at[o], p_peers[o]))
        else:
            resid_o[...] = value + x_all[dp].astype(f32)
    cot_line.step(1)
    for copy in gu_z:
        copy.wait_recv()
    gu_local.wait()
    gu_out = [move.push(gu_all.at[dp], gu_all.at[dp], peer) for peer in p_peers]
    gu_twin = [move.push(gu_all.at[dp], gu_all.at[dp], partner)]
    for copy in share_pr:
        copy.wait_recv()
    if fs_count > 2:
        cot_line.step(2)
    resid = resid_o[...]
    for o in range(pairs - 1):
        resid = resid + pr_in[o].astype(f32)
    resid_o[...] = resid
    act3_all[fs] = (resid * norm_scale(resid) * gains_o[1:2, :]).astype(jnp.bfloat16)
    act3_line.start()
    kept.append(move.local(resid_o, resid_out))
    for o, source in enumerate(p_from):
        src = source * CORES + core
        down_out[o].wait_recv()
        down_twin.append(move.push(down_all.at[src], down_all.at[src], partner))
    for hop in range(1, fs_count):
        act3_line.step(hop)
    for hop in range(3, fs_count):
        cot_line.step(hop)
    kept += [move.local(act3_all, act3_out), move.local(cot_all, cot_out)]
    for o, source in enumerate(p_from):
        src = source * CORES + core
        gu_out[o].wait_recv()
        gu_twin.append(move.push(gu_all.at[src], gu_all.at[src], partner))
    for copy in down_twin + gu_twin:
        copy.wait_recv()
    down_local.wait()
    for copy in kept:
        copy.wait()
    move.finish()
    for line in (in_line, out_line, cot_line, act3_line):
        line.finish()


def mixer_forward(x, cot, small, w_in, w_gate, w_up, w_out, w_down):
    dp_count, fs_count = lax.axis_size("dp"), lax.axis_size("fsdp")
    pairs = dp_count // CORES
    tokens, width = x.shape
    part = w_in.shape[0]
    feat = width // dp_count
    hid = w_gate.shape[1] // fs_count
    bf, f32 = jnp.bfloat16, jnp.float32
    shape = jax.ShapeDtypeStruct
    long = tokens + 2 * HALO
    in_vmem = [
        shape((dp_count, long, width), bf),
        shape((dp_count, long, 3 * feat), f32),
        shape((dp_count, tokens, feat), bf),
        shape((dp_count, fs_count, part, 3 * feat), bf),
        shape((fs_count, part, width), bf),
        shape((small.shape[0], width), f32),
        shape((small.shape[0], feat), f32),
        shape((tokens, width), f32),
    ]
    in_vmem += [shape((fs_count, tokens, width), bf)] * 2
    anywhere = [
        shape((dp_count, fs_count, part, 2 * hid), bf),
        shape((dp_count,) + w_down.shape, bf),
    ]
    slots = 20 * fs_count + 20 * pairs + 40
    return pl.pallas_call(
        functools.partial(mixer_forward_kernel, pairs, fs_count),
        out_shape=in_vmem + anywhere,
        in_specs=[
            pl.BlockSpec(memory_space=pltpu.VMEM if index == 2 else pltpu.HBM) for index in range(8)
        ],
        out_specs=[pl.BlockSpec(memory_space=pltpu.HBM)] * (len(in_vmem) + len(anywhere)),
        scratch_shapes=[pltpu.VMEM(item.shape, item.dtype) for item in in_vmem]
        + [
            pltpu.VMEM((dp_count, tokens, width), bf),
            pltpu.VMEM((dp_count, 2 * HALO, width), bf),
            pltpu.VMEM((dp_count, fs_count) + small.shape, bf),
            pltpu.VMEM(w_in.shape, bf),
            pltpu.VMEM(w_gate.shape, bf),
            pltpu.VMEM(w_up.shape, bf),
            pltpu.VMEM((CORES, pairs, part, 3 * feat), bf),
            pltpu.VMEM((fs_count, part, 2 * hid), bf),
            pltpu.VMEM((pairs, tokens, width), bf),
            pltpu.VMEM((pairs, tokens, width), bf),
            pltpu.VMEM((pairs - 1, tokens, width), bf),
            pltpu.VMEM((pairs - 1, tokens, width), bf),
            pltpu.SemaphoreType.DMA((24,)),
            pltpu.SemaphoreType.DMA((slots,)),
            pltpu.SemaphoreType.DMA((slots,)),
        ],
        compiler_params=pltpu.CompilerParams(
            collective_id=8, has_side_effects=True, vmem_limit_bytes=60 * 1024 * 1024
        ),
        name="mixer_forward",
    )(x, cot, small, w_in, w_gate, w_up, w_out, w_down)


def mixer_backward_kernel(
    pairs, fs_count,
    x_h, gains_ref, taps_ref, resid_h, act1_h, proj_h, act2_h, in_h, out_h,
    gu_h, act3_h, dgate_h, dup_h, act4_h, cot_h, down_h,
    out_o, gx_o, gin_fin, gout_o, gu_zi, gdown_o, small_o,
    x_ref, resid_ref, act1_ref, proj_ref, act2_ref, in_w, out_w,
    gu_ref, act3_ref, dgu_ref, act4_ref, cot_ref, down_ref,
    d3_own, d3_rx, dn_ref, dn_tx, dn_rx, acc, gin_acc,
    ggu_two, gd_all, gu_tw, down_tw, gu_chip, down_chip, gu_rx, down_rx, gu_zo,
    dres_all, dproj, taps_acc, gin_p, gin_tx, gin_rx, gout_p, gout_tx, gout_rx, gin_own, gin_stage,
    tw_out, tw_in, pr_out, pr_in, sm_own, sm_rx, tp_rx, sm_p, sm_tw, sm_pr,
    local_sem, sends, recvs,
):
    dp, fs, pair, core, partner, z_peers, p_peers, p_from = seats(pairs, fs_count)
    count = pairs * CORES
    tokens, width = x_ref.shape
    feat = width // count
    part = feat // fs_count
    hid = act4_ref.shape[1]
    inner = hid // count
    other = 1 - core
    twin_dp = pair * CORES + other
    move = Mover(sends, recvs, local_sem)
    f32, bf = jnp.float32, jnp.bfloat16
    order = [lax.rem(pair + o, pairs) for o in range(1, pairs)] + [pair]

    dgate_l = move.local(dgate_h, dgu_ref.at[:, pl.ds(0, hid)])
    dup_l = move.local(dup_h, dgu_ref.at[:, pl.ds(hid, hid)])
    gu_l = move.local(gu_h, gu_ref)
    greet(z_peers + p_peers + [partner])
    dgate_l.wait()
    dup_l.wait()
    gu_l.wait()
    act3_l = move.local(act3_h, act3_ref)
    act4_l = move.local(act4_h, act4_ref)
    cot_l = move.local(cot_h, cot_ref)
    down_l = move.local(down_h, down_ref)
    late = [
        move.local(src, dst)
        for src, dst in (
            (x_h, x_ref), (resid_h, resid_ref), (out_h, out_w), (proj_h, proj_ref),
            (in_h, in_w), (act1_h, act1_ref), (act2_h, act2_ref),
        )
    ]

    d3_z = []
    for o, peer in enumerate(z_peers + [(dp, fs)]):
        at = pl.ds(pl.multiple_of(peer[1] * tokens, tokens), tokens)
        d3_own[o] = product_nt(dgu_ref[at, :], gu_ref[...].reshape(width, 2 * hid)).astype(bf)
        if o < fs_count - 1:
            d3_z.append(move.push(d3_own.at[o], d3_rx.at[o], peer))
    dn = LineSum(move, lambda f: dn_ref[f], dn_tx, dn_rx, dp, fs, fs_count)
    gin_line = LineSum(move, lambda f: gin_p[:, f], gin_tx, gin_rx, dp, fs, fs_count)
    gout_line = LineSum(move, lambda f: gout_p[f], gout_tx, gout_rx, dp, fs, fs_count)
    act3_l.wait()

    def gu_partial(dest):
        left = act3_ref[:, :, pl.ds(pl.multiple_of(dest * feat, feat), feat)]
        return product_tn(left.reshape(fs_count * tokens, feat), dgu_ref[...])

    def down_slot(dest):
        return pl.ds(pl.multiple_of(dest * inner, inner), inner)

    gu_t, gu_p = [], []
    for o, j in enumerate(order):
        ggu_two[o] = gu_partial(j * CORES + other).astype(bf)
        gu_t.append(move.push(ggu_two.at[o], gu_tw.at[o], partner))
    for o, j in enumerate(order):
        value = gu_partial(j * CORES + core)
        gu_t[o].wait_recv()
        gu_chip[o] = (value + gu_tw[o].astype(f32)).astype(bf)
        if o < pairs - 1:
            gu_p.append(move.push(gu_chip.at[o], gu_rx.at[o], p_peers[o]))
    act4_l.wait()
    cot_l.wait()
    down_l.wait()
    chunk = 3 * 128 if hid % (3 * 128) == 0 else 128

    def down_step(c, carry):
        at = pl.ds(pl.multiple_of(c * chunk, chunk), chunk)
        gd_all[at, :] = product_tn(
            act4_ref[:, at], cot_ref[...].reshape(fs_count * tokens, width)
        ).astype(bf)
        return carry

    lax.fori_loop(0, hid // chunk, down_step, 0)
    down_t = [
        move.push(gd_all.at[down_slot(j * CORES + other)], down_tw.at[o], partner)
        for o, j in enumerate(order)
    ]

    def dn_step(f, carry):
        at = pl.ds(pl.multiple_of(f * tokens, tokens), tokens)
        dn_ref[f] = product(act4_ref[at, :], down_ref[...].reshape(hid, width)).astype(bf)
        return carry

    lax.fori_loop(0, fs_count, dn_step, 0)
    for copy in late:
        copy.wait()

    for copy in d3_z:
        copy.wait_recv()
    dact3 = d3_own[fs_count - 1].astype(f32)
    for o in range(fs_count - 1):
        dact3 = dact3 + d3_rx[o].astype(f32)
    resid = resid_ref[...]
    scale2 = norm_scale(resid)
    normed2 = resid * scale2
    sm_own[1:2, :] = jnp.sum(dact3 * normed2, axis=0, keepdims=True)
    dnormed = dact3 * gains_ref[1:2, :]
    dresid = cot_ref[fs].astype(f32) + scale2 * (
        dnormed - normed2 * jnp.mean(dnormed * normed2, axis=-1, keepdims=True)
    )
    gx_o[...] = dresid
    dres_all[dp, 0:tokens] = dresid.astype(bf)
    mine = dres_all.at[dp, pl.ds(0, tokens)]
    edge = dres_all.at[dp, pl.ds(tokens, HALO)]
    halo_z = move.push(dres_all.at[dp, pl.ds(0, HALO)], edge, z_peers[-1])
    dres_out = [move.push(mine, mine, peer) for peer in p_peers]
    dres_twin = [move.push(mine, mine, partner)]
    dn.start()
    down_p = []
    for o, j in enumerate(order):
        down_t[o].wait_recv()
        down_chip[o] = (
            gd_all[down_slot(j * CORES + core), :].astype(f32) + down_tw[o].astype(f32)
        ).astype(bf)
    halo_z.wait_recv()
    edge_out = [move.push(edge, edge, peer) for peer in p_peers]
    dres_twin.append(move.push(edge, edge, partner))
    for o, source in enumerate(p_from):
        src = source * CORES + core
        dres_out[o].wait_recv()
        edge_out[o].wait_recv()
        dres_twin.append(move.push(dres_all.at[src], dres_all.at[src], partner))
    for o, peer in enumerate(p_peers):
        down_p.append(move.push(down_chip.at[o], down_rx.at[o], peer))
    dn.step(1)
    for copy in dres_twin:
        copy.wait_recv()

    taps_acc[...] = jnp.zeros(taps_acc.shape, f32)

    def mixer_step(i, carry):
        dact2 = product_nt(dres_all[i], out_w[...].reshape(feat, width))
        bpart = proj_ref[i, :, 0:feat]
        cpart = proj_ref[i, :, feat : 2 * feat]
        xpart = proj_ref[i, :, 2 * feat :]
        gated = bpart * xpart
        conv = taps_ref[2:3, :] * gated[HALO : HALO + tokens]
        for k in range(1, KW):
            conv = conv + taps_ref[2 + k : 3 + k, :] * gated[HALO - k : HALO - k + tokens]
        dconv = dact2 * cpart[HALO:]
        dcpart = dact2[:tokens] * conv
        dgated = taps_ref[2:3, :] * dconv[:tokens]
        for k in range(1, KW):
            dgated = dgated + taps_ref[2 + k : 3 + k, :] * dconv[k : k + tokens]
        for k in range(KW):
            taps_acc[k : k + 1, :] += jnp.sum(
                dconv[:tokens] * gated[HALO - k : HALO - k + tokens], axis=0, keepdims=True
            )
        dproj[i, :, 0:feat] = (dgated * xpart[HALO : HALO + tokens]).astype(bf)
        dproj[i, :, feat : 2 * feat] = dcpart.astype(bf)
        dproj[i, :, 2 * feat :] = (dgated * bpart[HALO : HALO + tokens]).astype(bf)
        return carry

    lax.fori_loop(0, count, mixer_step, 0)

    sm_own[0:1, :] = jnp.zeros((1, width), f32)
    sm_own[2:, :] = jnp.zeros((sm_own.shape[0] - 2, width), f32)

    def in_partial(dest):
        value = product_nt(dproj[dest], in_w[...].reshape(width, 3 * feat))
        left = act1_ref[dest, pl.ds(HALO, tokens), :].astype(f32)
        sm_own[0:1, :] += jnp.sum(value * left, axis=0, keepdims=True)
        return value

    def gin_step(c, carry):
        left = act1_ref[:, pl.ds(HALO, tokens), pl.ds(pl.multiple_of(c * feat, feat), feat)]
        grad = product_tn(
            left.reshape(count * tokens, feat), dproj[...].reshape(count * tokens, 3 * feat)
        )
        gin_p[c] = grad.astype(bf).reshape(fs_count, part, 3 * feat)
        return carry

    for copy in gu_p:
        copy.wait_recv()
    total = gu_chip[pairs - 1].astype(f32)
    for o in range(pairs - 1):
        total = total + gu_rx[o].astype(f32)
    gu_zo[...] = total.astype(bf).reshape(fs_count, part, 2 * hid)
    gu_z = [move.push(gu_zo.at[peer[1]], gu_zi.at[fs], peer) for peer in z_peers]
    gu_zi[fs] = gu_zo[fs]

    lax.fori_loop(0, count, gin_step, 0)
    dn.step(2)
    gin_line.start()

    share_tw = []
    for o, j in enumerate(order):
        tw_out[o] = in_partial(j * CORES + other).astype(bf)
        share_tw.append(move.push(tw_out.at[o], tw_in.at[o], partner))

    gin_line.step(1)
    share_pr = []
    dact1 = None
    for o, j in enumerate(order):
        value = in_partial(j * CORES + core)
        share_tw[o].wait_recv()
        value = value + tw_in[o].astype(f32)
        if o < pairs - 1:
            pr_out[o] = value.astype(bf)
            share_pr.append(move.push(pr_out.at[o], pr_in.at[o], p_peers[o]))
        else:
            dact1 = value
    sm_own[0:1, :] = sm_own[0:1, :] / gains_ref[0:1, :]
    sm_z = [move.push(sm_own, sm_rx.at[o], peer) for o, peer in enumerate(z_peers)]
    taps_z = [move.push(taps_acc, tp_rx.at[o], peer) for o, peer in enumerate(z_peers)]
    gin_line.step(2)
    grad = product_tn(
        act2_ref[...].reshape(count * tokens, feat),
        dres_all[:, 0:tokens].reshape(count * tokens, width),
    )
    gout_p[...] = grad.astype(bf).reshape(fs_count, part, width)
    gout_line.start()
    for hop in range(3, fs_count):
        dn.step(hop)

    gout_line.step(1)
    for hop in range(3, fs_count):
        gin_line.step(hop)
    gin_line.total(gin_acc)
    for d in range(count):
        gin_own[d % CORES, d // CORES] = gin_acc[d].astype(bf)
    gin_t = move.push(gin_own.at[other], gin_stage, partner)
    gin_out = [
        move.push(gin_own.at[core, peer[0] // CORES], gin_fin.at[dp], peer) for peer in p_peers
    ]
    gin_fin[dp] = gin_own[core, pair]
    for copy in sm_z:
        copy.wait_recv()
    small_sum = sm_own[...]
    for o in range(fs_count - 1):
        small_sum = small_sum + sm_rx[o]
    for d in range(count):
        sm_p[d % CORES, d // CORES] = small_sum[:, d * feat : (d + 1) * feat]
    sm_t = move.push(sm_p.at[other], sm_tw, partner)
    gin_t.wait_recv()
    gin_via = [
        move.push(gin_stage.at[peer[0] // CORES], gin_fin.at[twin_dp], peer) for peer in p_peers
    ]
    gin_fin[twin_dp] = gin_stage[pair]


    for hop in range(2, fs_count):
        gout_line.step(hop)
    for copy in share_pr:
        copy.wait_recv()
    for o in range(pairs - 1):
        dact1 = dact1 + pr_in[o].astype(f32)
    hidden = x_ref[...].astype(f32)
    scale1 = norm_scale(hidden)
    normed1 = hidden * scale1
    dnormed = dact1 * gains_ref[0:1, :]
    gx_o[...] += scale1 * (dnormed - normed1 * jnp.mean(dnormed * normed1, axis=-1, keepdims=True))

    sm_t.wait_recv()
    for j in range(pairs):
        sm_tw[j] = sm_tw[j] + sm_p[core, j]
    sm_pair = [
        move.push(sm_tw.at[peer[0] // CORES], sm_pr.at[o], peer) for o, peer in enumerate(p_peers)
    ]
    for copy in down_p:
        copy.wait_recv()
    total = down_chip[pairs - 1].astype(f32)
    for o in range(pairs - 1):
        total = total + down_rx[o].astype(f32)
    gdown_o[...] = total
    dn.total(acc)
    out_o[...] = (resid_ref[...] + acc[...]).astype(bf)
    for copy in taps_z:
        copy.wait_recv()
    gout_line.total(gout_o)
    for copy in gu_z:
        copy.wait_recv()
    for copy in gin_out + gin_via:
        copy.wait_recv()
    for copy in sm_pair:
        copy.wait_recv()
    total = sm_tw[pair]
    for o in range(pairs - 1):
        total = total + sm_pr[o]
    taps = taps_acc[...]
    for o in range(fs_count - 1):
        taps = taps + tp_rx[o]
    small_o[0] = total
    small_o[1] = taps
    move.finish()
    for line in (dn, gin_line, gout_line):
        line.finish()


def mixer_backward(x, gains, taps, resid, act1, proj, act2, in_w, out_w, gu, act3, dgate, dup, act4, cot, down):
    dp_count, fs_count = lax.axis_size("dp"), lax.axis_size("fsdp")
    pairs = dp_count // CORES
    tokens, width = x.shape
    feat = width // dp_count
    part = feat // fs_count
    hid2 = 2 * dgate.shape[1]
    dgu = jax.ShapeDtypeStruct((dgate.shape[0], hid2), dgate.dtype)
    rows_down = down.shape[1]
    bf, f32 = jnp.bfloat16, jnp.float32
    shape = jax.ShapeDtypeStruct
    outs = [
        shape((tokens, width), bf),
        shape((tokens, width), f32),
        shape((dp_count, part, 3 * feat), bf),
        shape((part, width), f32),
        shape((fs_count, part, hid2), bf),
        shape((rows_down, width), f32),
        shape((2, 8, feat), f32),
    ]
    slots = 24 * fs_count + 20 * pairs + 40
    loaded = (x, resid, act1, proj, act2, in_w, out_w, gu, act3, dgu, act4, cot, down)
    scratch = [(item.shape, item.dtype) for item in loaded] + [
        ((fs_count, tokens, width), bf),
        ((fs_count - 1, tokens, width), bf),
        ((fs_count, tokens, width), bf),
        ((fs_count, tokens, width), bf),
        ((fs_count + 1, tokens, width), bf),
        ((tokens, width), f32),
        ((dp_count, part, 3 * feat), f32),
        ((pairs, feat, hid2), bf),
        ((hid2 // 2, width), bf),
        ((pairs, feat, hid2), bf),
        ((pairs, rows_down, width), bf),
        ((pairs, feat, hid2), bf),
        ((pairs, rows_down, width), bf),
        ((pairs - 1, feat, hid2), bf),
        ((pairs - 1, rows_down, width), bf),
        ((fs_count, part, hid2), bf),
        ((dp_count, tokens + HALO, width), bf),
        ((dp_count, tokens, 3 * feat), bf),
        ((8, feat), f32),
        ((dp_count, fs_count, part, 3 * feat), bf),
        ((fs_count, dp_count, part, 3 * feat), bf),
        ((fs_count + 1, dp_count, part, 3 * feat), bf),
        ((fs_count, part, width), bf),
        ((fs_count, part, width), bf),
        ((fs_count + 1, part, width), bf),
        ((CORES, pairs, part, 3 * feat), bf),
        ((pairs, part, 3 * feat), bf),
        ((pairs, tokens, width), bf),
        ((pairs, tokens, width), bf),
        ((pairs - 1, tokens, width), bf),
        ((pairs - 1, tokens, width), bf),
        ((8, width), f32),
        ((fs_count - 1, 8, width), f32),
        ((fs_count - 1, 8, feat), f32),
        ((CORES, pairs, 8, feat), f32),
        ((pairs, 8, feat), f32),
        ((pairs - 1, 8, feat), f32),
    ]
    return pl.pallas_call(
        functools.partial(mixer_backward_kernel, pairs, fs_count),
        out_shape=outs,
        in_specs=[
            pl.BlockSpec(memory_space=pltpu.VMEM if index in (1, 2) else pltpu.HBM)
            for index in range(16)
        ],
        out_specs=[pl.BlockSpec(memory_space=pltpu.VMEM)] * len(outs),
        scratch_shapes=[pltpu.VMEM(s, d) for s, d in scratch]
        + [pltpu.SemaphoreType.DMA((n,)) for n in (len(loaded) + 1, slots, slots)],
        compiler_params=pltpu.CompilerParams(
            collective_id=9, has_side_effects=True, vmem_limit_bytes=60 * 1024 * 1024
        ),
        name="mixer_backward",
    )(x, gains, taps, resid, act1, proj, act2, in_w, out_w, gu, act3, dgate, dup, act4, cot, down)


def finish_kernel(
    fs_count, count,
    out_i, gx_i, gin_h, gout_i, gu_h, gdown_i, small_i,
    out_o, gx_o, gin_o, gout_o, ggate_o, gup_o, gdown_o, gain1_o, gain2_o, taps_o,
    gin_fin, gu_zi, gin_v, gate_v, up_v, out_v, gx_v, gout_v, gdown_v, sems,
):
    part, feat = gout_i.shape[0], gin_fin.shape[2] // 3
    width, hid = gout_i.shape[1], gu_zi.shape[2] // 2
    inner = hid // count
    f32 = jnp.float32
    copies = []

    def send(src, dst):
        copy = pltpu.make_async_copy(src, dst, sems.at[len(copies)])
        copy.start()
        copies.append(copy)

    send(gin_h, gin_fin)
    send(gu_h, gu_zi)
    through = ((gx_i, gx_v, gx_o), (gdown_i, gdown_v, gdown_o), (out_i, out_v, out_o), (gout_i, gout_v, gout_o))
    for src, held, dst in through:
        send(src, held)
    gin_in, gu_in, *held_in = copies
    gin_count = len(copies)
    for copy, (src, held, dst) in zip(held_in, through):
        copy.wait()
        send(held, dst)
    gin_in.wait()
    for d in range(count):
        for k in range(3):
            gin_v[:, k * width + d * feat : k * width + (d + 1) * feat] = gin_fin[
                d, :, k * feat : (k + 1) * feat
            ].astype(f32)
    send(gin_v, gin_o)
    gu_in.wait()
    for which, (ref, dst) in enumerate(((gate_v, ggate_o), (up_v, gup_o))):
        wide = [gu_zi[f, :, which * hid : (which + 1) * hid].astype(f32) for f in range(fs_count)]
        pieces = [
            wide[f][:, d * inner : (d + 1) * inner] for d in range(count) for f in range(fs_count)
        ]
        ref[...] = jnp.concatenate(pieces, axis=1)
        send(ref, dst)
    fs = lax.axis_index("fsdp")
    small = small_i[...]
    mine = small[:, :, 0:part]
    for f in range(1, fs_count):
        mine = jnp.where(fs == f, small[:, :, f * part : (f + 1) * part], mine)
    gain1_o[...] = mine[0, 0:1]
    gain2_o[...] = mine[0, 1:2]
    taps_o[...] = mine[1, 0:KW]
    for copy in copies[gin_count:]:
        copy.wait()


def finish(out, gx, gin, gout, gu, gdown, small, wide_in, wide_ff):
    dp_count, fs_count = lax.axis_size("dp"), lax.axis_size("fsdp")
    part = gout.shape[0]
    f32 = jnp.float32
    shape = jax.ShapeDtypeStruct
    outs = [
        shape(out.shape, out.dtype),
        shape(gx.shape, f32),
        shape((part, wide_in), f32),
        shape(gout.shape, f32),
        shape((part, wide_ff), f32),
        shape((part, wide_ff), f32),
        shape(gdown.shape, f32),
        shape((1, part), f32),
        shape((1, part), f32),
        shape((KW, part), f32),
    ]
    return pl.pallas_call(
        functools.partial(finish_kernel, fs_count, dp_count),
        out_shape=outs,
        in_specs=[pl.BlockSpec(memory_space=pltpu.HBM)] * 6
        + [pl.BlockSpec(memory_space=pltpu.VMEM)],
        out_specs=[pl.BlockSpec(memory_space=pltpu.HBM)] * 7
        + [pl.BlockSpec(memory_space=pltpu.VMEM)] * 3,
        scratch_shapes=[
            pltpu.VMEM(gin.shape, gin.dtype),
            pltpu.VMEM(gu.shape, gu.dtype),
            pltpu.VMEM((part, wide_in), f32),
            pltpu.VMEM((part, wide_ff), f32),
            pltpu.VMEM((part, wide_ff), f32),
            pltpu.VMEM(out.shape, out.dtype),
            pltpu.VMEM(gx.shape, f32),
            pltpu.VMEM(gout.shape, f32),
            pltpu.VMEM(gdown.shape, f32),
            pltpu.SemaphoreType.DMA((13,)),
        ],
        compiler_params=pltpu.CompilerParams(vmem_limit_bytes=60 * 1024 * 1024),
        name="finish",
    )(out, gx, gin, gout, gu, gdown, small)


def split_tokens(
    inputs,
    gain_mixer,
    weight_in,
    conv_taps,
    weight_out,
    gain_ffn,
    weight_gate,
    weight_up,
    weight_down,
    cotangent,
):
    dp_count, fs_count = lax.axis_size("dp"), lax.axis_size("fsdp")
    fs = lax.axis_index("fsdp")
    tokens, width = inputs.shape[1:]
    part = weight_out.shape[0]
    hid = weight_gate.shape[1] // fs_count
    bf = jnp.bfloat16
    x, cot = inputs[0], cotangent[0]
    small = jnp.concatenate([gain_mixer[None], gain_ffn[None], conv_taps], axis=0)
    small = jnp.tile(jnp.pad(small, ((0, 16 - small.shape[0]), (0, 0))), (1, fs_count))
    lanes = lax.broadcasted_iota(jnp.int32, small.shape, 1)
    mine = (lanes >= fs * part) & (lanes < (fs + 1) * part)
    small = jnp.where(mine, small, jnp.zeros_like(small))
    (act1, proj, act2, in_w, out_w, gains, taps, resid, act3_all, cot_all, gu_all, down_rows) = mixer_forward(
        x, cot, small, weight_in, weight_gate, weight_up, weight_out, weight_down
    )
    gu_cols = gu_all.reshape(width, 2 * hid)
    gate_up = product(act3_all.reshape(-1, width), gu_cols)
    gate, upval = gate_up[:, :hid], gate_up[:, hid:]
    sig = jax.nn.sigmoid(gate)
    act4 = (gate * sig * upval).astype(bf)
    dact4 = product_nt(cot_all.reshape(-1, width), down_rows.reshape(hid, width))
    dgate = (dact4 * upval * sig * (1.0 + gate * (1.0 - sig))).astype(bf)
    dupval = (dact4 * gate * sig).astype(bf)
    parts = mixer_backward(
        x, gains, taps, resid, act1, proj, act2, in_w, out_w, gu_all, act3_all, dgate, dupval, act4, cot_all, down_rows
    )
    outputs, gx, gin, gout, ggate, gup, gdown, gain1, gain2, g_taps = finish(
        *parts, weight_in.shape[1], weight_gate.shape[1]
    )
    return (
        outputs[None], gx[None], gain1[0], gin, g_taps, gout, gain2[0], ggate, gup, gdown,
    )


def fits_tokens(inputs, weight_out, weight_gate):
    dp_count, fs_count = lax.axis_size("dp"), lax.axis_size("fsdp")
    tokens, width = inputs.shape[1:]
    return (
        dp_count % CORES == 0
        and dp_count > CORES
        and fs_count > 1
        and (width // dp_count) % 128 == 0
        and (weight_gate.shape[1] // fs_count) % 128 == 0
        and weight_out.shape[0] % 16 == 0
        and tokens % 16 == 0
        and inputs.shape[0] == 1
    )


def on_device(
    inputs,
    gain_mixer,
    weight_in,
    conv_taps,
    weight_out,
    gain_ffn,
    weight_gate,
    weight_up,
    weight_down,
    cotangent,
):
    form = split_tokens if fits_tokens(inputs, weight_out, weight_gate) else split_features
    return form(
        inputs,
        gain_mixer,
        weight_in,
        conv_taps,
        weight_out,
        gain_ffn,
        weight_gate,
        weight_up,
        weight_down,
        cotangent,
    )


def solution(mesh):
    in_specs = (
        P("dp", "fsdp", None),
        P(("dp", "fsdp")),
        P(("dp", "fsdp"), None),
        P(None, ("dp", "fsdp")),
        P(("dp", "fsdp"), None),
        P(("dp", "fsdp")),
        P(("dp", "fsdp"), None),
        P(("dp", "fsdp"), None),
        P(("dp", "fsdp"), None),
        P("dp", "fsdp", None),
    )
    out_specs = (
        P("dp", "fsdp", None),
        P("dp", "fsdp", None),
        P(("dp", "fsdp")),
        P(("dp", "fsdp"), None),
        P(None, ("dp", "fsdp")),
        P(("dp", "fsdp"), None),
        P(("dp", "fsdp")),
        P(("dp", "fsdp"), None),
        P(("dp", "fsdp"), None),
        P(("dp", "fsdp"), None),
    )
    return jax.shard_map(
        on_device, mesh=mesh, in_specs=in_specs, out_specs=out_specs, check_vma=False
    )
```

```python
import functools

import jax
import jax.numpy as jnp
from jax import lax
from jax.experimental import pallas as pl
from jax.experimental.pallas import tpu as pltpu
from jax.sharding import PartitionSpec as P

KW = 3


EPS = 1e-05

CORES = 2
MESH = pl.DeviceIdType.MESH


def product(left, right):
    return jnp.dot(left, right, preferred_element_type=jnp.float32)


def product_tn(left, right):
    return lax.dot_general(
        left, right, (((0,), (0,)), ((), ())), preferred_element_type=jnp.float32
    )


def product_nt(left, right):
    return lax.dot_general(
        left, right, (((1,), (1,)), ((), ())), preferred_element_type=jnp.float32
    )


def norm_forward(hidden, gain):
    scale = lax.rsqrt(jnp.mean(hidden * hidden, axis=-1, keepdims=True) + EPS)
    normed = hidden * scale
    return (normed, scale, normed * gain.astype(jnp.float32))


def norm_backward(dact, normed, scale, gain):
    dnormed = dact * gain.astype(jnp.float32)
    dhidden = scale * (dnormed - normed * jnp.mean(dnormed * normed, axis=-1, keepdims=True))
    return (dhidden, jnp.sum(dact * normed, axis=0))


def lagged(values, offset):
    zeros = jnp.zeros((offset, values.shape[1]), values.dtype)
    return jnp.concatenate([zeros, values[: values.shape[0] - offset]], axis=0)


def leading(values, offset):
    zeros = jnp.zeros((offset, values.shape[1]), values.dtype)
    return jnp.concatenate([values[offset:], zeros], axis=0)


def column_blocks(shard, lead, dp_count, fs_count):
    rows, columns = shard.shape
    inner = columns // (lead * dp_count * fs_count)
    pieces = shard.reshape(rows, lead, dp_count, fs_count, inner).transpose(3, 0, 1, 2, 4)
    return pieces.reshape(fs_count, rows, lead * dp_count * inner)


def column_join(blocks, lead, dp_count, fs_count):
    _, rows, columns = blocks.shape
    inner = columns // (lead * dp_count)
    pieces = blocks.reshape(fs_count, rows, lead, dp_count, inner).transpose(1, 2, 3, 0, 4)
    return pieces.reshape(rows, lead * dp_count * fs_count * inner)


def greet(peers):
    barrier = pltpu.get_barrier_semaphore()
    for peer in peers:
        pl.semaphore_signal(barrier, inc=1, device_id=peer, device_id_type=MESH)
    pl.semaphore_wait(barrier, len(peers))


def push(src, dst, sends, recvs, index, peer):
    copy = pltpu.make_async_remote_copy(
        src_ref=src,
        dst_ref=dst,
        send_sem=sends.at[index],
        recv_sem=recvs.at[index],
        device_id=peer,
        device_id_type=MESH,
    )
    copy.start()
    return copy


def place():
    dp, fs = lax.axis_index("dp"), lax.axis_index("fsdp")
    pair, core = dp // CORES, lax.rem(dp, CORES)
    return dp, fs, pair, core, (pair * CORES + 1 - core, fs)


def gather_kernel(
    pairs, fs_count,
    x_ref, cot_ref, small_ref, in_ref, gu_ref, out_ref, down_ref,
    x_all, cot_all, small_all, in_all, gu_all, out_all, down_all,
    local_sem, z_send, z_recv, p_send, p_recv, c_send, c_recv,
):
    dp, fs, pair, core, partner = place()
    z_peers = [(dp, lax.rem(fs + o, fs_count)) for o in range(1, fs_count)]
    p_peers = [(lax.rem(pair + o, pairs) * CORES + core, fs) for o in range(1, pairs)]
    p_from = [lax.rem(pair + pairs - o, pairs) * CORES + core for o in range(1, pairs)]
    greet(z_peers + p_peers + [partner])
    spread = [small_all, in_all, gu_all, out_all, down_all]

    across = [[None] * len(p_peers) for _ in spread]
    twins = [[None] * pairs for _ in spread]

    def spread_own(kind, src):
        dst = spread[kind].at[dp]
        for o, peer in enumerate(p_peers):
            across[kind][o] = push(src, dst, p_send, p_recv, (kind, o), peer)
        twins[kind][0] = push(src, dst, c_send, c_recv, (kind, 0), partner)

    along = [[], [], [], [], []]
    for o, peer in enumerate(z_peers):
        to = peer[1]
        along[0].append(push(small_ref, small_all.at[dp, fs], z_send, z_recv, (0, o), peer))
        along[1].append(push(in_ref.at[to], in_all.at[dp, fs], z_send, z_recv, (1, o), peer))
    for o, peer in enumerate(z_peers):
        to = peer[1]
        along[2].append(push(gu_ref.at[to], gu_all.at[dp, fs], z_send, z_recv, (2, o), peer))
    for o, peer in enumerate(z_peers):
        along[3].append(push(x_ref, x_all.at[fs], z_send, z_recv, (3, o), peer))
    for o, peer in enumerate(z_peers):
        along[4].append(push(cot_ref, cot_all.at[fs], z_send, z_recv, (4, o), peer))
    spread_own(3, out_ref)
    spread_own(4, down_ref)
    local = []
    for index, (src, dst) in enumerate(
        [
            (small_ref, small_all.at[dp, fs]),
            (in_ref.at[fs], in_all.at[dp, fs]),
            (gu_ref.at[fs], gu_all.at[dp, fs]),
            (x_ref, x_all.at[fs]),
            (cot_ref, cot_all.at[fs]),
            (out_ref, out_all.at[dp]),
            (down_ref, down_all.at[dp]),
        ]
    ):
        copy = pltpu.make_async_copy(src, dst, local_sem.at[index])
        copy.start()
        local.append(copy)
    for kind in range(3):
        local[kind].wait()
        for copy in along[kind]:
            copy.wait_recv()
        spread_own(kind, spread[kind].at[dp])
    for kind in (3, 0, 1, 4, 2):
        for o, source in enumerate(p_from):
            across[kind][o].wait_recv()
            block = spread[kind].at[source]
            twins[kind][o + 1] = push(block, block, c_send, c_recv, (kind, o + 1), partner)
    for copy in local[3:]:
        copy.wait()
    for copy in along[3] + along[4]:
        copy.wait_recv()
    for row in along + across:
        for copy in row:
            copy.wait_send()
    for row in twins:
        for copy in row:
            copy.wait()


def gather_all(x, cot, small, in_blocks, gu_blocks, out_shard, down_shard):
    dp_count, fs_count = lax.axis_size("dp"), lax.axis_size("fsdp")
    pairs = dp_count // CORES
    arrays = (x, cot, small, in_blocks, gu_blocks, out_shard, down_shard)
    shapes = (
        (fs_count,) + x.shape,
        (fs_count,) + cot.shape,
        (dp_count, fs_count) + small.shape,
        (dp_count,) + in_blocks.shape,
        (dp_count,) + gu_blocks.shape,
        (dp_count,) + out_shard.shape,
        (dp_count,) + down_shard.shape,
    )
    return pl.pallas_call(
        functools.partial(gather_kernel, pairs, fs_count),
        out_shape=[jax.ShapeDtypeStruct(shape, x.dtype) for shape in shapes],
        in_specs=[pl.BlockSpec(memory_space=pltpu.VMEM)] * len(arrays),
        out_specs=[pl.BlockSpec(memory_space=pl.ANY)] * len(shapes),
        scratch_shapes=[
            pltpu.SemaphoreType.DMA((7,)),
            pltpu.SemaphoreType.DMA((5, fs_count - 1)),
            pltpu.SemaphoreType.DMA((5, fs_count - 1)),
            pltpu.SemaphoreType.DMA((5, pairs - 1)),
            pltpu.SemaphoreType.DMA((5, pairs - 1)),
            pltpu.SemaphoreType.DMA((5, pairs)),
            pltpu.SemaphoreType.DMA((5, pairs)),
        ],
        compiler_params=pltpu.CompilerParams(collective_id=0, has_side_effects=True),
        name="gather_all",
    )(*arrays)


def line_kernel(count, fs_count, whole, *refs):
    sources, landed = refs[:count], refs[count : 2 * count]
    local_sem, sends, recvs = refs[2 * count :]
    dp, fs, _, _, _ = place()
    targets = [lax.rem(fs + o, fs_count) for o in range(1, fs_count)]
    greet([(dp, to) for to in targets])
    copies = [
        push(src if whole else src.at[to], dst.at[fs], sends, recvs, (k, o), (dp, to))
        for k, (src, dst) in enumerate(zip(sources, landed))
        for o, to in enumerate(targets)
    ]
    local = []
    for k, (src, dst) in enumerate(zip(sources, landed)):
        copy = pltpu.make_async_copy(src if whole else src.at[fs], dst.at[fs], local_sem.at[k])
        copy.start()
        local.append(copy)
    for copy in local + copies:
        copy.wait()


def along_line(arrays, whole, collective_id, name):
    fs_count = lax.axis_size("fsdp")
    count = len(arrays)
    return pl.pallas_call(
        functools.partial(line_kernel, count, fs_count, whole),
        out_shape=[
            jax.ShapeDtypeStruct(((fs_count,) + a.shape) if whole else a.shape, a.dtype)
            for a in arrays
        ],
        in_specs=[pl.BlockSpec(memory_space=pltpu.VMEM)] * count,
        out_specs=[pl.BlockSpec(memory_space=pl.ANY)] * count,
        scratch_shapes=[
            pltpu.SemaphoreType.DMA((count,)),
            pltpu.SemaphoreType.DMA((count, fs_count - 1)),
            pltpu.SemaphoreType.DMA((count, fs_count - 1)),
        ],
        compiler_params=pltpu.CompilerParams(collective_id=collective_id, has_side_effects=True),
        name=name,
    )(*arrays)


def whole_sequence(rows, collective_id, name):
    (received,) = along_line([rows], True, collective_id, name)
    return received.reshape(-1, rows.shape[1])


def token_pieces(partial_value):
    fs_count = lax.axis_size("fsdp")
    rows, columns = partial_value.shape
    return partial_value.astype(jnp.bfloat16).reshape(fs_count, rows // fs_count, columns)


def token_share(partial_value, collective_id, name):
    (received,) = along_line([token_pieces(partial_value)], False, collective_id, name)
    return jnp.sum(received.astype(jnp.float32), axis=0)


def token_share_async(partial_value):
    received = lax.all_to_all(
        token_pieces(partial_value), "fsdp", split_axis=0, concat_axis=0, tiled=True
    )
    return jnp.sum(received.astype(jnp.float32), axis=0)


def twin_kernel(count, pairs, *refs):
    partials, received = refs[:count], refs[count : 2 * count]
    sends, recvs = refs[2 * count :]
    _, _, _, core, partner = place()
    greet([partner])
    copies = [
        push(partial.at[j, 1 - core], landed.at[j], sends, recvs, (k, j), partner)
        for k, (partial, landed) in enumerate(zip(partials, received))
        for j in range(pairs)
    ]
    for copy in copies:
        copy.wait()


def pair_kernel(count, pairs, fs_count, *refs):
    partials, pieces = refs[:count], refs[count]
    received, pieces_in = refs[count + 1 : 2 * count + 1], refs[2 * count + 1]
    sends, recvs, z_sends, z_recvs = refs[2 * count + 2 :]
    dp, fs, pair, core, _ = place()
    targets = [lax.rem(pair + o, pairs) for o in range(1, pairs)]
    peers = [(to * CORES + core, fs) for to in targets]
    z_targets = [lax.rem(fs + o, fs_count) for o in range(1, fs_count)]
    greet(peers + [(dp, to) for to in z_targets])
    copies = [
        push(partial.at[to], landed.at[o], sends, recvs, (k, o), peer)
        for k, (partial, landed) in enumerate(zip(partials, received))
        for o, (to, peer) in enumerate(zip(targets, peers))
    ]
    copies += [
        push(pieces.at[to], pieces_in.at[o], z_sends, z_recvs, o, (dp, to))
        for o, to in enumerate(z_targets)
    ]
    for copy in copies:
        copy.wait()


def twin_exchange(partials):
    count = len(partials)
    pairs = lax.axis_size("dp") // CORES
    return pl.pallas_call(
        functools.partial(twin_kernel, count, pairs),
        out_shape=[jax.ShapeDtypeStruct((pairs,) + p.shape[-2:], p.dtype) for p in partials],
        in_specs=[pl.BlockSpec(memory_space=pl.ANY)] * count,
        out_specs=[pl.BlockSpec(memory_space=pl.ANY)] * count,
        scratch_shapes=[pltpu.SemaphoreType.DMA((count, pairs))] * 2,
        compiler_params=pltpu.CompilerParams(collective_id=1, has_side_effects=True),
        name="twin_exchange",
    )(*partials)


def pair_exchange(partials, pieces):
    count = len(partials)
    pairs, fs_count = lax.axis_size("dp") // CORES, lax.axis_size("fsdp")
    slots = [(pairs - 1, p) for p in partials] + [(fs_count - 1, pieces)]
    return pl.pallas_call(
        functools.partial(pair_kernel, count, pairs, fs_count),
        out_shape=[jax.ShapeDtypeStruct((n,) + p.shape[-2:], p.dtype) for n, p in slots],
        in_specs=[pl.BlockSpec(memory_space=pl.ANY)] * len(slots),
        out_specs=[pl.BlockSpec(memory_space=pl.ANY)] * len(slots),
        scratch_shapes=[
            pltpu.SemaphoreType.DMA((count, pairs - 1)),
            pltpu.SemaphoreType.DMA((count, pairs - 1)),
            pltpu.SemaphoreType.DMA((fs_count - 1,)),
            pltpu.SemaphoreType.DMA((fs_count - 1,)),
        ],
        compiler_params=pltpu.CompilerParams(collective_id=2, has_side_effects=True),
        name="pair_exchange",
    )(*partials, pieces)


def reduce_all(partials, pieces):
    dp_count = lax.axis_size("dp")
    pairs = dp_count // CORES
    dp = lax.axis_index("dp")
    core, pair = lax.rem(dp, CORES), dp // CORES
    split = [
        p.reshape(pairs, CORES, p.shape[0] // dp_count, p.shape[1])
        for p in partials
    ]
    landed = twin_exchange(split)
    chip = [
        (
            lax.dynamic_index_in_dim(p, core, axis=1, keepdims=False).astype(jnp.float32)
            + r.astype(jnp.float32)
        ).astype(p.dtype)
        for p, r in zip(split, landed)
    ]
    *others, pieces_in = pair_exchange(chip, pieces)
    own_piece = lax.dynamic_index_in_dim(pieces, lax.axis_index("fsdp"), axis=0, keepdims=False)
    tokens = own_piece.astype(jnp.float32) + jnp.sum(pieces_in.astype(jnp.float32), axis=0)
    return tokens, [
        lax.dynamic_index_in_dim(p, pair, axis=0, keepdims=False).astype(jnp.float32)
        + jnp.sum(r.astype(jnp.float32), axis=0)
        for p, r in zip(chip, others)
    ]


def split_features(
    inputs,
    gain_mixer,
    weight_in,
    conv_taps,
    weight_out,
    gain_ffn,
    weight_gate,
    weight_up,
    weight_down,
    cotangent,
):
    dp_count = lax.axis_size("dp")
    fs_count = lax.axis_size("fsdp")
    width = weight_out.shape[1]
    part = weight_out.shape[0]
    quarter = dp_count * part
    hid = dp_count * weight_down.shape[0]

    small = jnp.concatenate([gain_mixer[None], gain_ffn[None], conv_taps], axis=0)
    lanes = max(128, part)
    small = jnp.pad(small, ((0, 8 - small.shape[0]), (0, lanes - part)))
    gu_blocks = jnp.concatenate(
        [
            column_blocks(weight_gate, 1, dp_count, fs_count),
            column_blocks(weight_up, 1, dp_count, fs_count),
        ],
        axis=2,
    )
    grad_out = cotangent[0]
    x_all, grad_all, small_all, in_cols, gu_cols, out_rows, down_rows = gather_all(
        inputs[0],
        grad_out,
        small,
        column_blocks(weight_in, 3, dp_count, fs_count),
        gu_blocks,
        weight_out,
        weight_down,
    )
    x_all = x_all.reshape(-1, width)
    grad_all = grad_all.reshape(-1, width)
    in_cols = in_cols.reshape(width, 3 * quarter)
    gu_cols = gu_cols.reshape(width, 2 * hid)
    out_rows = out_rows.reshape(quarter, width)
    down_rows = down_rows.reshape(hid, width)
    small_all = small_all[:, :, : KW + 2, :part]
    gain1 = small_all[:, :, 0].reshape(width)
    gain2 = small_all[:, :, 1].reshape(width)
    taps32 = (
        lax.dynamic_index_in_dim(small_all, lax.axis_index("fsdp"), axis=1, keepdims=False)[:, 2:]
        .transpose(1, 0, 2)
        .reshape(KW, quarter)
        .astype(jnp.float32)
    )

    _, _, pre1_all = norm_forward(x_all.astype(jnp.float32), gain1)
    act1_all = pre1_all.astype(jnp.bfloat16)
    projected = product(act1_all, in_cols)
    bpart = projected[:, :quarter]
    cpart = projected[:, quarter : 2 * quarter]
    xpart = projected[:, 2 * quarter :]
    gated = bpart * xpart
    lagged_rows = [lagged(gated, offset) for offset in range(KW)]
    conv = taps32[0] * lagged_rows[0]
    for offset in range(1, KW):
        conv = conv + taps32[offset] * lagged_rows[offset]
    act2 = (cpart * conv).astype(jnp.bfloat16)
    hidden = inputs[0].astype(jnp.float32)
    normed1, scale1, _ = norm_forward(hidden, gain1)
    resid = hidden + token_share(product(act2, out_rows), 3, "share_out")
    normed2, scale2, pre2 = norm_forward(resid, gain2)
    act3_all = whole_sequence(pre2.astype(jnp.bfloat16), 4, "gather_ffn")
    gate_up = product(act3_all, gu_cols)
    gate, upval = gate_up[:, :hid], gate_up[:, hid:]
    sig = jax.nn.sigmoid(gate)
    act4 = (gate * sig * upval).astype(jnp.bfloat16)
    dact4 = product_nt(grad_all, down_rows)
    dgate = (dact4 * upval * sig * (1.0 + gate * (1.0 - sig))).astype(jnp.bfloat16)
    dupval = (dact4 * gate * sig).astype(jnp.bfloat16)
    dgu = jnp.concatenate([dgate, dupval], axis=1)
    dact3 = token_share(product_nt(dgu, gu_cols), 5, "share_ffn")
    down_pieces = token_pieces(product(act4, down_rows))
    dnorm2, g_gain2 = norm_backward(dact3, normed2, scale2, gain2)
    dresid = grad_out.astype(jnp.float32) + dnorm2
    dres_all = whole_sequence(dresid.astype(jnp.bfloat16), 6, "gather_dres")
    dact2 = product_nt(dres_all, out_rows)
    dcpart = dact2 * conv
    dconv = dact2 * cpart
    g_taps = jnp.stack(
        [jnp.sum(dconv * lagged_rows[offset], axis=0) for offset in range(KW)], axis=0
    )
    dgated = taps32[0] * dconv
    for offset in range(1, KW):
        dgated = dgated + taps32[offset] * leading(dconv, offset)
    dproj = jnp.concatenate([dgated * xpart, dcpart, dgated * bpart], axis=1).astype(jnp.bfloat16)
    dact1 = token_share_async(product_nt(dproj, in_cols))
    dnorm1, g_gain1 = norm_backward(dact1, normed1, scale1, gain1)
    grad_inputs = dresid + dnorm1

    own_column = (jnp.arange(fs_count) == lax.axis_index("fsdp"))[None, None, :, None]
    taps_spread = jnp.where(own_column, g_taps.reshape(KW, dp_count, 1, part), 0.0).reshape(KW, width)
    small_grad = jnp.concatenate([g_gain1[None], g_gain2[None], taps_spread], axis=0)
    small_grad = jnp.pad(small_grad, ((0, 8 - small_grad.shape[0]), (0, 0)))
    small_grad = small_grad.reshape(8, dp_count, fs_count, part).transpose(1, 2, 0, 3)
    small_grad = jnp.pad(small_grad, ((0, 0), (0, 0), (0, 0), (0, lanes - part)))
    down_sum, (g_small, g_gu, g_down, g_in, g_out) = reduce_all(
        [small_grad.reshape(dp_count * fs_count * 8, lanes)]
        + [
            grad.astype(jnp.bfloat16)
            for grad in (
                product_tn(act3_all, dgu),
                product_tn(act4, grad_all),
                product_tn(act1_all, dproj),
                product_tn(act2, dres_all),
            )
        ],
        down_pieces,
    )
    outputs = (resid + down_sum).astype(jnp.bfloat16)
    moved = jnp.concatenate([g_in, g_gu], axis=1).astype(jnp.bfloat16)
    moved, small_parts = along_line(
        [
            moved.reshape(fs_count, part, 3 * quarter + 2 * hid),
            g_small.reshape(fs_count, 8, lanes),
        ],
        False,
        7,
        "owner_exchange",
    )
    moved = moved.astype(jnp.float32)
    g_in_owned = moved[:, :, : 3 * quarter]
    g_gu_owned = moved[:, :, 3 * quarter :]
    small_owned = jnp.sum(small_parts, axis=0)[: KW + 2, :part]
    return (
        outputs[None],
        grad_inputs[None],
        small_owned[0],
        column_join(g_in_owned, 3, dp_count, fs_count),
        small_owned[2:],
        g_out,
        small_owned[1],
        column_join(g_gu_owned[:, :, :hid], 1, dp_count, fs_count),
        column_join(g_gu_owned[:, :, hid:], 1, dp_count, fs_count),
        g_down,
    )

HALO = 16


class Mover:
    def __init__(self, sends, recvs, locals_):
        self.sends, self.recvs, self.locals = sends, recvs, locals_
        self.count = 0
        self.local_count = 0
        self.open = []

    def push(self, src, dst, peer):
        copy = push(src, dst, self.sends, self.recvs, self.count, peer)
        self.count += 1
        self.open.append(copy)
        return copy

    def local(self, src, dst):
        copy = pltpu.make_async_copy(src, dst, self.locals.at[self.local_count])
        self.local_count += 1
        copy.start()
        return copy

    def finish(self):
        for copy in self.open:
            copy.wait_send()


class Line:
    def __init__(self, move, slot, dp, fs, fs_count):
        self.move, self.slot, self.dp, self.fs, self.size = move, slot, dp, fs, fs_count
        self.base = move.count
        move.count += CORES * fs_count

    def copy(self, source, up):
        index = self.base + CORES * source + (1 if up else 0)
        to = lax.rem(self.fs + (1 if up else self.size - 1), self.size)
        return pltpu.make_async_remote_copy(
            src_ref=self.slot(source),
            dst_ref=self.slot(source),
            send_sem=self.move.sends.at[index],
            recv_sem=self.move.recvs.at[index],
            device_id=(self.dp, to),
            device_id_type=MESH,
        )

    def start(self):
        @pl.when(self.fs < self.size - 1)
        def _():
            self.copy(self.fs, True).start()

        @pl.when(self.fs > 0)
        def _():
            self.copy(self.fs, False).start()

    def step(self, hop):
        below, above = self.fs - hop, self.fs + hop

        @pl.when(below >= 0)
        def _():
            self.copy(below, True).wait_recv()

            @pl.when(self.fs < self.size - 1)
            def _():
                self.copy(below, True).start()

        @pl.when(above < self.size)
        def _():
            self.copy(above, False).wait_recv()

            @pl.when(self.fs > 0)
            def _():
                self.copy(above, False).start()

    def finish(self):
        for hop in range(self.size):

            @pl.when((self.fs - hop >= 0) & (self.fs < self.size - 1))
            def _():
                self.copy(self.fs - hop, True).wait_send()

            @pl.when((self.fs + hop < self.size) & (self.fs > 0))
            def _():
                self.copy(self.fs + hop, False).wait_send()


class LineSum:
    def __init__(self, move, own, send, land, dp, fs, fs_count):
        self.move, self.own, self.send, self.land = move, own, send, land
        self.dp, self.fs, self.size = dp, fs, fs_count
        self.base = move.count
        move.count += CORES * fs_count

    def copy(self, dest, up, holder):
        index = self.base + CORES * dest + (1 if up else 0)
        to = lax.rem(holder + (1 if up else self.size - 1), self.size)
        slot = dest if up else jnp.where(dest == to, self.size, dest)
        return pltpu.make_async_remote_copy(
            src_ref=self.send.at[dest],
            dst_ref=self.land.at[slot],
            send_sem=self.move.sends.at[index],
            recv_sem=self.move.recvs.at[index],
            device_id=(self.dp, to),
            device_id_type=MESH,
        )

    def source(self, dest, up):
        return self.copy(dest, up, lax.rem(self.fs + (self.size - 1 if up else 1), self.size))

    def start(self):
        last = self.size - 1
        for far in range(last):

            @pl.when(self.fs == 0)
            def _():
                self.send[last - far] = self.own(last - far).astype(jnp.bfloat16)
                self.copy(last - far, True, self.fs).start()

            @pl.when(self.fs == last)
            def _():
                self.send[far] = self.own(far).astype(jnp.bfloat16)
                self.copy(far, False, self.fs).start()

    def relay(self, dest, up):
        self.source(dest, up).wait_recv()
        total = self.own(dest).astype(jnp.float32) + self.land[dest].astype(jnp.float32)
        self.send[dest] = total.astype(jnp.bfloat16)
        self.copy(dest, up, self.fs).start()

    def step(self, hop):
        last = self.size - 1
        if hop < last:

            @pl.when((self.fs >= 1) & (self.fs <= hop))
            def _():
                self.relay(self.fs + last - hop, True)

            @pl.when((self.fs < last) & (last - self.fs <= hop))
            def _():
                self.relay(self.fs + hop - last, False)

    def total(self, out):
        out[...] = self.own(self.fs).astype(jnp.float32)

        @pl.when(self.fs > 0)
        def _():
            self.source(self.fs, True).wait_recv()
            out[...] += self.land[self.fs].astype(jnp.float32)

        @pl.when(self.fs < self.size - 1)
        def _():
            self.source(self.fs, False).wait_recv()
            out[...] += self.land[self.size].astype(jnp.float32)

    def finish(self):
        for dest in range(self.size):

            @pl.when(self.fs < dest)
            def _():
                self.copy(dest, True, self.fs).wait_send()

            @pl.when(self.fs > dest)
            def _():
                self.copy(dest, False, self.fs).wait_send()


def seats(pairs, fs_count):
    dp, fs, pair, core, partner = place()
    z_peers = [(dp, lax.rem(fs + o, fs_count)) for o in range(1, fs_count)]
    p_peers = [(lax.rem(pair + o, pairs) * CORES + core, fs) for o in range(1, pairs)]
    p_from = [lax.rem(pair + pairs - o, pairs) for o in range(1, pairs)]
    return dp, fs, pair, core, partner, z_peers, p_peers, p_from


def norm_scale(hidden):
    return lax.rsqrt(jnp.mean(hidden * hidden, axis=-1, keepdims=True) + EPS)


def mixer_forward_kernel(
    pairs, fs_count,
    x_ref, cot_ref, small_ref, in_hbm, gate_hbm, up_hbm, out_ref, down_ref,
    act1_out, proj_out, act2_out, in_out_o, out_out, gains_out, taps_out, resid_out,
    act3_out, cot_out, gu_all, down_all,
    act1_o, proj_o, act2_o, in_all, out_all, gains_o, taps_o, resid_o, act3_all, cot_all,
    x_all, halo_all, small_all, in_ref, gate_ref, up_ref, in_blk, gu_blk,
    tw_out, tw_in, pr_out, pr_in, local_sem, sends, recvs,
):
    dp, fs, pair, core, partner, z_peers, p_peers, p_from = seats(pairs, fs_count)
    count = pairs * CORES
    tokens, width = x_ref.shape
    part = in_ref.shape[0]
    feat = width // count
    inner = gate_ref.shape[1] // (count * fs_count)
    hid = inner * count
    other = 1 - core
    move = Mover(sends, recvs, local_sem)
    f32 = jnp.float32

    in_local = move.local(in_hbm, in_ref)
    x_local = move.local(x_ref, x_all.at[dp])
    gate_local = move.local(gate_hbm, gate_ref)
    up_local = move.local(up_hbm, up_ref)
    out_local = move.local(out_ref, out_all.at[fs])
    cot_local = move.local(cot_ref, cot_all.at[fs])
    down_local = move.local(down_ref, down_all.at[dp])
    crossed = [(peer[0] + other - core, fs) for peer in p_peers]
    greet(z_peers + p_peers + crossed + [partner])
    small_z = [move.push(small_ref, small_all.at[dp, fs], peer) for peer in z_peers]
    halo_next = move.push(x_ref.at[pl.ds(tokens - HALO, HALO)], halo_all.at[dp, pl.ds(0, HALO)], z_peers[0])
    halo_prev = move.push(x_ref.at[pl.ds(0, HALO)], halo_all.at[dp, pl.ds(HALO, HALO)], z_peers[-1])
    in_local.wait()
    for to in range(count):
        for k in range(3):
            in_blk[to % CORES, to // CORES, :, k * feat : (k + 1) * feat] = in_ref[
                :, k * width + to * feat : k * width + (to + 1) * feat
            ]
    in_twin = move.push(in_blk.at[other, pair], in_all.at[dp, fs], partner)
    in_via = [
        move.push(in_blk.at[other, peer[0] // CORES], in_all.at[dp, fs], peer) for peer in crossed
    ]
    in_out = [move.push(in_blk.at[core, peer[0] // CORES], in_all.at[dp, fs], peer) for peer in p_peers]
    x_out = [move.push(x_ref, x_all.at[dp], peer) for peer in p_peers]
    x_twin = move.push(x_ref, x_all.at[dp], partner)
    small_all[dp, fs] = small_ref[...]
    in_all[dp, fs] = in_blk[core, pair]
    gate_local.wait()
    up_local.wait()
    for which, ref in enumerate((gate_ref, up_ref)):
        wide = ref[...].astype(f32)
        for to in range(fs_count):
            pieces = [
                wide[:, (d * fs_count + to) * inner : (d * fs_count + to + 1) * inner]
                for d in range(count)
            ]
            gu_blk[to, :, which * hid : (which + 1) * hid] = jnp.concatenate(pieces, axis=1).astype(
                jnp.bfloat16
            )
    gu_local = move.local(gu_blk.at[fs], gu_all.at[dp, fs])
    for copy in small_z:
        copy.wait_recv()
    small_out = [move.push(small_all.at[dp], small_all.at[dp], peer) for peer in p_peers]
    small_twin = [move.push(small_all.at[dp], small_all.at[dp], partner)]
    halo_next.wait_recv()
    halo_prev.wait_recv()
    halo_out = [move.push(halo_all.at[dp], halo_all.at[dp], peer) for peer in p_peers]
    halo_twin = [move.push(halo_all.at[dp], halo_all.at[dp], partner)]
    for copy in in_out + in_via + [in_twin]:
        copy.wait_recv()
    in_line = Line(move, lambda f: in_all.at[:, f], dp, fs, fs_count)
    out_line = Line(move, lambda f: out_all.at[f], dp, fs, fs_count)
    cot_line = Line(move, lambda f: cot_all.at[f], dp, fs, fs_count)
    act3_line = Line(move, lambda f: act3_all.at[f], dp, fs, fs_count)
    in_line.start()
    out_local.wait()
    out_line.start()
    down_out = [move.push(down_ref, down_all.at[dp], peer) for peer in p_peers]
    down_twin = [move.push(down_ref, down_all.at[dp], partner)]
    in_line.step(1)
    out_line.step(1)

    small_rel, x_rel = [], []
    for o, source in enumerate(p_from):
        src = source * CORES + core
        small_out[o].wait_recv()
        halo_out[o].wait_recv()
        x_out[o].wait_recv()
        small_rel.append(move.push(small_all.at[src], small_all.at[src], partner))
        x_rel.append(move.push(halo_all.at[src], halo_all.at[src], partner))
        x_rel.append(move.push(x_all.at[src], x_all.at[src], partner))
    in_line.step(2)
    out_line.step(2)
    gu_z = [move.push(gu_blk.at[peer[1]], gu_all.at[dp, fs], peer) for peer in z_peers]
    for copy in small_twin + small_rel + [x_twin] + halo_twin + x_rel:
        copy.wait_recv()
    x_local.wait()

    for d in range(count):
        total = small_all[d, 0].astype(f32)
        for f in range(1, fs_count):
            total = total + small_all[d, f].astype(f32)
        gains_o[:, d * feat : (d + 1) * feat] = total
    total = small_all[dp, 0].astype(f32)
    for f in range(1, fs_count):
        total = total + small_all[dp, f].astype(f32)
    taps_o[...] = total
    has_prev, has_next = fs > 0, fs < fs_count - 1

    def norm_step(i, carry):
        gain = gains_o[0:1, :]
        rows = x_all[i].astype(f32)
        act1_o[i, HALO : HALO + tokens] = (rows * norm_scale(rows) * gain).astype(jnp.bfloat16)
        edge = halo_all[i].astype(f32)
        edge = edge * norm_scale(edge) * gain
        act1_o[i, 0:HALO] = jnp.where(has_prev, edge[:HALO], 0.0).astype(jnp.bfloat16)
        act1_o[i, HALO + tokens :] = jnp.where(has_next, edge[HALO:], 0.0).astype(jnp.bfloat16)
        return carry

    lax.fori_loop(0, count, norm_step, 0)
    kept = [
        move.local(act1_o, act1_out), move.local(gains_o, gains_out), move.local(taps_o, taps_out)
    ]
    for hop in range(3, fs_count):
        in_line.step(hop)

    def project_step(i, carry):
        proj_o[i] = product(act1_o[i], in_all[...].reshape(width, 3 * feat))
        gated = proj_o[i, :, 0:feat] * proj_o[i, :, 2 * feat :]
        conv = taps_o[2:3, :] * gated[HALO : HALO + tokens]
        for k in range(1, KW):
            conv = conv + taps_o[2 + k : 3 + k, :] * gated[HALO - k : HALO - k + tokens]
        act2_o[i] = (proj_o[i, HALO : HALO + tokens, feat : 2 * feat] * conv).astype(jnp.bfloat16)
        return carry

    lax.fori_loop(0, count, project_step, 0)
    cot_local.wait()
    cot_line.start()
    kept += [
        move.local(proj_o, proj_out), move.local(act2_o, act2_out), move.local(in_all, in_out_o)
    ]
    for hop in range(3, fs_count):
        out_line.step(hop)
    kept.append(move.local(out_all, out_out))

    def out_partial(dest):
        return product(act2_o[dest], out_all[...].reshape(feat, width))

    order = [lax.rem(pair + o, pairs) for o in range(1, pairs)] + [pair]
    share_tw = []
    for o, j in enumerate(order):
        tw_out[o] = out_partial(j * CORES + other).astype(jnp.bfloat16)
        share_tw.append(move.push(tw_out.at[o], tw_in.at[o], partner))
    share_pr = []
    for o, j in enumerate(order):
        value = out_partial(j * CORES + core)
        share_tw[o].wait_recv()
        value = value + tw_in[o].astype(f32)
        if o < pairs - 1:
            pr_out[o] = value.astype(jnp.bfloat16)
            share_pr.append(move.push(pr_out.at[o], pr_in.at[o], p_peers[o]))
        else:
            resid_o[...] = value + x_all[dp].astype(f32)
    cot_line.step(1)
    for copy in gu_z:
        copy.wait_recv()
    gu_local.wait()
    gu_out = [move.push(gu_all.at[dp], gu_all.at[dp], peer) for peer in p_peers]
    gu_twin = [move.push(gu_all.at[dp], gu_all.at[dp], partner)]
    for copy in share_pr:
        copy.wait_recv()
    if fs_count > 2:
        cot_line.step(2)
    resid = resid_o[...]
    for o in range(pairs - 1):
        resid = resid + pr_in[o].astype(f32)
    resid_o[...] = resid
    act3_all[fs] = (resid * norm_scale(resid) * gains_o[1:2, :]).astype(jnp.bfloat16)
    act3_line.start()
    kept.append(move.local(resid_o, resid_out))
    for o, source in enumerate(p_from):
        src = source * CORES + core
        down_out[o].wait_recv()
        down_twin.append(move.push(down_all.at[src], down_all.at[src], partner))
    for hop in range(1, fs_count):
        act3_line.step(hop)
    for hop in range(3, fs_count):
        cot_line.step(hop)
    kept += [move.local(act3_all, act3_out), move.local(cot_all, cot_out)]
    for o, source in enumerate(p_from):
        src = source * CORES + core
        gu_out[o].wait_recv()
        gu_twin.append(move.push(gu_all.at[src], gu_all.at[src], partner))
    for copy in down_twin + gu_twin:
        copy.wait_recv()
    down_local.wait()
    for copy in kept:
        copy.wait()
    move.finish()
    for line in (in_line, out_line, cot_line, act3_line):
        line.finish()


def mixer_forward(x, cot, small, w_in, w_gate, w_up, w_out, w_down):
    dp_count, fs_count = lax.axis_size("dp"), lax.axis_size("fsdp")
    pairs = dp_count // CORES
    tokens, width = x.shape
    part = w_in.shape[0]
    feat = width // dp_count
    hid = w_gate.shape[1] // fs_count
    bf, f32 = jnp.bfloat16, jnp.float32
    shape = jax.ShapeDtypeStruct
    long = tokens + 2 * HALO
    in_vmem = [
        shape((dp_count, long, width), bf),
        shape((dp_count, long, 3 * feat), f32),
        shape((dp_count, tokens, feat), bf),
        shape((dp_count, fs_count, part, 3 * feat), bf),
        shape((fs_count, part, width), bf),
        shape((small.shape[0], width), f32),
        shape((small.shape[0], feat), f32),
        shape((tokens, width), f32),
    ]
    in_vmem += [shape((fs_count, tokens, width), bf)] * 2
    anywhere = [
        shape((dp_count, fs_count, part, 2 * hid), bf),
        shape((dp_count,) + w_down.shape, bf),
    ]
    slots = 20 * fs_count + 20 * pairs + 40
    return pl.pallas_call(
        functools.partial(mixer_forward_kernel, pairs, fs_count),
        out_shape=in_vmem + anywhere,
        in_specs=[
            pl.BlockSpec(memory_space=pltpu.VMEM if index == 2 else pltpu.HBM) for index in range(8)
        ],
        out_specs=[pl.BlockSpec(memory_space=pltpu.HBM)] * (len(in_vmem) + len(anywhere)),
        scratch_shapes=[pltpu.VMEM(item.shape, item.dtype) for item in in_vmem]
        + [
            pltpu.VMEM((dp_count, tokens, width), bf),
            pltpu.VMEM((dp_count, 2 * HALO, width), bf),
            pltpu.VMEM((dp_count, fs_count) + small.shape, bf),
            pltpu.VMEM(w_in.shape, bf),
            pltpu.VMEM(w_gate.shape, bf),
            pltpu.VMEM(w_up.shape, bf),
            pltpu.VMEM((CORES, pairs, part, 3 * feat), bf),
            pltpu.VMEM((fs_count, part, 2 * hid), bf),
            pltpu.VMEM((pairs, tokens, width), bf),
            pltpu.VMEM((pairs, tokens, width), bf),
            pltpu.VMEM((pairs - 1, tokens, width), bf),
            pltpu.VMEM((pairs - 1, tokens, width), bf),
            pltpu.SemaphoreType.DMA((24,)),
            pltpu.SemaphoreType.DMA((slots,)),
            pltpu.SemaphoreType.DMA((slots,)),
        ],
        compiler_params=pltpu.CompilerParams(
            collective_id=8, has_side_effects=True, vmem_limit_bytes=60 * 1024 * 1024
        ),
        name="mixer_forward",
    )(x, cot, small, w_in, w_gate, w_up, w_out, w_down)


def mixer_backward_kernel(
    pairs, fs_count,
    x_h, gains_ref, taps_ref, resid_h, act1_h, proj_h, act2_h, in_h, out_h,
    gu_h, act3_h, dgate_h, dup_h, act4_h, cot_h, down_h,
    out_o, gx_o, gin_fin, gout_o, gu_zi, gdown_o, small_o,
    x_ref, resid_ref, act1_ref, proj_ref, act2_ref, in_w, out_w,
    gu_ref, act3_ref, dgu_ref, act4_ref, cot_ref, down_ref,
    d3_own, d3_rx, dn_ref, dn_tx, dn_rx, acc, gin_acc,
    ggu_two, gd_all, gu_tw, down_tw, gu_chip, down_chip, gu_rx, down_rx, gu_zo,
    dres_all, dproj, taps_acc, gin_p, gin_tx, gin_rx, gout_p, gout_tx, gout_rx, gin_own, gin_stage,
    tw_out, tw_in, pr_out, pr_in, sm_own, sm_rx, tp_rx, sm_p, sm_tw, sm_pr,
    local_sem, sends, recvs,
):
    dp, fs, pair, core, partner, z_peers, p_peers, p_from = seats(pairs, fs_count)
    count = pairs * CORES
    tokens, width = x_ref.shape
    feat = width // count
    part = feat // fs_count
    hid = act4_ref.shape[1]
    inner = hid // count
    other = 1 - core
    twin_dp = pair * CORES + other
    move = Mover(sends, recvs, local_sem)
    f32, bf = jnp.float32, jnp.bfloat16
    order = [lax.rem(pair + o, pairs) for o in range(1, pairs)] + [pair]

    dgate_l = move.local(dgate_h, dgu_ref.at[:, pl.ds(0, hid)])
    dup_l = move.local(dup_h, dgu_ref.at[:, pl.ds(hid, hid)])
    gu_l = move.local(gu_h, gu_ref)
    greet(z_peers + p_peers + [partner])
    dgate_l.wait()
    dup_l.wait()
    gu_l.wait()
    act3_l = move.local(act3_h, act3_ref)
    act4_l = move.local(act4_h, act4_ref)
    cot_l = move.local(cot_h, cot_ref)
    down_l = move.local(down_h, down_ref)
    late = [
        move.local(src, dst)
        for src, dst in (
            (x_h, x_ref), (resid_h, resid_ref), (out_h, out_w), (proj_h, proj_ref),
            (in_h, in_w), (act1_h, act1_ref), (act2_h, act2_ref),
        )
    ]

    d3_z = []

    def d3_piece(o):
        to = (z_peers + [(dp, fs)])[o]
        at = pl.ds(pl.multiple_of(to[1] * tokens, tokens), tokens)
        d3_own[o] = product_nt(dgu_ref[at, :], gu_ref[...].reshape(width, 2 * hid)).astype(bf)
        if o < fs_count - 1:
            d3_z.append(move.push(d3_own.at[o], d3_rx.at[o], to))

    d3_piece(0)
    dn = LineSum(move, lambda f: dn_ref[f], dn_tx, dn_rx, dp, fs, fs_count)
    gin_line = LineSum(move, lambda f: gin_p[:, f], gin_tx, gin_rx, dp, fs, fs_count)
    gout_line = LineSum(move, lambda f: gout_p[f], gout_tx, gout_rx, dp, fs, fs_count)
    act3_l.wait()

    def gu_partial(dest):
        left = act3_ref[:, :, pl.ds(pl.multiple_of(dest * feat, feat), feat)]
        return product_tn(left.reshape(fs_count * tokens, feat), dgu_ref[...])

    def down_slot(dest):
        return pl.ds(pl.multiple_of(dest * inner, inner), inner)

    gu_t, gu_p = [], []

    def gu_twin(o):
        ggu_two[o] = gu_partial(order[o] * CORES + other).astype(bf)
        gu_t.append(move.push(ggu_two.at[o], gu_tw.at[o], partner))

    def gu_own(o):
        value = gu_partial(order[o] * CORES + core)
        gu_t[o].wait_recv()
        gu_chip[o] = (value + gu_tw[o].astype(f32)).astype(bf)
        if o < pairs - 1:
            gu_p.append(move.push(gu_chip.at[o], gu_rx.at[o], p_peers[o]))

    gu_twin(0)
    for o in range(max(pairs, fs_count)):
        if o + 1 < pairs:
            gu_twin(o + 1)
        if o + 1 < fs_count:
            d3_piece(o + 1)
        if o < pairs:
            gu_own(o)
    act4_l.wait()
    cot_l.wait()
    down_l.wait()
    chunk = 3 * 128 if hid % (3 * 128) == 0 else 128

    def down_step(c, carry):
        at = pl.ds(pl.multiple_of(c * chunk, chunk), chunk)
        gd_all[at, :] = product_tn(
            act4_ref[:, at], cot_ref[...].reshape(fs_count * tokens, width)
        ).astype(bf)
        return carry

    lax.fori_loop(0, hid // chunk, down_step, 0)
    down_t = [
        move.push(gd_all.at[down_slot(j * CORES + other)], down_tw.at[o], partner)
        for o, j in enumerate(order)
    ]

    def dn_step(f, carry):
        at = pl.ds(pl.multiple_of(f * tokens, tokens), tokens)
        dn_ref[f] = product(act4_ref[at, :], down_ref[...].reshape(hid, width)).astype(bf)
        return carry

    lax.fori_loop(0, fs_count, dn_step, 0)
    for copy in late:
        copy.wait()

    for copy in d3_z:
        copy.wait_recv()
    dact3 = d3_own[fs_count - 1].astype(f32)
    for o in range(fs_count - 1):
        dact3 = dact3 + d3_rx[o].astype(f32)
    resid = resid_ref[...]
    scale2 = norm_scale(resid)
    normed2 = resid * scale2
    sm_own[1:2, :] = jnp.sum(dact3 * normed2, axis=0, keepdims=True)
    dnormed = dact3 * gains_ref[1:2, :]
    dresid = cot_ref[fs].astype(f32) + scale2 * (
        dnormed - normed2 * jnp.mean(dnormed * normed2, axis=-1, keepdims=True)
    )
    gx_o[...] = dresid
    dres_all[dp, 0:tokens] = dresid.astype(bf)
    mine = dres_all.at[dp, pl.ds(0, tokens)]
    edge = dres_all.at[dp, pl.ds(tokens, HALO)]
    halo_z = move.push(dres_all.at[dp, pl.ds(0, HALO)], edge, z_peers[-1])
    dres_out = [move.push(mine, mine, peer) for peer in p_peers]
    dres_twin = [move.push(mine, mine, partner)]
    dn.start()
    down_p = []
    for o, j in enumerate(order):
        down_t[o].wait_recv()
        down_chip[o] = (
            gd_all[down_slot(j * CORES + core), :].astype(f32) + down_tw[o].astype(f32)
        ).astype(bf)
    halo_z.wait_recv()
    edge_out = [move.push(edge, edge, peer) for peer in p_peers]
    dres_twin.append(move.push(edge, edge, partner))
    for o, source in enumerate(p_from):
        src = source * CORES + core
        dres_out[o].wait_recv()
        edge_out[o].wait_recv()
        dres_twin.append(move.push(dres_all.at[src], dres_all.at[src], partner))
    for o, peer in enumerate(p_peers):
        down_p.append(move.push(down_chip.at[o], down_rx.at[o], peer))
    dn.step(1)
    for copy in dres_twin:
        copy.wait_recv()

    taps_acc[...] = jnp.zeros(taps_acc.shape, f32)

    def mixer_step(i, carry):
        dact2 = product_nt(dres_all[i], out_w[...].reshape(feat, width))
        bpart = proj_ref[i, :, 0:feat]
        cpart = proj_ref[i, :, feat : 2 * feat]
        xpart = proj_ref[i, :, 2 * feat :]
        gated = bpart * xpart
        conv = taps_ref[2:3, :] * gated[HALO : HALO + tokens]
        for k in range(1, KW):
            conv = conv + taps_ref[2 + k : 3 + k, :] * gated[HALO - k : HALO - k + tokens]
        dconv = dact2 * cpart[HALO:]
        dcpart = dact2[:tokens] * conv
        dgated = taps_ref[2:3, :] * dconv[:tokens]
        for k in range(1, KW):
            dgated = dgated + taps_ref[2 + k : 3 + k, :] * dconv[k : k + tokens]
        for k in range(KW):
            taps_acc[k : k + 1, :] += jnp.sum(
                dconv[:tokens] * gated[HALO - k : HALO - k + tokens], axis=0, keepdims=True
            )
        dproj[i, :, 0:feat] = (dgated * xpart[HALO : HALO + tokens]).astype(bf)
        dproj[i, :, feat : 2 * feat] = dcpart.astype(bf)
        dproj[i, :, 2 * feat :] = (dgated * bpart[HALO : HALO + tokens]).astype(bf)
        return carry

    lax.fori_loop(0, count, mixer_step, 0)

    sm_own[0:1, :] = jnp.zeros((1, width), f32)
    sm_own[2:, :] = jnp.zeros((sm_own.shape[0] - 2, width), f32)

    def in_partial(dest):
        value = product_nt(dproj[dest], in_w[...].reshape(width, 3 * feat))
        left = act1_ref[dest, pl.ds(HALO, tokens), :].astype(f32)
        sm_own[0:1, :] += jnp.sum(value * left, axis=0, keepdims=True)
        return value

    def gin_step(c, carry):
        left = act1_ref[:, pl.ds(HALO, tokens), pl.ds(pl.multiple_of(c * feat, feat), feat)]
        grad = product_tn(
            left.reshape(count * tokens, feat), dproj[...].reshape(count * tokens, 3 * feat)
        )
        gin_p[c] = grad.astype(bf).reshape(fs_count, part, 3 * feat)
        return carry

    for copy in gu_p:
        copy.wait_recv()
    total = gu_chip[pairs - 1].astype(f32)
    for o in range(pairs - 1):
        total = total + gu_rx[o].astype(f32)
    gu_zo[...] = total.astype(bf).reshape(fs_count, part, 2 * hid)
    gu_z = [move.push(gu_zo.at[peer[1]], gu_zi.at[fs], peer) for peer in z_peers]
    gu_zi[fs] = gu_zo[fs]

    lax.fori_loop(0, count, gin_step, 0)
    dn.step(2)
    gin_line.start()

    share_tw = []
    for o, j in enumerate(order):
        tw_out[o] = in_partial(j * CORES + other).astype(bf)
        share_tw.append(move.push(tw_out.at[o], tw_in.at[o], partner))

    gin_line.step(1)
    share_pr = []
    dact1 = None
    for o, j in enumerate(order):
        value = in_partial(j * CORES + core)
        share_tw[o].wait_recv()
        value = value + tw_in[o].astype(f32)
        if o < pairs - 1:
            pr_out[o] = value.astype(bf)
            share_pr.append(move.push(pr_out.at[o], pr_in.at[o], p_peers[o]))
        else:
            dact1 = value
    sm_own[0:1, :] = sm_own[0:1, :] / gains_ref[0:1, :]
    sm_z = [move.push(sm_own, sm_rx.at[o], peer) for o, peer in enumerate(z_peers)]
    taps_z = [move.push(taps_acc, tp_rx.at[o], peer) for o, peer in enumerate(z_peers)]
    gin_line.step(2)
    grad = product_tn(
        act2_ref[...].reshape(count * tokens, feat),
        dres_all[:, 0:tokens].reshape(count * tokens, width),
    )
    gout_p[...] = grad.astype(bf).reshape(fs_count, part, width)
    gout_line.start()
    for hop in range(3, fs_count):
        dn.step(hop)

    gout_line.step(1)
    for hop in range(3, fs_count):
        gin_line.step(hop)
    gin_line.total(gin_acc)
    for d in range(count):
        gin_own[d % CORES, d // CORES] = gin_acc[d].astype(bf)
    gin_t = move.push(gin_own.at[other], gin_stage, partner)
    gin_out = [
        move.push(gin_own.at[core, peer[0] // CORES], gin_fin.at[dp], peer) for peer in p_peers
    ]
    gin_fin[dp] = gin_own[core, pair]
    for copy in sm_z:
        copy.wait_recv()
    small_sum = sm_own[...]
    for o in range(fs_count - 1):
        small_sum = small_sum + sm_rx[o]
    for d in range(count):
        sm_p[d % CORES, d // CORES] = small_sum[:, d * feat : (d + 1) * feat]
    sm_t = move.push(sm_p.at[other], sm_tw, partner)
    gin_t.wait_recv()
    gin_via = [
        move.push(gin_stage.at[peer[0] // CORES], gin_fin.at[twin_dp], peer) for peer in p_peers
    ]
    gin_fin[twin_dp] = gin_stage[pair]


    for hop in range(2, fs_count):
        gout_line.step(hop)
    for copy in share_pr:
        copy.wait_recv()
    for o in range(pairs - 1):
        dact1 = dact1 + pr_in[o].astype(f32)
    hidden = x_ref[...].astype(f32)
    scale1 = norm_scale(hidden)
    normed1 = hidden * scale1
    dnormed = dact1 * gains_ref[0:1, :]
    gx_o[...] += scale1 * (dnormed - normed1 * jnp.mean(dnormed * normed1, axis=-1, keepdims=True))

    sm_t.wait_recv()
    for j in range(pairs):
        sm_tw[j] = sm_tw[j] + sm_p[core, j]
    sm_pair = [
        move.push(sm_tw.at[peer[0] // CORES], sm_pr.at[o], peer) for o, peer in enumerate(p_peers)
    ]
    for copy in down_p:
        copy.wait_recv()
    total = down_chip[pairs - 1].astype(f32)
    for o in range(pairs - 1):
        total = total + down_rx[o].astype(f32)
    gdown_o[...] = total
    dn.total(acc)
    out_o[...] = (resid_ref[...] + acc[...]).astype(bf)
    for copy in taps_z:
        copy.wait_recv()
    gout_line.total(gout_o)
    for copy in gu_z:
        copy.wait_recv()
    for copy in gin_out + gin_via:
        copy.wait_recv()
    for copy in sm_pair:
        copy.wait_recv()
    total = sm_tw[pair]
    for o in range(pairs - 1):
        total = total + sm_pr[o]
    taps = taps_acc[...]
    for o in range(fs_count - 1):
        taps = taps + tp_rx[o]
    small_o[0] = total
    small_o[1] = taps
    move.finish()
    for line in (dn, gin_line, gout_line):
        line.finish()


def mixer_backward(x, gains, taps, resid, act1, proj, act2, in_w, out_w, gu, act3, dgate, dup, act4, cot, down):
    dp_count, fs_count = lax.axis_size("dp"), lax.axis_size("fsdp")
    pairs = dp_count // CORES
    tokens, width = x.shape
    feat = width // dp_count
    part = feat // fs_count
    hid2 = 2 * dgate.shape[1]
    dgu = jax.ShapeDtypeStruct((dgate.shape[0], hid2), dgate.dtype)
    rows_down = down.shape[1]
    bf, f32 = jnp.bfloat16, jnp.float32
    shape = jax.ShapeDtypeStruct
    outs = [
        shape((tokens, width), bf),
        shape((tokens, width), f32),
        shape((dp_count, part, 3 * feat), bf),
        shape((part, width), f32),
        shape((fs_count, part, hid2), bf),
        shape((rows_down, width), f32),
        shape((2, 8, feat), f32),
    ]
    slots = 24 * fs_count + 20 * pairs + 40
    loaded = (x, resid, act1, proj, act2, in_w, out_w, gu, act3, dgu, act4, cot, down)
    scratch = [(item.shape, item.dtype) for item in loaded] + [
        ((fs_count, tokens, width), bf),
        ((fs_count - 1, tokens, width), bf),
        ((fs_count, tokens, width), bf),
        ((fs_count, tokens, width), bf),
        ((fs_count + 1, tokens, width), bf),
        ((tokens, width), f32),
        ((dp_count, part, 3 * feat), f32),
        ((pairs, feat, hid2), bf),
        ((hid2 // 2, width), bf),
        ((pairs, feat, hid2), bf),
        ((pairs, rows_down, width), bf),
        ((pairs, feat, hid2), bf),
        ((pairs, rows_down, width), bf),
        ((pairs - 1, feat, hid2), bf),
        ((pairs - 1, rows_down, width), bf),
        ((fs_count, part, hid2), bf),
        ((dp_count, tokens + HALO, width), bf),
        ((dp_count, tokens, 3 * feat), bf),
        ((8, feat), f32),
        ((dp_count, fs_count, part, 3 * feat), bf),
        ((fs_count, dp_count, part, 3 * feat), bf),
        ((fs_count + 1, dp_count, part, 3 * feat), bf),
        ((fs_count, part, width), bf),
        ((fs_count, part, width), bf),
        ((fs_count + 1, part, width), bf),
        ((CORES, pairs, part, 3 * feat), bf),
        ((pairs, part, 3 * feat), bf),
        ((pairs, tokens, width), bf),
        ((pairs, tokens, width), bf),
        ((pairs - 1, tokens, width), bf),
        ((pairs - 1, tokens, width), bf),
        ((8, width), f32),
        ((fs_count - 1, 8, width), f32),
        ((fs_count - 1, 8, feat), f32),
        ((CORES, pairs, 8, feat), f32),
        ((pairs, 8, feat), f32),
        ((pairs - 1, 8, feat), f32),
    ]
    return pl.pallas_call(
        functools.partial(mixer_backward_kernel, pairs, fs_count),
        out_shape=outs,
        in_specs=[
            pl.BlockSpec(memory_space=pltpu.VMEM if index in (1, 2) else pltpu.HBM)
            for index in range(16)
        ],
        out_specs=[pl.BlockSpec(memory_space=pltpu.VMEM)] * len(outs),
        scratch_shapes=[pltpu.VMEM(s, d) for s, d in scratch]
        + [pltpu.SemaphoreType.DMA((n,)) for n in (len(loaded) + 1, slots, slots)],
        compiler_params=pltpu.CompilerParams(
            collective_id=9, has_side_effects=True, vmem_limit_bytes=60 * 1024 * 1024
        ),
        name="mixer_backward",
    )(x, gains, taps, resid, act1, proj, act2, in_w, out_w, gu, act3, dgate, dup, act4, cot, down)


def finish_kernel(
    fs_count, count,
    out_i, gx_i, gin_h, gout_i, gu_h, gdown_i, small_i,
    out_o, gx_o, gin_o, gout_o, ggate_o, gup_o, gdown_o, gain1_o, gain2_o, taps_o,
    gin_fin, gu_zi, gin_v, gate_v, up_v, out_v, gx_v, gout_v, gdown_v, sems,
):
    part, feat = gout_i.shape[0], gin_fin.shape[2] // 3
    width, hid = gout_i.shape[1], gu_zi.shape[2] // 2
    inner = hid // count
    f32 = jnp.float32
    copies = []

    def send(src, dst):
        copy = pltpu.make_async_copy(src, dst, sems.at[len(copies)])
        copy.start()
        copies.append(copy)

    send(gin_h, gin_fin)
    send(gu_h, gu_zi)
    through = ((gx_i, gx_v, gx_o), (gdown_i, gdown_v, gdown_o), (out_i, out_v, out_o), (gout_i, gout_v, gout_o))
    for src, held, dst in through:
        send(src, held)
    gin_in, gu_in, *held_in = copies
    gin_count = len(copies)
    for copy, (src, held, dst) in zip(held_in, through):
        copy.wait()
        send(held, dst)
    gin_in.wait()
    for d in range(count):
        for k in range(3):
            gin_v[:, k * width + d * feat : k * width + (d + 1) * feat] = gin_fin[
                d, :, k * feat : (k + 1) * feat
            ].astype(f32)
    send(gin_v, gin_o)
    gu_in.wait()
    for which, (ref, dst) in enumerate(((gate_v, ggate_o), (up_v, gup_o))):
        wide = [gu_zi[f, :, which * hid : (which + 1) * hid].astype(f32) for f in range(fs_count)]
        pieces = [
            wide[f][:, d * inner : (d + 1) * inner] for d in range(count) for f in range(fs_count)
        ]
        ref[...] = jnp.concatenate(pieces, axis=1)
        send(ref, dst)
    fs = lax.axis_index("fsdp")
    small = small_i[...]
    mine = small[:, :, 0:part]
    for f in range(1, fs_count):
        mine = jnp.where(fs == f, small[:, :, f * part : (f + 1) * part], mine)
    gain1_o[...] = mine[0, 0:1]
    gain2_o[...] = mine[0, 1:2]
    taps_o[...] = mine[1, 0:KW]
    for copy in copies[gin_count:]:
        copy.wait()


def finish(out, gx, gin, gout, gu, gdown, small, wide_in, wide_ff):
    dp_count, fs_count = lax.axis_size("dp"), lax.axis_size("fsdp")
    part = gout.shape[0]
    f32 = jnp.float32
    shape = jax.ShapeDtypeStruct
    outs = [
        shape(out.shape, out.dtype),
        shape(gx.shape, f32),
        shape((part, wide_in), f32),
        shape(gout.shape, f32),
        shape((part, wide_ff), f32),
        shape((part, wide_ff), f32),
        shape(gdown.shape, f32),
        shape((1, part), f32),
        shape((1, part), f32),
        shape((KW, part), f32),
    ]
    return pl.pallas_call(
        functools.partial(finish_kernel, fs_count, dp_count),
        out_shape=outs,
        in_specs=[pl.BlockSpec(memory_space=pltpu.HBM)] * 6
        + [pl.BlockSpec(memory_space=pltpu.VMEM)],
        out_specs=[pl.BlockSpec(memory_space=pltpu.HBM)] * 7
        + [pl.BlockSpec(memory_space=pltpu.VMEM)] * 3,
        scratch_shapes=[
            pltpu.VMEM(gin.shape, gin.dtype),
            pltpu.VMEM(gu.shape, gu.dtype),
            pltpu.VMEM((part, wide_in), f32),
            pltpu.VMEM((part, wide_ff), f32),
            pltpu.VMEM((part, wide_ff), f32),
            pltpu.VMEM(out.shape, out.dtype),
            pltpu.VMEM(gx.shape, f32),
            pltpu.VMEM(gout.shape, f32),
            pltpu.VMEM(gdown.shape, f32),
            pltpu.SemaphoreType.DMA((13,)),
        ],
        compiler_params=pltpu.CompilerParams(vmem_limit_bytes=60 * 1024 * 1024),
        name="finish",
    )(out, gx, gin, gout, gu, gdown, small)


def split_tokens(
    inputs,
    gain_mixer,
    weight_in,
    conv_taps,
    weight_out,
    gain_ffn,
    weight_gate,
    weight_up,
    weight_down,
    cotangent,
):
    dp_count, fs_count = lax.axis_size("dp"), lax.axis_size("fsdp")
    fs = lax.axis_index("fsdp")
    tokens, width = inputs.shape[1:]
    part = weight_out.shape[0]
    hid = weight_gate.shape[1] // fs_count
    bf = jnp.bfloat16
    x, cot = inputs[0], cotangent[0]
    small = jnp.concatenate([gain_mixer[None], gain_ffn[None], conv_taps], axis=0)
    small = jnp.tile(jnp.pad(small, ((0, 16 - small.shape[0]), (0, 0))), (1, fs_count))
    lanes = lax.broadcasted_iota(jnp.int32, small.shape, 1)
    mine = (lanes >= fs * part) & (lanes < (fs + 1) * part)
    small = jnp.where(mine, small, jnp.zeros_like(small))
    (act1, proj, act2, in_w, out_w, gains, taps, resid, act3_all, cot_all, gu_all, down_rows) = mixer_forward(
        x, cot, small, weight_in, weight_gate, weight_up, weight_out, weight_down
    )
    gu_cols = gu_all.reshape(width, 2 * hid)
    gate_up = product(act3_all.reshape(-1, width), gu_cols)
    gate, upval = gate_up[:, :hid], gate_up[:, hid:]
    sig = jax.nn.sigmoid(gate)
    act4 = (gate * sig * upval).astype(bf)
    dact4 = product_nt(cot_all.reshape(-1, width), down_rows.reshape(hid, width))
    dgate = (dact4 * upval * sig * (1.0 + gate * (1.0 - sig))).astype(bf)
    dupval = (dact4 * gate * sig).astype(bf)
    parts = mixer_backward(
        x, gains, taps, resid, act1, proj, act2, in_w, out_w, gu_all, act3_all, dgate, dupval, act4, cot_all, down_rows
    )
    outputs, gx, gin, gout, ggate, gup, gdown, gain1, gain2, g_taps = finish(
        *parts, weight_in.shape[1], weight_gate.shape[1]
    )
    return (
        outputs[None], gx[None], gain1[0], gin, g_taps, gout, gain2[0], ggate, gup, gdown,
    )


def fits_tokens(inputs, weight_out, weight_gate):
    dp_count, fs_count = lax.axis_size("dp"), lax.axis_size("fsdp")
    tokens, width = inputs.shape[1:]
    return (
        dp_count % CORES == 0
        and dp_count > CORES
        and fs_count > 1
        and (width // dp_count) % 128 == 0
        and (weight_gate.shape[1] // fs_count) % 128 == 0
        and weight_out.shape[0] % 16 == 0
        and tokens % 16 == 0
        and inputs.shape[0] == 1
    )


def on_device(
    inputs,
    gain_mixer,
    weight_in,
    conv_taps,
    weight_out,
    gain_ffn,
    weight_gate,
    weight_up,
    weight_down,
    cotangent,
):
    form = split_tokens if fits_tokens(inputs, weight_out, weight_gate) else split_features
    return form(
        inputs,
        gain_mixer,
        weight_in,
        conv_taps,
        weight_out,
        gain_ffn,
        weight_gate,
        weight_up,
        weight_down,
        cotangent,
    )


def solution(mesh):
    in_specs = (
        P("dp", "fsdp", None),
        P(("dp", "fsdp")),
        P(("dp", "fsdp"), None),
        P(None, ("dp", "fsdp")),
        P(("dp", "fsdp"), None),
        P(("dp", "fsdp")),
        P(("dp", "fsdp"), None),
        P(("dp", "fsdp"), None),
        P(("dp", "fsdp"), None),
        P("dp", "fsdp", None),
    )
    out_specs = (
        P("dp", "fsdp", None),
        P("dp", "fsdp", None),
        P(("dp", "fsdp")),
        P(("dp", "fsdp"), None),
        P(None, ("dp", "fsdp")),
        P(("dp", "fsdp"), None),
        P(("dp", "fsdp")),
        P(("dp", "fsdp"), None),
        P(("dp", "fsdp"), None),
        P(("dp", "fsdp"), None),
    )
    return jax.shard_map(
        on_device, mesh=mesh, in_specs=in_specs, out_specs=out_specs, check_vma=False
    )
```

```python
import functools

import jax
import jax.numpy as jnp
from jax import lax
from jax.experimental import pallas as pl
from jax.experimental.pallas import tpu as pltpu
from jax.sharding import PartitionSpec as P

KW = 3


EPS = 1e-05

CORES = 2
MESH = pl.DeviceIdType.MESH


def product(left, right):
    return jnp.dot(left, right, preferred_element_type=jnp.float32)


def product_tn(left, right):
    return lax.dot_general(
        left, right, (((0,), (0,)), ((), ())), preferred_element_type=jnp.float32
    )


def product_nt(left, right):
    return lax.dot_general(
        left, right, (((1,), (1,)), ((), ())), preferred_element_type=jnp.float32
    )


def norm_forward(hidden, gain):
    scale = lax.rsqrt(jnp.mean(hidden * hidden, axis=-1, keepdims=True) + EPS)
    normed = hidden * scale
    return (normed, scale, normed * gain.astype(jnp.float32))


def norm_backward(dact, normed, scale, gain):
    dnormed = dact * gain.astype(jnp.float32)
    dhidden = scale * (dnormed - normed * jnp.mean(dnormed * normed, axis=-1, keepdims=True))
    return (dhidden, jnp.sum(dact * normed, axis=0))


def lagged(values, offset):
    zeros = jnp.zeros((offset, values.shape[1]), values.dtype)
    return jnp.concatenate([zeros, values[: values.shape[0] - offset]], axis=0)


def leading(values, offset):
    zeros = jnp.zeros((offset, values.shape[1]), values.dtype)
    return jnp.concatenate([values[offset:], zeros], axis=0)


def column_blocks(shard, lead, dp_count, fs_count):
    rows, columns = shard.shape
    inner = columns // (lead * dp_count * fs_count)
    pieces = shard.reshape(rows, lead, dp_count, fs_count, inner).transpose(3, 0, 1, 2, 4)
    return pieces.reshape(fs_count, rows, lead * dp_count * inner)


def column_join(blocks, lead, dp_count, fs_count):
    _, rows, columns = blocks.shape
    inner = columns // (lead * dp_count)
    pieces = blocks.reshape(fs_count, rows, lead, dp_count, inner).transpose(1, 2, 3, 0, 4)
    return pieces.reshape(rows, lead * dp_count * fs_count * inner)


def greet(peers):
    barrier = pltpu.get_barrier_semaphore()
    for peer in peers:
        pl.semaphore_signal(barrier, inc=1, device_id=peer, device_id_type=MESH)
    pl.semaphore_wait(barrier, len(peers))


def push(src, dst, sends, recvs, index, peer):
    copy = pltpu.make_async_remote_copy(
        src_ref=src,
        dst_ref=dst,
        send_sem=sends.at[index],
        recv_sem=recvs.at[index],
        device_id=peer,
        device_id_type=MESH,
    )
    copy.start()
    return copy


def place():
    dp, fs = lax.axis_index("dp"), lax.axis_index("fsdp")
    pair, core = dp // CORES, lax.rem(dp, CORES)
    return dp, fs, pair, core, (pair * CORES + 1 - core, fs)


def gather_kernel(
    pairs, fs_count,
    x_ref, cot_ref, small_ref, in_ref, gu_ref, out_ref, down_ref,
    x_all, cot_all, small_all, in_all, gu_all, out_all, down_all,
    local_sem, z_send, z_recv, p_send, p_recv, c_send, c_recv,
):
    dp, fs, pair, core, partner = place()
    z_peers = [(dp, lax.rem(fs + o, fs_count)) for o in range(1, fs_count)]
    p_peers = [(lax.rem(pair + o, pairs) * CORES + core, fs) for o in range(1, pairs)]
    p_from = [lax.rem(pair + pairs - o, pairs) * CORES + core for o in range(1, pairs)]
    greet(z_peers + p_peers + [partner])
    spread = [small_all, in_all, gu_all, out_all, down_all]

    across = [[None] * len(p_peers) for _ in spread]
    twins = [[None] * pairs for _ in spread]

    def spread_own(kind, src):
        dst = spread[kind].at[dp]
        for o, peer in enumerate(p_peers):
            across[kind][o] = push(src, dst, p_send, p_recv, (kind, o), peer)
        twins[kind][0] = push(src, dst, c_send, c_recv, (kind, 0), partner)

    along = [[], [], [], [], []]
    for o, peer in enumerate(z_peers):
        to = peer[1]
        along[0].append(push(small_ref, small_all.at[dp, fs], z_send, z_recv, (0, o), peer))
        along[1].append(push(in_ref.at[to], in_all.at[dp, fs], z_send, z_recv, (1, o), peer))
    for o, peer in enumerate(z_peers):
        to = peer[1]
        along[2].append(push(gu_ref.at[to], gu_all.at[dp, fs], z_send, z_recv, (2, o), peer))
    for o, peer in enumerate(z_peers):
        along[3].append(push(x_ref, x_all.at[fs], z_send, z_recv, (3, o), peer))
    for o, peer in enumerate(z_peers):
        along[4].append(push(cot_ref, cot_all.at[fs], z_send, z_recv, (4, o), peer))
    spread_own(3, out_ref)
    spread_own(4, down_ref)
    local = []
    for index, (src, dst) in enumerate(
        [
            (small_ref, small_all.at[dp, fs]),
            (in_ref.at[fs], in_all.at[dp, fs]),
            (gu_ref.at[fs], gu_all.at[dp, fs]),
            (x_ref, x_all.at[fs]),
            (cot_ref, cot_all.at[fs]),
            (out_ref, out_all.at[dp]),
            (down_ref, down_all.at[dp]),
        ]
    ):
        copy = pltpu.make_async_copy(src, dst, local_sem.at[index])
        copy.start()
        local.append(copy)
    for kind in range(3):
        local[kind].wait()
        for copy in along[kind]:
            copy.wait_recv()
        spread_own(kind, spread[kind].at[dp])
    for kind in (3, 0, 1, 4, 2):
        for o, source in enumerate(p_from):
            across[kind][o].wait_recv()
            block = spread[kind].at[source]
            twins[kind][o + 1] = push(block, block, c_send, c_recv, (kind, o + 1), partner)
    for copy in local[3:]:
        copy.wait()
    for copy in along[3] + along[4]:
        copy.wait_recv()
    for row in along + across:
        for copy in row:
            copy.wait_send()
    for row in twins:
        for copy in row:
            copy.wait()


def gather_all(x, cot, small, in_blocks, gu_blocks, out_shard, down_shard):
    dp_count, fs_count = lax.axis_size("dp"), lax.axis_size("fsdp")
    pairs = dp_count // CORES
    arrays = (x, cot, small, in_blocks, gu_blocks, out_shard, down_shard)
    shapes = (
        (fs_count,) + x.shape,
        (fs_count,) + cot.shape,
        (dp_count, fs_count) + small.shape,
        (dp_count,) + in_blocks.shape,
        (dp_count,) + gu_blocks.shape,
        (dp_count,) + out_shard.shape,
        (dp_count,) + down_shard.shape,
    )
    return pl.pallas_call(
        functools.partial(gather_kernel, pairs, fs_count),
        out_shape=[jax.ShapeDtypeStruct(shape, x.dtype) for shape in shapes],
        in_specs=[pl.BlockSpec(memory_space=pltpu.VMEM)] * len(arrays),
        out_specs=[pl.BlockSpec(memory_space=pl.ANY)] * len(shapes),
        scratch_shapes=[
            pltpu.SemaphoreType.DMA((7,)),
            pltpu.SemaphoreType.DMA((5, fs_count - 1)),
            pltpu.SemaphoreType.DMA((5, fs_count - 1)),
            pltpu.SemaphoreType.DMA((5, pairs - 1)),
            pltpu.SemaphoreType.DMA((5, pairs - 1)),
            pltpu.SemaphoreType.DMA((5, pairs)),
            pltpu.SemaphoreType.DMA((5, pairs)),
        ],
        compiler_params=pltpu.CompilerParams(collective_id=0, has_side_effects=True),
        name="gather_all",
    )(*arrays)


def line_kernel(count, fs_count, whole, *refs):
    sources, landed = refs[:count], refs[count : 2 * count]
    local_sem, sends, recvs = refs[2 * count :]
    dp, fs, _, _, _ = place()
    targets = [lax.rem(fs + o, fs_count) for o in range(1, fs_count)]
    greet([(dp, to) for to in targets])
    copies = [
        push(src if whole else src.at[to], dst.at[fs], sends, recvs, (k, o), (dp, to))
        for k, (src, dst) in enumerate(zip(sources, landed))
        for o, to in enumerate(targets)
    ]
    local = []
    for k, (src, dst) in enumerate(zip(sources, landed)):
        copy = pltpu.make_async_copy(src if whole else src.at[fs], dst.at[fs], local_sem.at[k])
        copy.start()
        local.append(copy)
    for copy in local + copies:
        copy.wait()


def along_line(arrays, whole, collective_id, name):
    fs_count = lax.axis_size("fsdp")
    count = len(arrays)
    return pl.pallas_call(
        functools.partial(line_kernel, count, fs_count, whole),
        out_shape=[
            jax.ShapeDtypeStruct(((fs_count,) + a.shape) if whole else a.shape, a.dtype)
            for a in arrays
        ],
        in_specs=[pl.BlockSpec(memory_space=pltpu.VMEM)] * count,
        out_specs=[pl.BlockSpec(memory_space=pl.ANY)] * count,
        scratch_shapes=[
            pltpu.SemaphoreType.DMA((count,)),
            pltpu.SemaphoreType.DMA((count, fs_count - 1)),
            pltpu.SemaphoreType.DMA((count, fs_count - 1)),
        ],
        compiler_params=pltpu.CompilerParams(collective_id=collective_id, has_side_effects=True),
        name=name,
    )(*arrays)


def whole_sequence(rows, collective_id, name):
    (received,) = along_line([rows], True, collective_id, name)
    return received.reshape(-1, rows.shape[1])


def token_pieces(partial_value):
    fs_count = lax.axis_size("fsdp")
    rows, columns = partial_value.shape
    return partial_value.astype(jnp.bfloat16).reshape(fs_count, rows // fs_count, columns)


def token_share(partial_value, collective_id, name):
    (received,) = along_line([token_pieces(partial_value)], False, collective_id, name)
    return jnp.sum(received.astype(jnp.float32), axis=0)


def token_share_async(partial_value):
    received = lax.all_to_all(
        token_pieces(partial_value), "fsdp", split_axis=0, concat_axis=0, tiled=True
    )
    return jnp.sum(received.astype(jnp.float32), axis=0)


def twin_kernel(count, pairs, *refs):
    partials, received = refs[:count], refs[count : 2 * count]
    sends, recvs = refs[2 * count :]
    _, _, _, core, partner = place()
    greet([partner])
    copies = [
        push(partial.at[j, 1 - core], landed.at[j], sends, recvs, (k, j), partner)
        for k, (partial, landed) in enumerate(zip(partials, received))
        for j in range(pairs)
    ]
    for copy in copies:
        copy.wait()


def pair_kernel(count, pairs, fs_count, *refs):
    partials, pieces = refs[:count], refs[count]
    received, pieces_in = refs[count + 1 : 2 * count + 1], refs[2 * count + 1]
    sends, recvs, z_sends, z_recvs = refs[2 * count + 2 :]
    dp, fs, pair, core, _ = place()
    targets = [lax.rem(pair + o, pairs) for o in range(1, pairs)]
    peers = [(to * CORES + core, fs) for to in targets]
    z_targets = [lax.rem(fs + o, fs_count) for o in range(1, fs_count)]
    greet(peers + [(dp, to) for to in z_targets])
    copies = [
        push(partial.at[to], landed.at[o], sends, recvs, (k, o), peer)
        for k, (partial, landed) in enumerate(zip(partials, received))
        for o, (to, peer) in enumerate(zip(targets, peers))
    ]
    copies += [
        push(pieces.at[to], pieces_in.at[o], z_sends, z_recvs, o, (dp, to))
        for o, to in enumerate(z_targets)
    ]
    for copy in copies:
        copy.wait()


def twin_exchange(partials):
    count = len(partials)
    pairs = lax.axis_size("dp") // CORES
    return pl.pallas_call(
        functools.partial(twin_kernel, count, pairs),
        out_shape=[jax.ShapeDtypeStruct((pairs,) + p.shape[-2:], p.dtype) for p in partials],
        in_specs=[pl.BlockSpec(memory_space=pl.ANY)] * count,
        out_specs=[pl.BlockSpec(memory_space=pl.ANY)] * count,
        scratch_shapes=[pltpu.SemaphoreType.DMA((count, pairs))] * 2,
        compiler_params=pltpu.CompilerParams(collective_id=1, has_side_effects=True),
        name="twin_exchange",
    )(*partials)


def pair_exchange(partials, pieces):
    count = len(partials)
    pairs, fs_count = lax.axis_size("dp") // CORES, lax.axis_size("fsdp")
    slots = [(pairs - 1, p) for p in partials] + [(fs_count - 1, pieces)]
    return pl.pallas_call(
        functools.partial(pair_kernel, count, pairs, fs_count),
        out_shape=[jax.ShapeDtypeStruct((n,) + p.shape[-2:], p.dtype) for n, p in slots],
        in_specs=[pl.BlockSpec(memory_space=pl.ANY)] * len(slots),
        out_specs=[pl.BlockSpec(memory_space=pl.ANY)] * len(slots),
        scratch_shapes=[
            pltpu.SemaphoreType.DMA((count, pairs - 1)),
            pltpu.SemaphoreType.DMA((count, pairs - 1)),
            pltpu.SemaphoreType.DMA((fs_count - 1,)),
            pltpu.SemaphoreType.DMA((fs_count - 1,)),
        ],
        compiler_params=pltpu.CompilerParams(collective_id=2, has_side_effects=True),
        name="pair_exchange",
    )(*partials, pieces)


def reduce_all(partials, pieces):
    dp_count = lax.axis_size("dp")
    pairs = dp_count // CORES
    dp = lax.axis_index("dp")
    core, pair = lax.rem(dp, CORES), dp // CORES
    split = [
        p.reshape(pairs, CORES, p.shape[0] // dp_count, p.shape[1])
        for p in partials
    ]
    landed = twin_exchange(split)
    chip = [
        (
            lax.dynamic_index_in_dim(p, core, axis=1, keepdims=False).astype(jnp.float32)
            + r.astype(jnp.float32)
        ).astype(p.dtype)
        for p, r in zip(split, landed)
    ]
    *others, pieces_in = pair_exchange(chip, pieces)
    own_piece = lax.dynamic_index_in_dim(pieces, lax.axis_index("fsdp"), axis=0, keepdims=False)
    tokens = own_piece.astype(jnp.float32) + jnp.sum(pieces_in.astype(jnp.float32), axis=0)
    return tokens, [
        lax.dynamic_index_in_dim(p, pair, axis=0, keepdims=False).astype(jnp.float32)
        + jnp.sum(r.astype(jnp.float32), axis=0)
        for p, r in zip(chip, others)
    ]


def split_features(
    inputs,
    gain_mixer,
    weight_in,
    conv_taps,
    weight_out,
    gain_ffn,
    weight_gate,
    weight_up,
    weight_down,
    cotangent,
):
    dp_count = lax.axis_size("dp")
    fs_count = lax.axis_size("fsdp")
    width = weight_out.shape[1]
    part = weight_out.shape[0]
    quarter = dp_count * part
    hid = dp_count * weight_down.shape[0]

    small = jnp.concatenate([gain_mixer[None], gain_ffn[None], conv_taps], axis=0)
    lanes = max(128, part)
    small = jnp.pad(small, ((0, 8 - small.shape[0]), (0, lanes - part)))
    gu_blocks = jnp.concatenate(
        [
            column_blocks(weight_gate, 1, dp_count, fs_count),
            column_blocks(weight_up, 1, dp_count, fs_count),
        ],
        axis=2,
    )
    grad_out = cotangent[0]
    x_all, grad_all, small_all, in_cols, gu_cols, out_rows, down_rows = gather_all(
        inputs[0],
        grad_out,
        small,
        column_blocks(weight_in, 3, dp_count, fs_count),
        gu_blocks,
        weight_out,
        weight_down,
    )
    x_all = x_all.reshape(-1, width)
    grad_all = grad_all.reshape(-1, width)
    in_cols = in_cols.reshape(width, 3 * quarter)
    gu_cols = gu_cols.reshape(width, 2 * hid)
    out_rows = out_rows.reshape(quarter, width)
    down_rows = down_rows.reshape(hid, width)
    small_all = small_all[:, :, : KW + 2, :part]
    gain1 = small_all[:, :, 0].reshape(width)
    gain2 = small_all[:, :, 1].reshape(width)
    taps32 = (
        lax.dynamic_index_in_dim(small_all, lax.axis_index("fsdp"), axis=1, keepdims=False)[:, 2:]
        .transpose(1, 0, 2)
        .reshape(KW, quarter)
        .astype(jnp.float32)
    )

    _, _, pre1_all = norm_forward(x_all.astype(jnp.float32), gain1)
    act1_all = pre1_all.astype(jnp.bfloat16)
    projected = product(act1_all, in_cols)
    bpart = projected[:, :quarter]
    cpart = projected[:, quarter : 2 * quarter]
    xpart = projected[:, 2 * quarter :]
    gated = bpart * xpart
    lagged_rows = [lagged(gated, offset) for offset in range(KW)]
    conv = taps32[0] * lagged_rows[0]
    for offset in range(1, KW):
        conv = conv + taps32[offset] * lagged_rows[offset]
    act2 = (cpart * conv).astype(jnp.bfloat16)
    hidden = inputs[0].astype(jnp.float32)
    normed1, scale1, _ = norm_forward(hidden, gain1)
    resid = hidden + token_share(product(act2, out_rows), 3, "share_out")
    normed2, scale2, pre2 = norm_forward(resid, gain2)
    act3_all = whole_sequence(pre2.astype(jnp.bfloat16), 4, "gather_ffn")
    gate_up = product(act3_all, gu_cols)
    gate, upval = gate_up[:, :hid], gate_up[:, hid:]
    sig = jax.nn.sigmoid(gate)
    act4 = (gate * sig * upval).astype(jnp.bfloat16)
    dact4 = product_nt(grad_all, down_rows)
    dgate = (dact4 * upval * sig * (1.0 + gate * (1.0 - sig))).astype(jnp.bfloat16)
    dupval = (dact4 * gate * sig).astype(jnp.bfloat16)
    dgu = jnp.concatenate([dgate, dupval], axis=1)
    dact3 = token_share(product_nt(dgu, gu_cols), 5, "share_ffn")
    down_pieces = token_pieces(product(act4, down_rows))
    dnorm2, g_gain2 = norm_backward(dact3, normed2, scale2, gain2)
    dresid = grad_out.astype(jnp.float32) + dnorm2
    dres_all = whole_sequence(dresid.astype(jnp.bfloat16), 6, "gather_dres")
    dact2 = product_nt(dres_all, out_rows)
    dcpart = dact2 * conv
    dconv = dact2 * cpart
    g_taps = jnp.stack(
        [jnp.sum(dconv * lagged_rows[offset], axis=0) for offset in range(KW)], axis=0
    )
    dgated = taps32[0] * dconv
    for offset in range(1, KW):
        dgated = dgated + taps32[offset] * leading(dconv, offset)
    dproj = jnp.concatenate([dgated * xpart, dcpart, dgated * bpart], axis=1).astype(jnp.bfloat16)
    dact1 = token_share_async(product_nt(dproj, in_cols))
    dnorm1, g_gain1 = norm_backward(dact1, normed1, scale1, gain1)
    grad_inputs = dresid + dnorm1

    own_column = (jnp.arange(fs_count) == lax.axis_index("fsdp"))[None, None, :, None]
    taps_spread = jnp.where(own_column, g_taps.reshape(KW, dp_count, 1, part), 0.0).reshape(KW, width)
    small_grad = jnp.concatenate([g_gain1[None], g_gain2[None], taps_spread], axis=0)
    small_grad = jnp.pad(small_grad, ((0, 8 - small_grad.shape[0]), (0, 0)))
    small_grad = small_grad.reshape(8, dp_count, fs_count, part).transpose(1, 2, 0, 3)
    small_grad = jnp.pad(small_grad, ((0, 0), (0, 0), (0, 0), (0, lanes - part)))
    down_sum, (g_small, g_gu, g_down, g_in, g_out) = reduce_all(
        [small_grad.reshape(dp_count * fs_count * 8, lanes)]
        + [
            grad.astype(jnp.bfloat16)
            for grad in (
                product_tn(act3_all, dgu),
                product_tn(act4, grad_all),
                product_tn(act1_all, dproj),
                product_tn(act2, dres_all),
            )
        ],
        down_pieces,
    )
    outputs = (resid + down_sum).astype(jnp.bfloat16)
    moved = jnp.concatenate([g_in, g_gu], axis=1).astype(jnp.bfloat16)
    moved, small_parts = along_line(
        [
            moved.reshape(fs_count, part, 3 * quarter + 2 * hid),
            g_small.reshape(fs_count, 8, lanes),
        ],
        False,
        7,
        "owner_exchange",
    )
    moved = moved.astype(jnp.float32)
    g_in_owned = moved[:, :, : 3 * quarter]
    g_gu_owned = moved[:, :, 3 * quarter :]
    small_owned = jnp.sum(small_parts, axis=0)[: KW + 2, :part]
    return (
        outputs[None],
        grad_inputs[None],
        small_owned[0],
        column_join(g_in_owned, 3, dp_count, fs_count),
        small_owned[2:],
        g_out,
        small_owned[1],
        column_join(g_gu_owned[:, :, :hid], 1, dp_count, fs_count),
        column_join(g_gu_owned[:, :, hid:], 1, dp_count, fs_count),
        g_down,
    )

HALO = 16


class Mover:
    def __init__(self, sends, recvs, locals_):
        self.sends, self.recvs, self.locals = sends, recvs, locals_
        self.count = 0
        self.local_count = 0
        self.open = []

    def push(self, src, dst, peer):
        copy = push(src, dst, self.sends, self.recvs, self.count, peer)
        self.count += 1
        self.open.append(copy)
        return copy

    def local(self, src, dst):
        copy = pltpu.make_async_copy(src, dst, self.locals.at[self.local_count])
        self.local_count += 1
        copy.start()
        return copy

    def finish(self):
        for copy in self.open:
            copy.wait_send()


class Line:
    def __init__(self, move, slot, dp, fs, fs_count):
        self.move, self.slot, self.dp, self.fs, self.size = move, slot, dp, fs, fs_count
        self.base = move.count
        move.count += CORES * fs_count

    def copy(self, source, up):
        index = self.base + CORES * source + (1 if up else 0)
        to = lax.rem(self.fs + (1 if up else self.size - 1), self.size)
        return pltpu.make_async_remote_copy(
            src_ref=self.slot(source),
            dst_ref=self.slot(source),
            send_sem=self.move.sends.at[index],
            recv_sem=self.move.recvs.at[index],
            device_id=(self.dp, to),
            device_id_type=MESH,
        )

    def start(self):
        @pl.when(self.fs < self.size - 1)
        def _():
            self.copy(self.fs, True).start()

        @pl.when(self.fs > 0)
        def _():
            self.copy(self.fs, False).start()

    def step(self, hop):
        below, above = self.fs - hop, self.fs + hop

        @pl.when(below >= 0)
        def _():
            self.copy(below, True).wait_recv()

            @pl.when(self.fs < self.size - 1)
            def _():
                self.copy(below, True).start()

        @pl.when(above < self.size)
        def _():
            self.copy(above, False).wait_recv()

            @pl.when(self.fs > 0)
            def _():
                self.copy(above, False).start()

    def finish(self):
        for hop in range(self.size):

            @pl.when((self.fs - hop >= 0) & (self.fs < self.size - 1))
            def _():
                self.copy(self.fs - hop, True).wait_send()

            @pl.when((self.fs + hop < self.size) & (self.fs > 0))
            def _():
                self.copy(self.fs + hop, False).wait_send()


class LineSum:
    def __init__(self, move, own, send, land, dp, fs, fs_count):
        self.move, self.own, self.send, self.land = move, own, send, land
        self.dp, self.fs, self.size = dp, fs, fs_count
        self.base = move.count
        move.count += CORES * fs_count

    def copy(self, dest, up, holder):
        index = self.base + CORES * dest + (1 if up else 0)
        to = lax.rem(holder + (1 if up else self.size - 1), self.size)
        slot = dest if up else jnp.where(dest == to, self.size, dest)
        return pltpu.make_async_remote_copy(
            src_ref=self.send.at[dest],
            dst_ref=self.land.at[slot],
            send_sem=self.move.sends.at[index],
            recv_sem=self.move.recvs.at[index],
            device_id=(self.dp, to),
            device_id_type=MESH,
        )

    def source(self, dest, up):
        return self.copy(dest, up, lax.rem(self.fs + (self.size - 1 if up else 1), self.size))

    def start(self):
        last = self.size - 1
        for far in range(last):

            @pl.when(self.fs == 0)
            def _():
                self.send[last - far] = self.own(last - far).astype(jnp.bfloat16)
                self.copy(last - far, True, self.fs).start()

            @pl.when(self.fs == last)
            def _():
                self.send[far] = self.own(far).astype(jnp.bfloat16)
                self.copy(far, False, self.fs).start()

    def relay(self, dest, up):
        self.source(dest, up).wait_recv()
        total = self.own(dest).astype(jnp.float32) + self.land[dest].astype(jnp.float32)
        self.send[dest] = total.astype(jnp.bfloat16)
        self.copy(dest, up, self.fs).start()

    def step(self, hop):
        last = self.size - 1
        if hop < last:

            @pl.when((self.fs >= 1) & (self.fs <= hop))
            def _():
                self.relay(self.fs + last - hop, True)

            @pl.when((self.fs < last) & (last - self.fs <= hop))
            def _():
                self.relay(self.fs + hop - last, False)

    def total(self, out):
        out[...] = self.own(self.fs).astype(jnp.float32)

        @pl.when(self.fs > 0)
        def _():
            self.source(self.fs, True).wait_recv()
            out[...] += self.land[self.fs].astype(jnp.float32)

        @pl.when(self.fs < self.size - 1)
        def _():
            self.source(self.fs, False).wait_recv()
            out[...] += self.land[self.size].astype(jnp.float32)

    def finish(self):
        for dest in range(self.size):

            @pl.when(self.fs < dest)
            def _():
                self.copy(dest, True, self.fs).wait_send()

            @pl.when(self.fs > dest)
            def _():
                self.copy(dest, False, self.fs).wait_send()


def seats(pairs, fs_count):
    dp, fs, pair, core, partner = place()
    z_peers = [(dp, lax.rem(fs + o, fs_count)) for o in range(1, fs_count)]
    p_peers = [(lax.rem(pair + o, pairs) * CORES + core, fs) for o in range(1, pairs)]
    p_from = [lax.rem(pair + pairs - o, pairs) for o in range(1, pairs)]
    return dp, fs, pair, core, partner, z_peers, p_peers, p_from


def norm_scale(hidden):
    return lax.rsqrt(jnp.mean(hidden * hidden, axis=-1, keepdims=True) + EPS)


def mixer_forward_kernel(
    pairs, fs_count,
    x_ref, cot_ref, small_ref, in_hbm, gate_hbm, up_hbm, out_ref, down_ref,
    act1_out, proj_out, act2_out, in_out_o, out_out, gains_out, taps_out, resid_out,
    act3_out, cot_out, gu_all, down_all,
    act1_o, proj_o, act2_o, in_all, out_all, gains_o, taps_o, resid_o, act3_all, cot_all,
    x_all, halo_all, small_all, in_ref, gate_ref, up_ref, in_blk, gu_blk,
    tw_out, tw_in, pr_out, pr_in, local_sem, sends, recvs,
):
    dp, fs, pair, core, partner, z_peers, p_peers, p_from = seats(pairs, fs_count)
    count = pairs * CORES
    tokens, width = x_ref.shape
    part = in_ref.shape[0]
    feat = width // count
    inner = gate_ref.shape[1] // (count * fs_count)
    hid = inner * count
    other = 1 - core
    move = Mover(sends, recvs, local_sem)
    f32 = jnp.float32

    in_local = move.local(in_hbm, in_ref)
    x_local = move.local(x_ref, x_all.at[dp])
    gate_local = move.local(gate_hbm, gate_ref)
    up_local = move.local(up_hbm, up_ref)
    out_local = move.local(out_ref, out_all.at[fs])
    cot_local = move.local(cot_ref, cot_all.at[fs])
    down_local = move.local(down_ref, down_all.at[dp])
    crossed = [(peer[0] + other - core, fs) for peer in p_peers]
    greet(z_peers + p_peers + crossed + [partner])
    small_z = [move.push(small_ref, small_all.at[dp, fs], peer) for peer in z_peers]
    halo_next = move.push(x_ref.at[pl.ds(tokens - HALO, HALO)], halo_all.at[dp, pl.ds(0, HALO)], z_peers[0])
    halo_prev = move.push(x_ref.at[pl.ds(0, HALO)], halo_all.at[dp, pl.ds(HALO, HALO)], z_peers[-1])
    in_local.wait()
    for to in range(count):
        for k in range(3):
            in_blk[to % CORES, to // CORES, :, k * feat : (k + 1) * feat] = in_ref[
                :, k * width + to * feat : k * width + (to + 1) * feat
            ]
    in_twin = move.push(in_blk.at[other, pair], in_all.at[dp, fs], partner)
    in_via = [
        move.push(in_blk.at[other, peer[0] // CORES], in_all.at[dp, fs], peer) for peer in crossed
    ]
    in_out = [move.push(in_blk.at[core, peer[0] // CORES], in_all.at[dp, fs], peer) for peer in p_peers]
    x_out = [move.push(x_ref, x_all.at[dp], peer) for peer in p_peers]
    x_twin = move.push(x_ref, x_all.at[dp], partner)
    small_all[dp, fs] = small_ref[...]
    in_all[dp, fs] = in_blk[core, pair]
    gate_local.wait()
    up_local.wait()
    for which, ref in enumerate((gate_ref, up_ref)):
        wide = ref[...].astype(f32)
        for to in range(fs_count):
            pieces = [
                wide[:, (d * fs_count + to) * inner : (d * fs_count + to + 1) * inner]
                for d in range(count)
            ]
            gu_blk[to, :, which * hid : (which + 1) * hid] = jnp.concatenate(pieces, axis=1).astype(
                jnp.bfloat16
            )
    gu_local = move.local(gu_blk.at[fs], gu_all.at[dp, fs])
    for copy in small_z:
        copy.wait_recv()
    small_out = [move.push(small_all.at[dp], small_all.at[dp], peer) for peer in p_peers]
    small_twin = [move.push(small_all.at[dp], small_all.at[dp], partner)]
    halo_next.wait_recv()
    halo_prev.wait_recv()
    halo_out = [move.push(halo_all.at[dp], halo_all.at[dp], peer) for peer in p_peers]
    halo_twin = [move.push(halo_all.at[dp], halo_all.at[dp], partner)]
    for copy in in_out + in_via + [in_twin]:
        copy.wait_recv()
    in_line = Line(move, lambda f: in_all.at[:, f], dp, fs, fs_count)
    out_line = Line(move, lambda f: out_all.at[f], dp, fs, fs_count)
    cot_line = Line(move, lambda f: cot_all.at[f], dp, fs, fs_count)
    act3_line = Line(move, lambda f: act3_all.at[f], dp, fs, fs_count)
    in_line.start()
    out_local.wait()
    out_line.start()
    down_out = [move.push(down_ref, down_all.at[dp], peer) for peer in p_peers]
    down_twin = [move.push(down_ref, down_all.at[dp], partner)]
    in_line.step(1)
    out_line.step(1)

    small_rel, x_rel = [], []
    for o, source in enumerate(p_from):
        src = source * CORES + core
        small_out[o].wait_recv()
        halo_out[o].wait_recv()
        x_out[o].wait_recv()
        small_rel.append(move.push(small_all.at[src], small_all.at[src], partner))
        x_rel.append(move.push(halo_all.at[src], halo_all.at[src], partner))
        x_rel.append(move.push(x_all.at[src], x_all.at[src], partner))
    in_line.step(2)
    out_line.step(2)
    gu_z = [move.push(gu_blk.at[peer[1]], gu_all.at[dp, fs], peer) for peer in z_peers]
    for copy in small_twin + small_rel + [x_twin] + halo_twin + x_rel:
        copy.wait_recv()
    x_local.wait()

    for d in range(count):
        total = small_all[d, 0].astype(f32)
        for f in range(1, fs_count):
            total = total + small_all[d, f].astype(f32)
        gains_o[:, d * feat : (d + 1) * feat] = total
    total = small_all[dp, 0].astype(f32)
    for f in range(1, fs_count):
        total = total + small_all[dp, f].astype(f32)
    taps_o[...] = total
    has_prev, has_next = fs > 0, fs < fs_count - 1

    def norm_step(i, carry):
        gain = gains_o[0:1, :]
        rows = x_all[i].astype(f32)
        act1_o[i, HALO : HALO + tokens] = (rows * norm_scale(rows) * gain).astype(jnp.bfloat16)
        edge = halo_all[i].astype(f32)
        edge = edge * norm_scale(edge) * gain
        act1_o[i, 0:HALO] = jnp.where(has_prev, edge[:HALO], 0.0).astype(jnp.bfloat16)
        act1_o[i, HALO + tokens :] = jnp.where(has_next, edge[HALO:], 0.0).astype(jnp.bfloat16)
        return carry

    lax.fori_loop(0, count, norm_step, 0)
    kept = [
        move.local(act1_o, act1_out), move.local(gains_o, gains_out), move.local(taps_o, taps_out)
    ]
    for hop in range(3, fs_count):
        in_line.step(hop)

    def project_step(i, carry):
        proj_o[i] = product(act1_o[i], in_all[...].reshape(width, 3 * feat))
        gated = proj_o[i, :, 0:feat] * proj_o[i, :, 2 * feat :]
        conv = taps_o[2:3, :] * gated[HALO : HALO + tokens]
        for k in range(1, KW):
            conv = conv + taps_o[2 + k : 3 + k, :] * gated[HALO - k : HALO - k + tokens]
        act2_o[i] = (proj_o[i, HALO : HALO + tokens, feat : 2 * feat] * conv).astype(jnp.bfloat16)
        return carry

    lax.fori_loop(0, count, project_step, 0)
    cot_local.wait()
    cot_line.start()
    kept += [
        move.local(proj_o, proj_out), move.local(act2_o, act2_out), move.local(in_all, in_out_o)
    ]
    for hop in range(3, fs_count):
        out_line.step(hop)
    kept.append(move.local(out_all, out_out))

    def out_partial(dest):
        return product(act2_o[dest], out_all[...].reshape(feat, width))

    order = [lax.rem(pair + o, pairs) for o in range(1, pairs)] + [pair]
    share_tw, share_pr = [], []

    def share_twin(o):
        tw_out[o] = out_partial(order[o] * CORES + other).astype(jnp.bfloat16)
        share_tw.append(move.push(tw_out.at[o], tw_in.at[o], partner))

    share_twin(0)
    for o, j in enumerate(order):
        if o + 1 < pairs:
            share_twin(o + 1)
        value = out_partial(j * CORES + core)
        share_tw[o].wait_recv()
        value = value + tw_in[o].astype(f32)
        if o < pairs - 1:
            pr_out[o] = value.astype(jnp.bfloat16)
            share_pr.append(move.push(pr_out.at[o], pr_in.at[o], p_peers[o]))
        else:
            resid_o[...] = value + x_all[dp].astype(f32)
    cot_line.step(1)
    for copy in gu_z:
        copy.wait_recv()
    gu_local.wait()
    gu_out = [move.push(gu_all.at[dp], gu_all.at[dp], peer) for peer in p_peers]
    gu_twin = [move.push(gu_all.at[dp], gu_all.at[dp], partner)]
    for copy in share_pr:
        copy.wait_recv()
    if fs_count > 2:
        cot_line.step(2)
    resid = resid_o[...]
    for o in range(pairs - 1):
        resid = resid + pr_in[o].astype(f32)
    resid_o[...] = resid
    act3_all[fs] = (resid * norm_scale(resid) * gains_o[1:2, :]).astype(jnp.bfloat16)
    act3_line.start()
    kept.append(move.local(resid_o, resid_out))
    for o, source in enumerate(p_from):
        src = source * CORES + core
        down_out[o].wait_recv()
        down_twin.append(move.push(down_all.at[src], down_all.at[src], partner))
    for hop in range(1, fs_count):
        act3_line.step(hop)
    for hop in range(3, fs_count):
        cot_line.step(hop)
    kept += [move.local(act3_all, act3_out), move.local(cot_all, cot_out)]
    for o, source in enumerate(p_from):
        src = source * CORES + core
        gu_out[o].wait_recv()
        gu_twin.append(move.push(gu_all.at[src], gu_all.at[src], partner))
    for copy in down_twin + gu_twin:
        copy.wait_recv()
    down_local.wait()
    for copy in kept:
        copy.wait()
    move.finish()
    for line in (in_line, out_line, cot_line, act3_line):
        line.finish()


def mixer_forward(x, cot, small, w_in, w_gate, w_up, w_out, w_down):
    dp_count, fs_count = lax.axis_size("dp"), lax.axis_size("fsdp")
    pairs = dp_count // CORES
    tokens, width = x.shape
    part = w_in.shape[0]
    feat = width // dp_count
    hid = w_gate.shape[1] // fs_count
    bf, f32 = jnp.bfloat16, jnp.float32
    shape = jax.ShapeDtypeStruct
    long = tokens + 2 * HALO
    in_vmem = [
        shape((dp_count, long, width), bf),
        shape((dp_count, long, 3 * feat), f32),
        shape((dp_count, tokens, feat), bf),
        shape((dp_count, fs_count, part, 3 * feat), bf),
        shape((fs_count, part, width), bf),
        shape((small.shape[0], width), f32),
        shape((small.shape[0], feat), f32),
        shape((tokens, width), f32),
    ]
    in_vmem += [shape((fs_count, tokens, width), bf)] * 2
    anywhere = [
        shape((dp_count, fs_count, part, 2 * hid), bf),
        shape((dp_count,) + w_down.shape, bf),
    ]
    slots = 20 * fs_count + 20 * pairs + 40
    return pl.pallas_call(
        functools.partial(mixer_forward_kernel, pairs, fs_count),
        out_shape=in_vmem + anywhere,
        in_specs=[
            pl.BlockSpec(memory_space=pltpu.VMEM if index == 2 else pltpu.HBM) for index in range(8)
        ],
        out_specs=[pl.BlockSpec(memory_space=pltpu.HBM)] * (len(in_vmem) + len(anywhere)),
        scratch_shapes=[pltpu.VMEM(item.shape, item.dtype) for item in in_vmem]
        + [
            pltpu.VMEM((dp_count, tokens, width), bf),
            pltpu.VMEM((dp_count, 2 * HALO, width), bf),
            pltpu.VMEM((dp_count, fs_count) + small.shape, bf),
            pltpu.VMEM(w_in.shape, bf),
            pltpu.VMEM(w_gate.shape, bf),
            pltpu.VMEM(w_up.shape, bf),
            pltpu.VMEM((CORES, pairs, part, 3 * feat), bf),
            pltpu.VMEM((fs_count, part, 2 * hid), bf),
            pltpu.VMEM((pairs, tokens, width), bf),
            pltpu.VMEM((pairs, tokens, width), bf),
            pltpu.VMEM((pairs - 1, tokens, width), bf),
            pltpu.VMEM((pairs - 1, tokens, width), bf),
            pltpu.SemaphoreType.DMA((24,)),
            pltpu.SemaphoreType.DMA((slots,)),
            pltpu.SemaphoreType.DMA((slots,)),
        ],
        compiler_params=pltpu.CompilerParams(
            collective_id=8, has_side_effects=True, vmem_limit_bytes=60 * 1024 * 1024
        ),
        name="mixer_forward",
    )(x, cot, small, w_in, w_gate, w_up, w_out, w_down)


def mixer_backward_kernel(
    pairs, fs_count,
    x_h, gains_ref, taps_ref, resid_h, act1_h, proj_h, act2_h, in_h, out_h,
    gu_h, act3_h, dgate_h, dup_h, act4_h, cot_h, down_h,
    out_o, gx_o, gin_fin, gout_o, gu_zi, gdown_o, small_o,
    x_ref, resid_ref, act1_ref, proj_ref, act2_ref, in_w, out_w,
    gu_ref, act3_ref, dgu_ref, act4_ref, cot_ref, down_ref,
    d3_own, d3_rx, dn_ref, dn_tx, dn_rx, acc, gin_acc,
    ggu_two, gd_all, gu_tw, down_tw, gu_chip, down_chip, gu_rx, down_rx, gu_zo,
    dres_all, dproj, taps_acc, gin_p, gin_tx, gin_rx, gout_p, gout_tx, gout_rx, gin_own, gin_stage,
    tw_out, tw_in, pr_out, pr_in, sm_own, sm_rx, tp_rx, sm_p, sm_tw, sm_pr,
    local_sem, sends, recvs,
):
    dp, fs, pair, core, partner, z_peers, p_peers, p_from = seats(pairs, fs_count)
    count = pairs * CORES
    tokens, width = x_ref.shape
    feat = width // count
    part = feat // fs_count
    hid = act4_ref.shape[1]
    inner = hid // count
    other = 1 - core
    twin_dp = pair * CORES + other
    move = Mover(sends, recvs, local_sem)
    f32, bf = jnp.float32, jnp.bfloat16
    order = [lax.rem(pair + o, pairs) for o in range(1, pairs)] + [pair]

    dgate_l = move.local(dgate_h, dgu_ref.at[:, pl.ds(0, hid)])
    dup_l = move.local(dup_h, dgu_ref.at[:, pl.ds(hid, hid)])
    gu_l = move.local(gu_h, gu_ref)
    greet(z_peers + p_peers + [partner])
    dgate_l.wait()
    dup_l.wait()
    gu_l.wait()
    act3_l = move.local(act3_h, act3_ref)
    act4_l = move.local(act4_h, act4_ref)
    cot_l = move.local(cot_h, cot_ref)
    down_l = move.local(down_h, down_ref)
    late = [
        move.local(src, dst)
        for src, dst in (
            (x_h, x_ref), (resid_h, resid_ref), (out_h, out_w), (proj_h, proj_ref),
            (in_h, in_w), (act1_h, act1_ref), (act2_h, act2_ref),
        )
    ]

    d3_z = []

    def d3_piece(o):
        to = (z_peers + [(dp, fs)])[o]
        at = pl.ds(pl.multiple_of(to[1] * tokens, tokens), tokens)
        d3_own[o] = product_nt(dgu_ref[at, :], gu_ref[...].reshape(width, 2 * hid)).astype(bf)
        if o < fs_count - 1:
            d3_z.append(move.push(d3_own.at[o], d3_rx.at[o], to))

    d3_piece(0)
    dn = LineSum(move, lambda f: dn_ref[f], dn_tx, dn_rx, dp, fs, fs_count)
    gin_line = LineSum(move, lambda f: gin_p[:, f], gin_tx, gin_rx, dp, fs, fs_count)
    gout_line = LineSum(move, lambda f: gout_p[f], gout_tx, gout_rx, dp, fs, fs_count)
    act3_l.wait()

    def gu_partial(dest):
        left = act3_ref[:, :, pl.ds(pl.multiple_of(dest * feat, feat), feat)]
        return product_tn(left.reshape(fs_count * tokens, feat), dgu_ref[...])

    def down_slot(dest):
        return pl.ds(pl.multiple_of(dest * inner, inner), inner)

    gu_t, gu_p = [], []

    def gu_twin(o):
        ggu_two[o] = gu_partial(order[o] * CORES + other).astype(bf)
        gu_t.append(move.push(ggu_two.at[o], gu_tw.at[o], partner))

    def gu_own(o):
        value = gu_partial(order[o] * CORES + core)
        gu_t[o].wait_recv()
        gu_chip[o] = (value + gu_tw[o].astype(f32)).astype(bf)
        if o < pairs - 1:
            gu_p.append(move.push(gu_chip.at[o], gu_rx.at[o], p_peers[o]))

    gu_twin(0)
    for o in range(max(pairs, fs_count)):
        if o + 1 < pairs:
            gu_twin(o + 1)
        if o + 1 < fs_count:
            d3_piece(o + 1)
        if o < pairs:
            gu_own(o)
    act4_l.wait()
    cot_l.wait()
    down_l.wait()
    chunk = 3 * 128 if hid % (3 * 128) == 0 else 128

    def down_step(c, carry):
        at = pl.ds(pl.multiple_of(c * chunk, chunk), chunk)
        gd_all[at, :] = product_tn(
            act4_ref[:, at], cot_ref[...].reshape(fs_count * tokens, width)
        ).astype(bf)
        return carry

    lax.fori_loop(0, hid // chunk, down_step, 0)
    down_t = [
        move.push(gd_all.at[down_slot(j * CORES + other)], down_tw.at[o], partner)
        for o, j in enumerate(order)
    ]

    def dn_step(f, carry):
        at = pl.ds(pl.multiple_of(f * tokens, tokens), tokens)
        dn_ref[f] = product(act4_ref[at, :], down_ref[...].reshape(hid, width)).astype(bf)
        return carry

    lax.fori_loop(0, fs_count, dn_step, 0)
    for copy in late:
        copy.wait()

    for copy in d3_z:
        copy.wait_recv()
    dact3 = d3_own[fs_count - 1].astype(f32)
    for o in range(fs_count - 1):
        dact3 = dact3 + d3_rx[o].astype(f32)
    resid = resid_ref[...]
    scale2 = norm_scale(resid)
    normed2 = resid * scale2
    sm_own[1:2, :] = jnp.sum(dact3 * normed2, axis=0, keepdims=True)
    dnormed = dact3 * gains_ref[1:2, :]
    dresid = cot_ref[fs].astype(f32) + scale2 * (
        dnormed - normed2 * jnp.mean(dnormed * normed2, axis=-1, keepdims=True)
    )
    gx_o[...] = dresid
    dres_all[dp, 0:tokens] = dresid.astype(bf)
    mine = dres_all.at[dp, pl.ds(0, tokens)]
    edge = dres_all.at[dp, pl.ds(tokens, HALO)]
    halo_z = move.push(dres_all.at[dp, pl.ds(0, HALO)], edge, z_peers[-1])
    dres_out = [move.push(mine, mine, peer) for peer in p_peers]
    dres_twin = [move.push(mine, mine, partner)]
    dn.start()
    down_p = []
    for o, j in enumerate(order):
        down_t[o].wait_recv()
        down_chip[o] = (
            gd_all[down_slot(j * CORES + core), :].astype(f32) + down_tw[o].astype(f32)
        ).astype(bf)
    halo_z.wait_recv()
    edge_out = [move.push(edge, edge, peer) for peer in p_peers]
    dres_twin.append(move.push(edge, edge, partner))
    for o, source in enumerate(p_from):
        src = source * CORES + core
        dres_out[o].wait_recv()
        edge_out[o].wait_recv()
        dres_twin.append(move.push(dres_all.at[src], dres_all.at[src], partner))
    for o, peer in enumerate(p_peers):
        down_p.append(move.push(down_chip.at[o], down_rx.at[o], peer))
    dn.step(1)
    for copy in dres_twin:
        copy.wait_recv()

    taps_acc[...] = jnp.zeros(taps_acc.shape, f32)

    def mixer_step(i, carry):
        dact2 = product_nt(dres_all[i], out_w[...].reshape(feat, width))
        bpart = proj_ref[i, :, 0:feat]
        cpart = proj_ref[i, :, feat : 2 * feat]
        xpart = proj_ref[i, :, 2 * feat :]
        gated = bpart * xpart
        conv = taps_ref[2:3, :] * gated[HALO : HALO + tokens]
        for k in range(1, KW):
            conv = conv + taps_ref[2 + k : 3 + k, :] * gated[HALO - k : HALO - k + tokens]
        dconv = dact2 * cpart[HALO:]
        dcpart = dact2[:tokens] * conv
        dgated = taps_ref[2:3, :] * dconv[:tokens]
        for k in range(1, KW):
            dgated = dgated + taps_ref[2 + k : 3 + k, :] * dconv[k : k + tokens]
        for k in range(KW):
            taps_acc[k : k + 1, :] += jnp.sum(
                dconv[:tokens] * gated[HALO - k : HALO - k + tokens], axis=0, keepdims=True
            )
        dproj[i, :, 0:feat] = (dgated * xpart[HALO : HALO + tokens]).astype(bf)
        dproj[i, :, feat : 2 * feat] = dcpart.astype(bf)
        dproj[i, :, 2 * feat :] = (dgated * bpart[HALO : HALO + tokens]).astype(bf)
        return carry

    lax.fori_loop(0, count, mixer_step, 0)

    sm_own[0:1, :] = jnp.zeros((1, width), f32)
    sm_own[2:, :] = jnp.zeros((sm_own.shape[0] - 2, width), f32)

    def in_partial(dest):
        value = product_nt(dproj[dest], in_w[...].reshape(width, 3 * feat))
        left = act1_ref[dest, pl.ds(HALO, tokens), :].astype(f32)
        sm_own[0:1, :] += jnp.sum(value * left, axis=0, keepdims=True)
        return value

    def gin_step(c, carry):
        left = act1_ref[:, pl.ds(HALO, tokens), pl.ds(pl.multiple_of(c * feat, feat), feat)]
        grad = product_tn(
            left.reshape(count * tokens, feat), dproj[...].reshape(count * tokens, 3 * feat)
        )
        gin_p[c] = grad.astype(bf).reshape(fs_count, part, 3 * feat)
        return carry

    for copy in gu_p:
        copy.wait_recv()
    total = gu_chip[pairs - 1].astype(f32)
    for o in range(pairs - 1):
        total = total + gu_rx[o].astype(f32)
    gu_zo[...] = total.astype(bf).reshape(fs_count, part, 2 * hid)
    gu_z = [move.push(gu_zo.at[peer[1]], gu_zi.at[fs], peer) for peer in z_peers]
    gu_zi[fs] = gu_zo[fs]

    lax.fori_loop(0, count, gin_step, 0)
    dn.step(2)
    gin_line.start()

    share_tw, share_pr = [], []

    def share_twin(o):
        tw_out[o] = in_partial(order[o] * CORES + other).astype(bf)
        share_tw.append(move.push(tw_out.at[o], tw_in.at[o], partner))

    share_twin(0)
    dact1 = None
    for o, j in enumerate(order):
        if o + 1 < pairs:
            share_twin(o + 1)
        if o == pairs // 2:
            gin_line.step(1)
        value = in_partial(j * CORES + core)
        share_tw[o].wait_recv()
        value = value + tw_in[o].astype(f32)
        if o < pairs - 1:
            pr_out[o] = value.astype(bf)
            share_pr.append(move.push(pr_out.at[o], pr_in.at[o], p_peers[o]))
        else:
            dact1 = value
    sm_own[0:1, :] = sm_own[0:1, :] / gains_ref[0:1, :]
    sm_z = [move.push(sm_own, sm_rx.at[o], peer) for o, peer in enumerate(z_peers)]
    taps_z = [move.push(taps_acc, tp_rx.at[o], peer) for o, peer in enumerate(z_peers)]
    gin_line.step(2)
    grad = product_tn(
        act2_ref[...].reshape(count * tokens, feat),
        dres_all[:, 0:tokens].reshape(count * tokens, width),
    )
    gout_p[...] = grad.astype(bf).reshape(fs_count, part, width)
    gout_line.start()
    for hop in range(3, fs_count):
        dn.step(hop)

    gout_line.step(1)
    for hop in range(3, fs_count):
        gin_line.step(hop)
    gin_line.total(gin_acc)
    for d in range(count):
        gin_own[d % CORES, d // CORES] = gin_acc[d].astype(bf)
    gin_t = move.push(gin_own.at[other], gin_stage, partner)
    gin_out = [
        move.push(gin_own.at[core, peer[0] // CORES], gin_fin.at[dp], peer) for peer in p_peers
    ]
    gin_fin[dp] = gin_own[core, pair]
    for copy in sm_z:
        copy.wait_recv()
    small_sum = sm_own[...]
    for o in range(fs_count - 1):
        small_sum = small_sum + sm_rx[o]
    for d in range(count):
        sm_p[d % CORES, d // CORES] = small_sum[:, d * feat : (d + 1) * feat]
    sm_t = move.push(sm_p.at[other], sm_tw, partner)
    gin_t.wait_recv()
    gin_via = [
        move.push(gin_stage.at[peer[0] // CORES], gin_fin.at[twin_dp], peer) for peer in p_peers
    ]
    gin_fin[twin_dp] = gin_stage[pair]


    for hop in range(2, fs_count):
        gout_line.step(hop)
    for copy in share_pr:
        copy.wait_recv()
    for o in range(pairs - 1):
        dact1 = dact1 + pr_in[o].astype(f32)
    hidden = x_ref[...].astype(f32)
    scale1 = norm_scale(hidden)
    normed1 = hidden * scale1
    dnormed = dact1 * gains_ref[0:1, :]
    gx_o[...] += scale1 * (dnormed - normed1 * jnp.mean(dnormed * normed1, axis=-1, keepdims=True))

    sm_t.wait_recv()
    for j in range(pairs):
        sm_tw[j] = sm_tw[j] + sm_p[core, j]
    sm_pair = [
        move.push(sm_tw.at[peer[0] // CORES], sm_pr.at[o], peer) for o, peer in enumerate(p_peers)
    ]
    for copy in down_p:
        copy.wait_recv()
    total = down_chip[pairs - 1].astype(f32)
    for o in range(pairs - 1):
        total = total + down_rx[o].astype(f32)
    gdown_o[...] = total
    dn.total(acc)
    out_o[...] = (resid_ref[...] + acc[...]).astype(bf)
    for copy in taps_z:
        copy.wait_recv()
    gout_line.total(gout_o)
    for copy in gu_z:
        copy.wait_recv()
    for copy in gin_out + gin_via:
        copy.wait_recv()
    for copy in sm_pair:
        copy.wait_recv()
    total = sm_tw[pair]
    for o in range(pairs - 1):
        total = total + sm_pr[o]
    taps = taps_acc[...]
    for o in range(fs_count - 1):
        taps = taps + tp_rx[o]
    small_o[0] = total
    small_o[1] = taps
    move.finish()
    for line in (dn, gin_line, gout_line):
        line.finish()


def mixer_backward(x, gains, taps, resid, act1, proj, act2, in_w, out_w, gu, act3, dgate, dup, act4, cot, down):
    dp_count, fs_count = lax.axis_size("dp"), lax.axis_size("fsdp")
    pairs = dp_count // CORES
    tokens, width = x.shape
    feat = width // dp_count
    part = feat // fs_count
    hid2 = 2 * dgate.shape[1]
    dgu = jax.ShapeDtypeStruct((dgate.shape[0], hid2), dgate.dtype)
    rows_down = down.shape[1]
    bf, f32 = jnp.bfloat16, jnp.float32
    shape = jax.ShapeDtypeStruct
    outs = [
        shape((tokens, width), bf),
        shape((tokens, width), f32),
        shape((dp_count, part, 3 * feat), bf),
        shape((part, width), f32),
        shape((fs_count, part, hid2), bf),
        shape((rows_down, width), f32),
        shape((2, 8, feat), f32),
    ]
    slots = 24 * fs_count + 20 * pairs + 40
    loaded = (x, resid, act1, proj, act2, in_w, out_w, gu, act3, dgu, act4, cot, down)
    scratch = [(item.shape, item.dtype) for item in loaded] + [
        ((fs_count, tokens, width), bf),
        ((fs_count - 1, tokens, width), bf),
        ((fs_count, tokens, width), bf),
        ((fs_count, tokens, width), bf),
        ((fs_count + 1, tokens, width), bf),
        ((tokens, width), f32),
        ((dp_count, part, 3 * feat), f32),
        ((pairs, feat, hid2), bf),
        ((hid2 // 2, width), bf),
        ((pairs, feat, hid2), bf),
        ((pairs, rows_down, width), bf),
        ((pairs, feat, hid2), bf),
        ((pairs, rows_down, width), bf),
        ((pairs - 1, feat, hid2), bf),
        ((pairs - 1, rows_down, width), bf),
        ((fs_count, part, hid2), bf),
        ((dp_count, tokens + HALO, width), bf),
        ((dp_count, tokens, 3 * feat), bf),
        ((8, feat), f32),
        ((dp_count, fs_count, part, 3 * feat), bf),
        ((fs_count, dp_count, part, 3 * feat), bf),
        ((fs_count + 1, dp_count, part, 3 * feat), bf),
        ((fs_count, part, width), bf),
        ((fs_count, part, width), bf),
        ((fs_count + 1, part, width), bf),
        ((CORES, pairs, part, 3 * feat), bf),
        ((pairs, part, 3 * feat), bf),
        ((pairs, tokens, width), bf),
        ((pairs, tokens, width), bf),
        ((pairs - 1, tokens, width), bf),
        ((pairs - 1, tokens, width), bf),
        ((8, width), f32),
        ((fs_count - 1, 8, width), f32),
        ((fs_count - 1, 8, feat), f32),
        ((CORES, pairs, 8, feat), f32),
        ((pairs, 8, feat), f32),
        ((pairs - 1, 8, feat), f32),
    ]
    return pl.pallas_call(
        functools.partial(mixer_backward_kernel, pairs, fs_count),
        out_shape=outs,
        in_specs=[
            pl.BlockSpec(memory_space=pltpu.VMEM if index in (1, 2) else pltpu.HBM)
            for index in range(16)
        ],
        out_specs=[pl.BlockSpec(memory_space=pltpu.VMEM)] * len(outs),
        scratch_shapes=[pltpu.VMEM(s, d) for s, d in scratch]
        + [pltpu.SemaphoreType.DMA((n,)) for n in (len(loaded) + 1, slots, slots)],
        compiler_params=pltpu.CompilerParams(
            collective_id=9, has_side_effects=True, vmem_limit_bytes=60 * 1024 * 1024
        ),
        name="mixer_backward",
    )(x, gains, taps, resid, act1, proj, act2, in_w, out_w, gu, act3, dgate, dup, act4, cot, down)


def finish_kernel(
    fs_count, count,
    out_i, gx_i, gin_h, gout_i, gu_h, gdown_i, small_i,
    out_o, gx_o, gin_o, gout_o, ggate_o, gup_o, gdown_o, gain1_o, gain2_o, taps_o,
    gin_fin, gu_zi, gin_v, gate_v, up_v, out_v, gx_v, gout_v, gdown_v, sems,
):
    part, feat = gout_i.shape[0], gin_fin.shape[2] // 3
    width, hid = gout_i.shape[1], gu_zi.shape[2] // 2
    inner = hid // count
    f32 = jnp.float32
    copies = []

    def send(src, dst):
        copy = pltpu.make_async_copy(src, dst, sems.at[len(copies)])
        copy.start()
        copies.append(copy)

    send(gin_h, gin_fin)
    send(gu_h, gu_zi)
    through = ((gx_i, gx_v, gx_o), (gdown_i, gdown_v, gdown_o), (out_i, out_v, out_o), (gout_i, gout_v, gout_o))
    for src, held, dst in through:
        send(src, held)
    gin_in, gu_in, *held_in = copies
    gin_count = len(copies)
    for copy, (src, held, dst) in zip(held_in, through):
        copy.wait()
        send(held, dst)
    gin_in.wait()
    for d in range(count):
        for k in range(3):
            gin_v[:, k * width + d * feat : k * width + (d + 1) * feat] = gin_fin[
                d, :, k * feat : (k + 1) * feat
            ].astype(f32)
    send(gin_v, gin_o)
    gu_in.wait()
    for which, (ref, dst) in enumerate(((gate_v, ggate_o), (up_v, gup_o))):
        wide = [gu_zi[f, :, which * hid : (which + 1) * hid].astype(f32) for f in range(fs_count)]
        pieces = [
            wide[f][:, d * inner : (d + 1) * inner] for d in range(count) for f in range(fs_count)
        ]
        ref[...] = jnp.concatenate(pieces, axis=1)
        send(ref, dst)
    fs = lax.axis_index("fsdp")
    small = small_i[...]
    mine = small[:, :, 0:part]
    for f in range(1, fs_count):
        mine = jnp.where(fs == f, small[:, :, f * part : (f + 1) * part], mine)
    gain1_o[...] = mine[0, 0:1]
    gain2_o[...] = mine[0, 1:2]
    taps_o[...] = mine[1, 0:KW]
    for copy in copies[gin_count:]:
        copy.wait()


def finish(out, gx, gin, gout, gu, gdown, small, wide_in, wide_ff):
    dp_count, fs_count = lax.axis_size("dp"), lax.axis_size("fsdp")
    part = gout.shape[0]
    f32 = jnp.float32
    shape = jax.ShapeDtypeStruct
    outs = [
        shape(out.shape, out.dtype),
        shape(gx.shape, f32),
        shape((part, wide_in), f32),
        shape(gout.shape, f32),
        shape((part, wide_ff), f32),
        shape((part, wide_ff), f32),
        shape(gdown.shape, f32),
        shape((1, part), f32),
        shape((1, part), f32),
        shape((KW, part), f32),
    ]
    return pl.pallas_call(
        functools.partial(finish_kernel, fs_count, dp_count),
        out_shape=outs,
        in_specs=[pl.BlockSpec(memory_space=pltpu.HBM)] * 6
        + [pl.BlockSpec(memory_space=pltpu.VMEM)],
        out_specs=[pl.BlockSpec(memory_space=pltpu.HBM)] * 7
        + [pl.BlockSpec(memory_space=pltpu.VMEM)] * 3,
        scratch_shapes=[
            pltpu.VMEM(gin.shape, gin.dtype),
            pltpu.VMEM(gu.shape, gu.dtype),
            pltpu.VMEM((part, wide_in), f32),
            pltpu.VMEM((part, wide_ff), f32),
            pltpu.VMEM((part, wide_ff), f32),
            pltpu.VMEM(out.shape, out.dtype),
            pltpu.VMEM(gx.shape, f32),
            pltpu.VMEM(gout.shape, f32),
            pltpu.VMEM(gdown.shape, f32),
            pltpu.SemaphoreType.DMA((13,)),
        ],
        compiler_params=pltpu.CompilerParams(vmem_limit_bytes=60 * 1024 * 1024),
        name="finish",
    )(out, gx, gin, gout, gu, gdown, small)


def split_tokens(
    inputs,
    gain_mixer,
    weight_in,
    conv_taps,
    weight_out,
    gain_ffn,
    weight_gate,
    weight_up,
    weight_down,
    cotangent,
):
    dp_count, fs_count = lax.axis_size("dp"), lax.axis_size("fsdp")
    fs = lax.axis_index("fsdp")
    tokens, width = inputs.shape[1:]
    part = weight_out.shape[0]
    hid = weight_gate.shape[1] // fs_count
    bf = jnp.bfloat16
    x, cot = inputs[0], cotangent[0]
    small = jnp.concatenate([gain_mixer[None], gain_ffn[None], conv_taps], axis=0)
    small = jnp.tile(jnp.pad(small, ((0, 16 - small.shape[0]), (0, 0))), (1, fs_count))
    lanes = lax.broadcasted_iota(jnp.int32, small.shape, 1)
    mine = (lanes >= fs * part) & (lanes < (fs + 1) * part)
    small = jnp.where(mine, small, jnp.zeros_like(small))
    (act1, proj, act2, in_w, out_w, gains, taps, resid, act3_all, cot_all, gu_all, down_rows) = mixer_forward(
        x, cot, small, weight_in, weight_gate, weight_up, weight_out, weight_down
    )
    gu_cols = gu_all.reshape(width, 2 * hid)
    gate_up = product(act3_all.reshape(-1, width), gu_cols)
    gate, upval = gate_up[:, :hid], gate_up[:, hid:]
    sig = jax.nn.sigmoid(gate)
    act4 = (gate * sig * upval).astype(bf)
    dact4 = product_nt(cot_all.reshape(-1, width), down_rows.reshape(hid, width))
    dgate = (dact4 * upval * sig * (1.0 + gate * (1.0 - sig))).astype(bf)
    dupval = (dact4 * gate * sig).astype(bf)
    parts = mixer_backward(
        x, gains, taps, resid, act1, proj, act2, in_w, out_w, gu_all, act3_all, dgate, dupval, act4, cot_all, down_rows
    )
    outputs, gx, gin, gout, ggate, gup, gdown, gain1, gain2, g_taps = finish(
        *parts, weight_in.shape[1], weight_gate.shape[1]
    )
    return (
        outputs[None], gx[None], gain1[0], gin, g_taps, gout, gain2[0], ggate, gup, gdown,
    )


def fits_tokens(inputs, weight_out, weight_gate):
    dp_count, fs_count = lax.axis_size("dp"), lax.axis_size("fsdp")
    tokens, width = inputs.shape[1:]
    return (
        dp_count % CORES == 0
        and dp_count > CORES
        and fs_count > 1
        and (width // dp_count) % 128 == 0
        and (weight_gate.shape[1] // fs_count) % 128 == 0
        and weight_out.shape[0] % 16 == 0
        and tokens % 16 == 0
        and inputs.shape[0] == 1
    )


def on_device(
    inputs,
    gain_mixer,
    weight_in,
    conv_taps,
    weight_out,
    gain_ffn,
    weight_gate,
    weight_up,
    weight_down,
    cotangent,
):
    form = split_tokens if fits_tokens(inputs, weight_out, weight_gate) else split_features
    return form(
        inputs,
        gain_mixer,
        weight_in,
        conv_taps,
        weight_out,
        gain_ffn,
        weight_gate,
        weight_up,
        weight_down,
        cotangent,
    )


def solution(mesh):
    in_specs = (
        P("dp", "fsdp", None),
        P(("dp", "fsdp")),
        P(("dp", "fsdp"), None),
        P(None, ("dp", "fsdp")),
        P(("dp", "fsdp"), None),
        P(("dp", "fsdp")),
        P(("dp", "fsdp"), None),
        P(("dp", "fsdp"), None),
        P(("dp", "fsdp"), None),
        P("dp", "fsdp", None),
    )
    out_specs = (
        P("dp", "fsdp", None),
        P("dp", "fsdp", None),
        P(("dp", "fsdp")),
        P(("dp", "fsdp"), None),
        P(None, ("dp", "fsdp")),
        P(("dp", "fsdp"), None),
        P(("dp", "fsdp")),
        P(("dp", "fsdp"), None),
        P(("dp", "fsdp"), None),
        P(("dp", "fsdp"), None),
    )
    return jax.shard_map(
        on_device, mesh=mesh, in_specs=in_specs, out_specs=out_specs, check_vma=False
    )
```
